32 devices in a mesh: dp: 8 (over y, x, core), tensor: 4 (over z).
Axes of the slice: x: 2, y: 2, z: 4, core: 2. Of those that a mesh axis runs over, the one named last changes fastest.
Arguments:
- inputs: float32 [8192, 1536], P(('dp', 'tensor')), may hold values from -80 to 80
- norm_gains: float32 [1, 2, 1536], replicated, may hold values from 0.5 to 1.5
- w_qkv: bfloat16 [1, 1536, 3072], P(None, 'dp', 'tensor'), may hold values from -0.15625 to 0.15625
- w_gate_up: bfloat16 [1, 1536, 2, 4096], P(None, 'dp', None, 'tensor'), may hold values from -0.15625 to 0.15625
- w_out: bfloat16 [1, 1536, 1536], P(None, 'dp', 'tensor'), may hold values from -2.5 to 2.5
- w_down: bfloat16 [1, 1536, 4096], P(None, 'dp', 'tensor'), may hold values from -0.09375 to 0.09375
- segments: int32 [8192], P('dp'), may hold values from 0 to 8, as said below
- positions: int32 [8192], P('dp'), may hold values from 0 to 799, as said below
- cotangent: bfloat16 [8192, 1536], P(('dp', 'tensor')), may hold values from -6 to 6
Outputs:
- output: float32 [8192, 1536], P(('dp', 'tensor'))
- input_grad: float32 [8192, 1536], P(('dp', 'tensor'))
- grad_qkv: float32 [1, 1536, 3072], P(None, 'dp', 'tensor')
- grad_gate_up: float32 [1, 1536, 2, 4096], P(None, 'dp', None, 'tensor')
- grad_out: float32 [1, 1536, 1536], P(None, 'dp', 'tensor')
- grad_down: float32 [1, 1536, 4096], P(None, 'dp', 'tensor')
- grad_gains: float32 [1, 2, 1536], replicated
- rms_stats: float32 [1, 4], replicated
The draws below stay inside these ranges and needn't reach their ends.
Inputs may be any that keep to these rules, and one draw needn't show every extreme that they name: `segments`: within each group of 1024 consecutive tokens (one index of dp), the tokens form blocks of 32: 24 prompt blocks with segment 0 and one block for each continuation 1 to 8, in a drawn order of blocks. Within a group the prompt's tokens have positions 0 to 767, rising along the group; each continuation's tokens have positions 768 to 799 in order.
All inputs are finite; a program needn't handle non-finite values.
Results may differ from the reference program's by a relative error of at most 0.012.
The reference program's roundings to bfloat16 on the way count: a program that leaves them out, or rounds other values in their place, can miss the bound.
Values may be sent and summed in bfloat16 or wider, within the bound.
A program may use at most 192 MiB of HBM per device.

```python
import jax
import jax.numpy as jnp
from jax import lax

D = 1536
HEADS = 16
KV_HEADS = 8
HEAD_WIDTH = 96
FF = 4096
LAYERS = 1
PROMPT = 768
CONTS = 8
CONT = 32
GROUP = 1024
TOKENS = 8192


def layout(base_key):
    groups = TOKENS // GROUP
    prompt_blocks = PROMPT // CONT
    blocks = prompt_blocks + CONTS

    def one_group(group_index):
        slot_order = jax.random.permutation(jax.random.fold_in(base_key, group_index), blocks).astype(jnp.int32)
        is_prompt = (slot_order < prompt_blocks).astype(jnp.int32)
        prompt_rank = jnp.cumsum(is_prompt) - 1
        segment = jnp.where(is_prompt == 1, 0, slot_order - prompt_blocks + 1).astype(jnp.int32)
        offset = jnp.arange(CONT, dtype=jnp.int32)
        first_position = jnp.where(is_prompt == 1, prompt_rank * CONT, PROMPT).astype(jnp.int32)
        position = first_position[:, None] + offset[None, :]
        segment = jnp.broadcast_to(segment[:, None], (blocks, CONT))
        return (segment.reshape(-1), position.reshape(-1))
    segment_ids, position_ids = jax.vmap(one_group)(jnp.arange(groups, dtype=jnp.int32))
    return (segment_ids.reshape(-1), position_ids.reshape(-1))


def draw_segments(key, part):
    return layout(jax.random.fold_in(key, 7))[0]


def draw_positions(key, part):
    return layout(jax.random.fold_in(key, 7))[1]


def draw_inputs(key, part):
    row_key, col_key, base_key = jax.random.split(key, 3)
    row_place = jnp.arange(TOKENS, dtype=jnp.float32) / TOKENS
    base_values = jax.random.normal(base_key, (TOKENS, D), jnp.float32)
    row_ramp = jnp.exp(row_place * jnp.log(3.0))
    column = jnp.exp(jax.random.uniform(col_key, (D,), jnp.float32, -0.5, 0.5))
    jitter = jnp.exp(jax.random.uniform(row_key, (TOKENS,), jnp.float32, -0.3, 0.3))
    return base_values * (row_ramp * jitter)[:, None] * column[None, :]


def with_spikes(result, rng, source, target, parts, factor):
    owner, partner = [(jnp.arange(result.shape[axis_at]) // (result.shape[axis_at] // parts)).reshape([-1 if axis == axis_at else 1 for axis in range(result.ndim)]) for axis_at in (source, target)]
    chosen = jax.random.permutation(rng, parts)[partner]
    strong = (owner == chosen) | (owner == (partner + parts // 2) % parts)
    return jnp.where(strong, factor * result, result)


def block_levels(own_key, extent, cuts, least, largest):
    level, own = 1.0, jax.random.fold_in(own_key, 6)
    for axis_at, blocks in cuts:
        heights = jnp.exp(jax.random.uniform(jax.random.fold_in(own, axis_at), (blocks,), jnp.float32, least / len(cuts), largest / len(cuts)))
        level = level * jnp.repeat(heights, extent[axis_at] // blocks).reshape([-1 if axis == axis_at else 1 for axis in range(len(extent))])
    return level


def normal_values(rng, extent, deviation, reach, pieces=(), kind=jnp.bfloat16):
    result = deviation * jax.random.normal(rng, extent, jnp.float32)
    if pieces:
        result = result * block_levels(rng, extent, pieces, -0.22, 0.18)
    return jnp.clip(result, -reach, reach).astype(kind)


def noise_with(key, shape, width, bound, cuts, heavy, kind=jnp.bfloat16):
    values = width * jax.random.normal(key, shape, jnp.float32)
    if cuts:
        values = values * block_levels(key, shape, cuts, -0.22, 0.18)
    return jnp.clip(with_spikes(values, jax.random.fold_in(key, 3), *heavy), -bound, bound).astype(kind)


def setup_inputs(seed: int = 0) -> dict:
    key_of = jax.random.split(jax.random.key(seed), 10)
    inputs = draw_inputs(jax.random.fold_in(key_of[9], 71), 0)
    norm_gains = jnp.clip(1.0 + 0.1 * jax.random.normal(key_of[1], (LAYERS, 2, D), jnp.float32), 0.5, 1.5)
    w_qkv = normal_values(key_of[2], (LAYERS, D, (HEADS + 2 * KV_HEADS) * HEAD_WIDTH), D ** -0.5, 0.15625, ((1, 8), (2, 4)))
    w_gate_up = normal_values(key_of[3], (LAYERS, D, 2, FF), D ** -0.5, 0.15625, ((1, 8), (3, 4)))
    w_out = normal_values(key_of[4], (LAYERS, D, HEADS * HEAD_WIDTH), (max(1, HEADS * HEAD_WIDTH // 256)) ** -0.5, 2.5, ((1, 8), (2, 4)))
    w_down = normal_values(key_of[5], (LAYERS, D, FF), FF ** -0.5, 0.09375, ((1, 8), (2, 4)))
    segments = draw_segments(jax.random.fold_in(key_of[9], 71), 0)
    positions = draw_positions(jax.random.fold_in(key_of[9], 71), 0)
    cotangent = noise_with(key_of[8], (TOKENS, D), 1.0, 6.0, ((0, 32),), (0, 1, 32, 2.75))
    return {"inputs": inputs, "norm_gains": norm_gains, "w_qkv": w_qkv, "w_gate_up": w_gate_up, "w_out": w_out, "w_down": w_down, "segments": segments, "positions": positions, "cotangent": cotangent}


@jax.custom_vjp
def lower_precision(v):
    return lax.optimization_barrier(v.astype(jnp.bfloat16)).astype(jnp.float32)

@jax.custom_vjp
def low_back(v):
    return v

def low_keep(v):
    return (lower_precision(v), None)

def low_pass(kept, grad):
    return (grad,)

def back_keep(v):
    return (v, None)

def back_low(kept, grad):
    return (lower_precision(grad),)
lower_precision.defvjp(low_keep, low_pass)
low_back.defvjp(back_keep, back_low)
norm_eps = 1e-05
rope_base = 100000.0
highest_precision = lax.Precision.HIGHEST

def normalize(values, gain):
    return values * lax.rsqrt(lax.optimization_barrier(jnp.mean(values * values, axis=-1, keepdims=True)) + norm_eps) * gain

def rope_tables(position):
    freq_steps = jnp.arange(HEAD_WIDTH // 2, dtype=jnp.float32) * (2.0 / HEAD_WIDTH)
    inverse = jnp.power(rope_base, -freq_steps)
    angles = position.astype(jnp.float32)[:, None] * inverse[None, :]
    return (jnp.cos(angles), jnp.sin(angles))

def rotate(values, cosine_table, sine_table):
    half_dim = values.shape[-1] // 2
    first_half = values[..., :half_dim]
    second_half = values[..., half_dim:]
    return jnp.concatenate([first_half * cosine_table - second_half * sine_table, second_half * cosine_table + first_half * sine_table], axis=-1)

def visible(query_segment, query_position, key_segment, key_position):
    same_doc = (key_segment[None, :] == 0) | (key_segment[None, :] == query_segment[:, None])
    return same_doc & (key_position[None, :] <= query_position[:, None])

def attend_group(query_matrix, key_matrix, value_matrix, segment_ids, position_ids):
    allowed = visible(segment_ids, position_ids, segment_ids, position_ids)
    attention_scores = jnp.einsum('mely,cey->elmc', query_matrix, key_matrix, precision=highest_precision) * HEAD_WIDTH ** (-0.5)
    attention_scores = jnp.where(allowed[None, None], low_back(attention_scores), -1e+30)
    row_top = lax.optimization_barrier(jnp.max(attention_scores, axis=-1, keepdims=True))
    weights = jnp.exp(attention_scores - row_top)
    probability_full = weights / lax.optimization_barrier(jnp.sum(weights, axis=-1, keepdims=True))
    mixed_rows_block = jnp.einsum('zbvq,qzo->vzbo', lower_precision(probability_full), value_matrix, precision=highest_precision)
    return lower_precision(low_back(mixed_rows_block))

def attend_item(block_item):
    return jax.checkpoint(attend_group)(*block_item)

def layer_pass(hidden, gains_one, qkv_one, gate_up_one, out_one, down_one, segments, positions):
    tokens = hidden.shape[0]
    repeat = HEADS // KV_HEADS
    groups = tokens // GROUP
    cosine_table, sine_table = rope_tables(positions)
    normed = lower_precision(normalize(hidden, gains_one[0]))
    joined_rows = low_back(jnp.dot(normed, qkv_one, precision=highest_precision)).reshape(tokens, KV_HEADS, repeat + 2, HEAD_WIDTH)
    query_matrix = lower_precision(rotate(joined_rows[:, :, :repeat], cosine_table[:, None, None, :], sine_table[:, None, None, :]))
    key_matrix = lower_precision(rotate(joined_rows[:, :, repeat], cosine_table[:, None, :], sine_table[:, None, :]))
    value_matrix = lower_precision(joined_rows[:, :, repeat + 1])
    mixed_all = lax.map(attend_item, (query_matrix.reshape(groups, GROUP, KV_HEADS, repeat, HEAD_WIDTH), key_matrix.reshape(groups, GROUP, KV_HEADS, HEAD_WIDTH), value_matrix.reshape(groups, GROUP, KV_HEADS, HEAD_WIDTH), segments.reshape(groups, GROUP), positions.reshape(groups, GROUP)))
    branch = low_back(jnp.dot(mixed_all.reshape(tokens, HEADS * HEAD_WIDTH), out_one.T, precision=highest_precision))
    middle = hidden + branch
    normed_two = lower_precision(normalize(middle, gains_one[1]))
    gate_rows = low_back(jnp.dot(normed_two, gate_up_one[:, 0], precision=highest_precision))
    up_rows = low_back(jnp.dot(normed_two, gate_up_one[:, 1], precision=highest_precision))
    product = lower_precision(jax.nn.silu(gate_rows) * up_rows)
    branch_two = low_back(jnp.dot(product, down_one.T, precision=highest_precision))
    output = middle + branch_two
    squares = jnp.stack([jnp.sum(middle * middle), jnp.sum(output * output), jnp.sum(branch * branch), jnp.sum(branch_two * branch_two)])
    return (output, squares)

def reference(inputs, norm_gains, w_qkv, w_gate_up, w_out, w_down, segments, positions, cotangent):

    def forward(hidden, gains_all, qkv_all, gate_up_all, out_all, down_all):
        stat_list = []
        for layer_index in range(LAYERS):
            hidden, squares = layer_pass(hidden, gains_all[layer_index], qkv_all[layer_index], gate_up_all[layer_index], out_all[layer_index], down_all[layer_index], segments, positions)
            stat_list.append(squares)
        return (hidden, jnp.stack(stat_list))
    output, backward, squares = jax.vjp(forward, inputs, norm_gains, w_qkv.astype(jnp.float32), w_gate_up.astype(jnp.float32), w_out.astype(jnp.float32), w_down.astype(jnp.float32), has_aux=True)
    grad_list = backward(cotangent.astype(jnp.float32))
    rms_values = jnp.sqrt(squares / (inputs.shape[0] * inputs.shape[1]))
    return (output, grad_list[0], grad_list[2], grad_list[3], grad_list[4], grad_list[5], grad_list[1], rms_values)
```

```python
import functools

import jax
import jax.numpy as jnp
from jax import lax
from jax.experimental import pallas as pl
from jax.experimental.pallas import tpu as pltpu
from jax.sharding import PartitionSpec as P

HEADS = 16
KV_HEADS = 8
HEAD_WIDTH = 96
REPEAT = HEADS // KV_HEADS
LANES = 128

norm_eps = 1e-05
rope_base = 100000.0
MESH = pl.DeviceIdType.MESH
BF = jnp.bfloat16
F32 = jnp.float32
VMEM_LIMIT = 60 * 2**20


def nn(a, b):
    return lax.dot_general(a, b, (((1,), (0,)), ((), ())), preferred_element_type=F32)


def nt(a, b):
    return lax.dot_general(a, b, (((1,), (1,)), ((), ())), preferred_element_type=F32)


def tn(a, b):
    return lax.dot_general(a, b, (((0,), (0,)), ((), ())), preferred_element_type=F32)


def rows_at(index, size):
    return pl.ds(pl.multiple_of(index * size, size), size)


def entry_barrier(n, others=()):
    z = lax.axis_index("tensor")
    barrier = pltpu.get_barrier_semaphore()

    @pl.when(z > 0)
    def _():
        pl.semaphore_signal(barrier, inc=1, device_id={"tensor": z - 1}, device_id_type=MESH)

    @pl.when(z < n - 1)
    def _():
        pl.semaphore_signal(barrier, inc=1, device_id={"tensor": z + 1}, device_id_type=MESH)

    for other in others:
        pl.semaphore_signal(barrier, inc=1, device_id=other, device_id_type=MESH)

    @pl.when((z > 0) & (z < n - 1))
    def _():
        pl.semaphore_wait(barrier, 2 + len(others))

    @pl.when((z == 0) | (z == n - 1))
    def _():
        pl.semaphore_wait(barrier, 1 + len(others))


def bit_of(index, bit):
    return (index // (1 << bit)) % 2


def across(index, bit):
    return index + (1 << bit) * (1 - 2 * bit_of(index, bit))


class Gather:
    def __init__(self, n, at, send_sem, recv_sem):
        self.n, self.at, self.send_sem, self.recv_sem = n, at, send_sem, recv_sem
        self.z = lax.axis_index("tensor")

    def copy(self, slot, step, side, source=None):
        block = self.at(slot)
        return pltpu.make_async_remote_copy(
            src_ref=block if source is None else source,
            dst_ref=block,
            send_sem=self.send_sem.at[side, step],
            recv_sem=self.recv_sem.at[side, step],
            device_id={"tensor": self.z + 1 - 2 * side},
            device_id_type=MESH,
        )

    def sends(self, step, side):
        z, n = self.z, self.n
        slot = z - (1 - 2 * side) * (step - 1)
        target = z + 1 - 2 * side
        return slot, (slot >= 0) & (slot < n) & (target >= 0) & (target < n)

    def send(self, step, side, source=None):
        slot, valid = self.sends(step, side)

        @pl.when(valid)
        def _():
            self.copy(slot, step, side, source).start()

    def begin(self, source=None):
        self.send(1, 0, source)
        self.send(1, 1, source)

    def arrive(self, step, side, forward=True):
        z, n = self.z, self.n
        slot = z - (1 - 2 * side) * step

        @pl.when((slot >= 0) & (slot < n))
        def _():
            self.copy(slot, step, side).wait_recv()

        if forward is True:
            self.send(step + 1, side)
        return slot, (slot >= 0) & (slot < n)

    def drain(self, source=None):
        for step in range(1, self.n):
            for side in range(2):
                slot, valid = self.sends(step, side)

                @pl.when(valid)
                def _(slot=slot, step=step, side=side):
                    self.copy(slot, step, side, source if step == 1 else None).wait_send()


class Scatter:
    def __init__(self, n, buffer, send_sem, recv_sem):
        self.n, self.buffer, self.send_sem, self.recv_sem = n, buffer, send_sem, recv_sem
        self.z = lax.axis_index("tensor")

    def copy(self, step, side):
        return pltpu.make_async_remote_copy(
            src_ref=self.buffer.at[side, step - 1],
            dst_ref=self.buffer.at[side, step],
            send_sem=self.send_sem.at[side, step],
            recv_sem=self.recv_sem.at[side, step],
            device_id={"tensor": self.z + 1 - 2 * side},
            device_id_type=MESH,
        )

    def turn(self, step, side):
        z, n = self.z, self.n
        return z + (1 - 2 * side) * (n - step), step >= 1 + z + side * (n - 1 - 2 * z)

    def has_source(self, side):
        source = self.z - (1 - 2 * side)
        return (source >= 0) & (source < self.n)

    def push(self, step, side, part):
        slot = self.buffer.at[side, step - 1]
        has_source = self.has_source(side)

        @pl.when(has_source)
        def _():
            self.copy(step - 1, side).wait_recv()
            slot[...] = (part() + slot[...].astype(F32)).astype(BF)

        @pl.when(jnp.logical_not(has_source))
        def _():
            slot[...] = part().astype(BF)

        self.copy(step, side).start()

    def settle(self, total_ref):
        for side in range(2):

            @pl.when(self.has_source(side))
            def _(side=side):
                self.copy(self.n - 1, side).wait_recv()
                total_ref[...] += self.buffer[side, self.n - 1].astype(F32)

    def drain(self):
        for step in range(1, self.n):
            for side in range(2):

                @pl.when(self.turn(step, side)[1])
                def _(step=step, side=side):
                    self.copy(step, side).wait_send()


def by_rows(rows, body, block=32):
    def step(index, carry):
        body(rows_at(index, block))
        return carry

    lax.fori_loop(0, rows // block, step, 0)


def norm_rows(values, gain):
    inverse = lax.rsqrt(jnp.mean(values * values, axis=-1, keepdims=True) + norm_eps)
    return values * inverse * gain, inverse


def spread_kernel(n, x_ref, gain_ref, all_ref, own, send_sem, recv_sem, own_sem):
    z = lax.axis_index("tensor")
    tokens = x_ref.shape[0]
    gain = gain_ref[...]

    def normalize(rows):
        own[rows, :] = norm_rows(x_ref[rows, :], gain)[0].astype(BF)

    by_rows(tokens, normalize)
    entry_barrier(n)
    gather = Gather(n, lambda slot: all_ref.at[rows_at(slot, tokens)], send_sem, recv_sem)
    gather.begin(own)
    keep = pltpu.make_async_copy(own, all_ref.at[rows_at(z, tokens)], own_sem)
    keep.start()
    for step in range(1, n):
        for side in range(2):
            gather.arrive(step, side, forward=step < n - 1)
    keep.wait()
    gather.drain(own)


def spread(n, x, gain):
    tokens, width = x.shape
    return pl.pallas_call(
        functools.partial(spread_kernel, n),
        out_shape=jax.ShapeDtypeStruct((n * tokens, width), BF),
        in_specs=[pl.BlockSpec(memory_space=pltpu.VMEM)] * 2,
        out_specs=pl.BlockSpec(memory_space=pl.ANY),
        scratch_shapes=[
            pltpu.VMEM((tokens, width), BF),
            pltpu.SemaphoreType.DMA((2, n)),
            pltpu.SemaphoreType.DMA((2, n)),
            pltpu.SemaphoreType.DMA,
        ],
        compiler_params=pltpu.CompilerParams(
            collective_id=1, has_side_effects=True, vmem_limit_bytes=VMEM_LIMIT
        ),
        cost_estimate=pl.CostEstimate(
            flops=10 * tokens * width, bytes_accessed=100 * tokens * width * 2, transcendentals=0
        ),
        name="spread_normed",
    )(x, gain)


def attend_kernel(
    n,
    kv_local,
    g1_ref,
    wqkv_hbm,
    wout_hbm,
    gf_ref,
    x_ref,
    gain_ref,
    cos_ref,
    sin_low_ref,
    sin_high_ref,
    key_seg_ref,
    key_pos_ref,
    query_seg_ref,
    query_pos_ref,
    q_ref,
    k_ref,
    v_ref,
    o_ref,
    prob_hbm,
    gf_all,
    m_ref,
    n2_ref,
    stat_ref,
    g1,
    wqkv,
    wout,
    v_t,
    bias,
    prob,
    part,
    sums,
    load_sem,
    chunk_sem,
    prob_sem,
    own_sem,
    ag_send,
    ag_recv,
    rs_send,
    rs_recv,
):
    z = lax.axis_index("tensor")
    tokens, width = x_ref.shape
    heads = REPEAT * kv_local
    load_w = pltpu.make_async_copy(wqkv_hbm, wqkv, load_sem.at[0])
    load_w.start()
    load_o = pltpu.make_async_copy(wout_hbm, wout, load_sem.at[1])

    def load_chunk(slot):
        rows = rows_at(slot, tokens)
        return pltpu.make_async_copy(g1_ref.at[rows], g1.at[rows], chunk_sem.at[slot])

    for slot in range(n):
        load_chunk(slot).start()
    load_o.start()
    entry_barrier(n)
    gather = Gather(n, lambda slot: gf_all.at[rows_at(slot, tokens)], ag_send, ag_recv)
    gather.begin(gf_ref)
    keep = pltpu.make_async_copy(gf_ref, gf_all.at[rows_at(z, tokens)], own_sem)
    keep.start()
    load_w.wait()

    group_width = (REPEAT + 2) * LANES

    def project(slot, carry):
        load_chunk(slot).wait()
        rows = rows_at(slot, tokens)
        cosine, low, high = cos_ref[rows, :], sin_low_ref[rows, :], sin_high_ref[rows, :]

        def turn(values):
            return (
                values * cosine
                + pltpu.roll(values, LANES - HEAD_WIDTH // 2, 1) * low
                + pltpu.roll(values, HEAD_WIDTH // 2, 1) * high
            ).astype(BF)

        for group in range(kv_local):
            joined = nn(g1[rows, :], wqkv[:, group * group_width : (group + 1) * group_width])
            for member in range(REPEAT):
                q_ref[group * REPEAT + member, rows, :] = turn(
                    joined[:, member * LANES : (member + 1) * LANES]
                )
            k_ref[group, rows, :] = turn(joined[:, REPEAT * LANES : (REPEAT + 1) * LANES])
            values = joined[:, (REPEAT + 1) * LANES :]
            v_ref[group, rows, :] = values.astype(BF)
        return carry

    lax.fori_loop(0, n, project, 0)
    for group in range(kv_local):
        v_t[group] = v_ref[group].astype(F32).T.astype(BF)
    load_o.wait()
    scatter = Scatter(n, sums, rs_send, rs_recv)
    log2_scale = HEAD_WIDTH ** (-0.5) * 1.4426950408889634

    def attend(target):
        rows = rows_at(target, tokens)
        key_seg, key_pos = key_seg_ref[...], key_pos_ref[...]
        seen = (key_seg == 0) | (key_seg == query_seg_ref[target])
        seen = seen & (key_pos <= query_pos_ref[target])
        bias[...] = jnp.where(seen, 0.0, -1e30)
        for head in range(heads):
            group = head // REPEAT
            scores = nt(k_ref[group], q_ref[head, rows, :]) * log2_scale + bias[...]
            top = jnp.max(scores, axis=0, keepdims=True)
            weights = jnp.exp2(scores - top)
            total = jnp.sum(weights, axis=0, keepdims=True)
            prob[head] = (weights * (1.0 / total)).astype(BF)
            mixed = nn(v_t[group], prob[head])
            o_ref[rows, head * LANES : (head + 1) * LANES] = mixed.T.astype(BF)
        out = pltpu.make_async_copy(prob, prob_hbm.at[target], prob_sem)
        out.start()
        for first in range(0, width, 512):
            part[:, first : first + 512] = nt(o_ref[rows, :], wout[first : first + 512, :])
        out.wait()

    def turn_of(index, carry):
        step, side = index // 2 + 1, index % 2
        target, valid = scatter.turn(step, side)

        @pl.when(valid)
        def _():
            attend(target)
            scatter.push(step, side, lambda: part[...])

        gather.arrive(step, side, forward=None)

        @pl.when(step < n - 1)
        def _():
            gather.send(step + 1, side)

        return carry

    lax.fori_loop(0, 2 * (n - 1), turn_of, 0)
    attend(z)
    scatter.settle(part)
    gain = gain_ref[...]
    stat_ref[...] = jnp.zeros_like(stat_ref)

    def finish(rows):
        branch = part[rows, :]
        middle = x_ref[rows, :] + branch
        m_ref[rows, :] = middle
        n2_ref[rows, :] = norm_rows(middle, gain)[0].astype(BF)
        stat_ref[0:1, :] += jnp.sum(middle * middle, axis=0, keepdims=True)
        stat_ref[1:2, :] += jnp.sum(branch * branch, axis=0, keepdims=True)

    by_rows(tokens, finish)
    keep.wait()
    gather.drain(gf_ref)
    scatter.drain()


def attend(n, kv_local, g1, wqkv, wout, gf, x, gain, tables, keys, queries):
    tokens, width = x.shape
    group_len = n * tokens
    heads = REPEAT * kv_local
    vmem = pl.BlockSpec(memory_space=pltpu.VMEM)
    hbm = pl.BlockSpec(memory_space=pl.ANY)
    flops = 2 * group_len * (
        width * wqkv.shape[1] + width * wout.shape[1] + 2 * heads * group_len * LANES
    )
    return pl.pallas_call(
        functools.partial(attend_kernel, n, kv_local),
        out_shape=(
            jax.ShapeDtypeStruct((heads, group_len, LANES), BF),
            jax.ShapeDtypeStruct((kv_local, group_len, LANES), BF),
            jax.ShapeDtypeStruct((kv_local, group_len, LANES), BF),
            jax.ShapeDtypeStruct((group_len, heads * LANES), BF),
            jax.ShapeDtypeStruct((n, heads, group_len, tokens), BF),
            jax.ShapeDtypeStruct((group_len, width), BF),
            jax.ShapeDtypeStruct((tokens, width), F32),
            jax.ShapeDtypeStruct((tokens, width), BF),
            jax.ShapeDtypeStruct((8, width), F32),
        ),
        in_specs=[hbm, hbm, hbm] + [vmem] * 10,
        out_specs=(vmem, vmem, vmem, vmem, hbm, hbm, vmem, vmem, vmem),
        scratch_shapes=[
            pltpu.VMEM((group_len, width), BF),
            pltpu.VMEM(wqkv.shape, BF),
            pltpu.VMEM(wout.shape, BF),
            pltpu.VMEM((kv_local, LANES, group_len), BF),
            pltpu.VMEM((group_len, tokens), F32),
            pltpu.VMEM((heads, group_len, tokens), BF),
            pltpu.VMEM((tokens, width), F32),
            pltpu.VMEM((2, n, tokens, width), BF),
            pltpu.SemaphoreType.DMA((2,)),
            pltpu.SemaphoreType.DMA((n,)),
            pltpu.SemaphoreType.DMA,
            pltpu.SemaphoreType.DMA,
            pltpu.SemaphoreType.DMA((2, n)),
            pltpu.SemaphoreType.DMA((2, n)),
            pltpu.SemaphoreType.DMA((2, n)),
            pltpu.SemaphoreType.DMA((2, n)),
        ],
        compiler_params=pltpu.CompilerParams(
            collective_id=2, has_side_effects=True, vmem_limit_bytes=VMEM_LIMIT
        ),
        cost_estimate=pl.CostEstimate(
            flops=flops, bytes_accessed=200 * tokens * width * 2, transcendentals=0
        ),
        name="attend_forward",
    )(g1, wqkv, wout, gf, x, gain, *tables, *keys, *queries)


def feed_kernel(
    n,
    chunks,
    n2_ref,
    gf_hbm,
    wgu_hbm,
    wd_hbm,
    m_ref,
    gain_ref,
    cot_ref,
    z_hbm,
    dm_ref,
    ga_ref,
    dgain_ref,
    dwgu_ref,
    n2_all,
    gf_all,
    z_all,
    dgu,
    wgu,
    wd,
    part,
    dn2,
    sums,
    load_sem,
    gf_sem,
    z_sem,
    ag_send,
    ag_recv,
    rs_send,
    rs_recv,
):
    z = lax.axis_index("tensor")
    tokens, width = n2_ref.shape
    ff = wd_hbm.shape[1]
    piece = tokens // chunks
    rows_chunk = n * piece
    load_gu = pltpu.make_async_copy(wgu_hbm, wgu, load_sem.at[0])
    load_d = pltpu.make_async_copy(wd_hbm, wd, load_sem.at[1])

    def load_gf(chunk, slot):
        return pltpu.make_async_copy(
            gf_hbm.at[pl.ds(pl.multiple_of(slot * tokens + chunk * piece, piece), piece)],
            gf_all.at[pl.ds(pl.multiple_of(chunk * rows_chunk + slot * piece, piece), piece)],
            gf_sem.at[chunk, slot],
        )

    load_gu.start()
    load_d.start()
    for chunk in range(chunks):
        for slot in range(n):
            load_gf(chunk, slot).start()
        n2_all[pl.ds(pl.multiple_of(chunk * rows_chunk + z * piece, piece), piece), :] = n2_ref[
            chunk * piece : (chunk + 1) * piece, :
        ]
    entry_barrier(n)

    def gather_of(chunk):
        return Gather(
            n,
            lambda slot: n2_all.at[
                pl.ds(pl.multiple_of(chunk * rows_chunk + slot * piece, piece), piece)
            ],
            ag_send.at[chunk],
            ag_recv.at[chunk],
        )

    def scatter_of(chunk):
        return Scatter(n, sums.at[chunk], rs_send.at[chunk], rs_recv.at[chunk])

    for chunk in range(chunks):
        gather_of(chunk).begin()

    def gather_step(chunk, step):
        gather = gather_of(chunk)
        for side in range(2):
            gather.arrive(step, side, forward=step < n - 1)

    def scatter_step(chunk, step):
        scatter = scatter_of(chunk)
        for side in range(2):
            target, valid = scatter.turn(step, side)

            @pl.when(valid)
            def _():
                scatter.push(
                    step, side, lambda: part[chunk % 2, rows_at(target, piece), :]
                )

    def scatter_end(chunk):
        own = dn2.at[rows_at(chunk, piece)]
        own[...] = part[chunk % 2, rows_at(z, piece), :]
        scatter_of(chunk).settle(own)

    for step in range(1, n):
        gather_step(0, step)
    load_gu.wait()
    load_d.wait()
    block = 256
    hidden_blocks = ff // block
    out_blocks = width // 512

    def hidden_block(chunk, index):
        rows = rows_at(chunk, rows_chunk)
        cols = rows_at(index, block)
        up_cols = pl.ds(pl.multiple_of(ff + index * block, block), block)
        gate = nn(n2_all[rows, :], wgu[:, cols])
        up = nn(n2_all[rows, :], wgu[:, up_cols])
        dz = nn(gf_all[rows, :], wd[:, cols])
        s = 1.0 / (1.0 + jnp.exp(-gate))
        act = gate * s
        z_all[rows, cols] = (act * up).astype(BF)
        dgu[rows, cols] = (dz * up * (s * (1.0 + gate * (1.0 - s)))).astype(BF)
        dgu[rows, up_cols] = (dz * act).astype(BF)

    def out_block(chunk, index):
        rows = rows_at(chunk, rows_chunk)
        cols = rows_at(index, 512)
        part[chunk % 2, :, cols] = nt(dgu[rows, :], wgu[cols, :])

    def z_out(chunk):
        rows = rows_at(chunk, rows_chunk)
        return pltpu.make_async_copy(z_all.at[rows], z_hbm.at[rows], z_sem.at[chunk])

    def stage(chunk, carry):
        for slot in range(n):
            load_gf(chunk, slot).wait()
        pieces = [functools.partial(hidden_block, chunk, i) for i in range(hidden_blocks)]
        pieces += [functools.partial(out_block, chunk, i) for i in range(out_blocks)]
        done = 0
        for step in range(1, n):
            until = len(pieces) * step // n
            for run in pieces[done:until]:
                run()
            done = until

            @pl.when(chunk + 1 < chunks)
            def _(step=step):
                gather_step(chunk + 1, step)

            @pl.when(chunk >= 1)
            def _(step=step):
                scatter_step(chunk - 1, step)

        for run in pieces[done:]:
            run()
        z_out(chunk).start()

        @pl.when(chunk >= 1)
        def _():
            scatter_end(chunk - 1)

        return carry

    lax.fori_loop(0, chunks, stage, 0)

    def grad_gu(first, last):
        def body(index, carry):
            cols = rows_at(index, 256)
            dwgu_ref[:, cols] = tn(n2_all[...], dgu[:, cols]).astype(BF)
            return carry

        lax.fori_loop(first, last, body, 0)

    blocks = 2 * ff // 256
    for step in range(1, n):
        scatter_step(chunks - 1, step)
        grad_gu(blocks * (step - 1) // (n - 1), blocks * step // (n - 1))
    scatter_end(chunks - 1)
    gain = gain_ref[...]
    dgain_ref[...] = jnp.zeros_like(dgain_ref)

    def finish(rows):
        middle = m_ref[rows, :]
        dn = dn2[rows, :]
        inverse = lax.rsqrt(jnp.mean(middle * middle, axis=-1, keepdims=True) + norm_eps)
        scaled = dn * gain
        dgain_ref[0:1, :] += jnp.sum(dn * middle * inverse, axis=0, keepdims=True)
        dm = (
            inverse * scaled
            - middle * inverse**3 * jnp.mean(scaled * middle, axis=-1, keepdims=True)
            + cot_ref[rows, :].astype(F32)
        )
        dm_ref[rows, :] = dm
        ga_ref[rows, :] = dm.astype(BF)

    by_rows(tokens, finish)
    for chunk in range(chunks):
        z_out(chunk).wait()
        gather_of(chunk).drain()
        scatter_of(chunk).drain()


def feed(n, chunks, n2, gf_all, wgu, wd, m, gain, cot):
    tokens, width = n2.shape
    group_len = n * tokens
    ff = wd.shape[1]
    vmem = pl.BlockSpec(memory_space=pltpu.VMEM)
    hbm = pl.BlockSpec(memory_space=pl.ANY)
    return pl.pallas_call(
        functools.partial(feed_kernel, n, chunks),
        out_shape=(
            jax.ShapeDtypeStruct((group_len, ff), BF),
            jax.ShapeDtypeStruct((tokens, width), F32),
            jax.ShapeDtypeStruct((tokens, width), BF),
            jax.ShapeDtypeStruct((8, width), F32),
            jax.ShapeDtypeStruct((width, 2 * ff), BF),
        ),
        in_specs=[vmem, hbm, hbm, hbm, vmem, vmem, vmem],
        out_specs=(hbm, vmem, vmem, vmem, vmem),
        scratch_shapes=[
            pltpu.VMEM((group_len, width), BF),
            pltpu.VMEM((group_len, width), BF),
            pltpu.VMEM((group_len, ff), BF),
            pltpu.VMEM((group_len, 2 * ff), BF),
            pltpu.VMEM((width, 2 * ff), BF),
            pltpu.VMEM((width, ff), BF),
            pltpu.VMEM((2, group_len // chunks, width), F32),
            pltpu.VMEM((tokens, width), F32),
            pltpu.VMEM((chunks, 2, n, tokens // chunks, width), BF),
            pltpu.SemaphoreType.DMA((2,)),
            pltpu.SemaphoreType.DMA((chunks, n)),
            pltpu.SemaphoreType.DMA((chunks,)),
            pltpu.SemaphoreType.DMA((chunks, 2, n)),
            pltpu.SemaphoreType.DMA((chunks, 2, n)),
            pltpu.SemaphoreType.DMA((chunks, 2, n)),
            pltpu.SemaphoreType.DMA((chunks, 2, n)),
        ],
        compiler_params=pltpu.CompilerParams(
            collective_id=3, has_side_effects=True, vmem_limit_bytes=VMEM_LIMIT
        ),
        cost_estimate=pl.CostEstimate(
            flops=18 * group_len * width * ff, bytes_accessed=250 * tokens * width * 2, transcendentals=0
        ),
        name="feed_both",
    )(n2, gf_all, wgu, wd, m, gain, cot)


def attend_back_kernel(
    n,
    kv_local,
    chunks,
    ga_ref,
    wout_hbm,
    wd_hbm,
    z_hbm,
    prob_hbm,
    g1_hbm,
    gf_hbm,
    m_ref,
    q_ref,
    k_ref,
    v_ref,
    o_ref,
    cos_ref,
    sin_low_ref,
    sin_high_ref,
    out_ref,
    stat_ref,
    dqkv_ref,
    dwd_ref,
    dw_ref,
    ga_all,
    g1,
    gf,
    wout,
    wd,
    z_all,
    k_t,
    prob,
    dk,
    dv,
    part,
    sums,
    load_sem,
    gf_sem,
    prob_sem,
    ag_send,
    ag_recv,
    rs_send,
    rs_recv,
):
    z = lax.axis_index("tensor")
    tokens, width = ga_ref.shape
    heads = REPEAT * kv_local
    group_len = n * tokens
    piece = tokens // chunks
    scale = HEAD_WIDTH ** (-0.5)
    loads = [
        pltpu.make_async_copy(source, target, load_sem.at[index])
        for index, (source, target) in enumerate(
            [(wout_hbm, wout), (z_hbm, z_all), (wd_hbm, wd), (g1_hbm, g1)]
        )
    ]
    for load in loads:
        load.start()
    load_out, load_z, load_d, load_g1 = loads

    def load_gf(chunk, slot):
        return pltpu.make_async_copy(
            gf_hbm.at[pl.ds(pl.multiple_of(slot * tokens + chunk * piece, piece), piece)],
            gf.at[pl.ds(pl.multiple_of((chunk * n + slot) * piece, piece), piece)],
            gf_sem.at[chunk, slot],
        )

    for chunk in range(chunks):
        for slot in range(n):
            load_gf(chunk, slot).start()

    def load_prob(slot, place):
        return pltpu.make_async_copy(prob_hbm.at[slot], prob.at[place], prob_sem.at[place])

    ga_all[rows_at(z, tokens), :] = ga_ref[...]
    entry_barrier(n)
    gather = Gather(n, lambda slot: ga_all.at[rows_at(slot, tokens)], ag_send, ag_recv)
    gather.begin()
    load_prob(z, 0).start()
    scatter = Scatter(n, sums, rs_send, rs_recv)
    for group in range(kv_local):
        k_t[group] = k_ref[group].astype(F32).T.astype(BF)
    dk[...] = jnp.zeros_like(dk)
    dv[...] = jnp.zeros_like(dv)
    load_out.wait()
    load_z.wait()
    load_d.wait()
    group_lanes = (REPEAT + 2) * LANES

    def turn_back(values, rows):
        return (
            values * cos_ref[rows, :]
            - pltpu.roll(values, LANES - HEAD_WIDTH // 2, 1) * sin_low_ref[rows, :]
            - pltpu.roll(values, HEAD_WIDTH // 2, 1) * sin_high_ref[rows, :]
        )

    def back(slot, place):
        rows = rows_at(slot, tokens)
        d_o = nn(ga_all[rows, :], wout[...])
        for head in range(heads):
            group = head // REPEAT
            lanes = slice(head * LANES, (head + 1) * LANES)
            do_h = d_o[:, lanes].astype(BF)
            both = do_h.astype(F32) * o_ref[rows, lanes].astype(F32)
            delta = jnp.sum(both.T, axis=0, keepdims=True)
            dprob = nt(v_ref[group], do_h)
            weights = prob[place, head]
            ds = (weights.astype(F32) * (dprob - delta)).astype(BF)
            dv[group] += nn(weights, do_h)
            dk[group] += nn(ds, q_ref[head, rows, :])
            dq = nn(k_t[group], ds).T * scale
            first = group * group_lanes + (head % REPEAT) * LANES
            dqkv_ref[rows, first : first + LANES] = turn_back(dq, rows).astype(BF)

    def feed_rows(target):
        pieces = [
            z_all[
                pl.ds(
                    pl.multiple_of(chunk * n * piece + target * piece, piece), piece
                ),
                :,
            ]
            for chunk in range(chunks)
        ]
        rows = jnp.concatenate(pieces, axis=0) if chunks > 1 else pieces[0]
        for first in range(0, width, 512):
            part[:, first : first + 512] = nt(rows, wd[first : first + 512, :])

    def turn_of(index, carry):
        step, side = index // 2 + 1, index % 2
        target, sends = scatter.turn(step, side)

        @pl.when(sends)
        def _():
            feed_rows(target)
            scatter.push(step, side, lambda: part[...])

        slot, valid = gather.arrive(step, side, forward=None)

        @pl.when(step < n - 1)
        def _():
            gather.send(step + 1, side)

        @pl.when(valid)
        def _():
            load_prob(slot, 1).start()
            load_prob(slot, 1).wait()
            back(slot, 1)

        return carry

    load_prob(z, 0).wait()
    back(z, 0)
    for chunk in range(chunks):
        for slot in range(n):
            load_gf(chunk, slot).wait()
    down_blocks = dwd_ref.shape[1] // 256

    def grad_down(first, last):
        def body(index, carry):
            cols = rows_at(index, 256)
            dwd_ref[:, cols] = tn(gf[...], z_all[:, cols]).astype(BF)
            return carry

        lax.fori_loop(first, last, body, 0)

    for step in range(1, n):
        lax.fori_loop(2 * (step - 1), 2 * step, turn_of, 0)
        grad_down(down_blocks * (step - 1) // (n - 1), down_blocks * step // (n - 1))

    def finish_keys(slot, carry):
        rows = rows_at(slot, tokens)
        for group in range(kv_local):
            first = group * group_lanes + REPEAT * LANES
            dqkv_ref[rows, first : first + LANES] = turn_back(
                dk[group, rows, :] * scale, rows
            ).astype(BF)
            dqkv_ref[rows, first + LANES : first + 2 * LANES] = dv[group, rows, :].astype(BF)
        return carry

    lax.fori_loop(0, n, finish_keys, 0)
    load_g1.wait()
    feed_rows(z)
    out_lanes = heads * LANES

    def grad_qkv(index, carry):
        cols = rows_at(index, 256)
        place = pl.ds(pl.multiple_of(out_lanes + index * 256, 256), 256)
        dw_ref[:, place] = tn(g1[...], dqkv_ref[:, cols]).astype(BF)
        return carry

    lax.fori_loop(0, dqkv_ref.shape[1] // 256, grad_qkv, 0)

    def grad_out(index, carry):
        cols = rows_at(index, 256)
        dw_ref[:, cols] = tn(ga_all[...], o_ref[:, cols]).astype(BF)
        return carry

    lax.fori_loop(0, out_lanes // 256, grad_out, 0)
    scatter.settle(part)
    stat_ref[...] = jnp.zeros_like(stat_ref)

    def finish(rows):
        branch = part[rows, :]
        result = m_ref[rows, :] + branch
        out_ref[rows, :] = result
        stat_ref[0:1, :] += jnp.sum(result * result, axis=0, keepdims=True)
        stat_ref[1:2, :] += jnp.sum(branch * branch, axis=0, keepdims=True)

    by_rows(tokens, finish)
    gather.drain()
    scatter.drain()


def attend_back(n, kv_local, chunks, ga, wout, wd, z_all, prob, g1, gf, m, q, k, v, o, tables):
    tokens, width = ga.shape
    group_len = n * tokens
    heads = REPEAT * kv_local
    ff = wd.shape[1]
    lanes = (REPEAT + 2) * kv_local * LANES
    vmem = pl.BlockSpec(memory_space=pltpu.VMEM)
    hbm = pl.BlockSpec(memory_space=pl.ANY)
    return pl.pallas_call(
        functools.partial(attend_back_kernel, n, kv_local, chunks),
        out_shape=(
            jax.ShapeDtypeStruct((tokens, width), F32),
            jax.ShapeDtypeStruct((8, width), F32),
            jax.ShapeDtypeStruct((group_len, lanes), BF),
            jax.ShapeDtypeStruct((width, ff), BF),
            jax.ShapeDtypeStruct((width, heads * LANES + lanes), BF),
        ),
        in_specs=[vmem] + [hbm] * 6 + [vmem] * 8,
        out_specs=(vmem,) * 5,
        scratch_shapes=[
            pltpu.VMEM((group_len, width), BF),
            pltpu.VMEM((group_len, width), BF),
            pltpu.VMEM((group_len, width), BF),
            pltpu.VMEM(wout.shape, BF),
            pltpu.VMEM(wd.shape, BF),
            pltpu.VMEM((group_len, ff), BF),
            pltpu.VMEM((kv_local, LANES, group_len), BF),
            pltpu.VMEM((2, heads, group_len, tokens), BF),
            pltpu.VMEM((kv_local, group_len, LANES), F32),
            pltpu.VMEM((kv_local, group_len, LANES), F32),
            pltpu.VMEM((tokens, width), F32),
            pltpu.VMEM((2, n, tokens, width), BF),
            pltpu.SemaphoreType.DMA((4,)),
            pltpu.SemaphoreType.DMA((chunks, n)),
            pltpu.SemaphoreType.DMA((2,)),
            pltpu.SemaphoreType.DMA((2, n)),
            pltpu.SemaphoreType.DMA((2, n)),
            pltpu.SemaphoreType.DMA((2, n)),
            pltpu.SemaphoreType.DMA((2, n)),
        ],
        compiler_params=pltpu.CompilerParams(
            collective_id=4, has_side_effects=True, vmem_limit_bytes=VMEM_LIMIT
        ),
        cost_estimate=pl.CostEstimate(
            flops=8 * group_len * width * ff, bytes_accessed=200 * tokens * width * 2, transcendentals=0
        ),
        name="attend_backward",
    )(ga, wout, wd, z_all, prob, g1, gf, m, q, k, v, o, *tables)


class Halving:
    def __init__(self, size, rows, grad, keep, buffer, keep_sem, send_sem, recv_sem):
        self.rows, self.grad, self.keep, self.buffer = rows, grad, keep, buffer
        self.keep_sem, self.send_sem, self.recv_sem = keep_sem, send_sem, recv_sem
        self.me = lax.axis_index("dp")
        self.bits = size.bit_length() - 1
        rest = list(range(1, self.bits))
        self.orders = ([0] + rest, [0] + rest[::-1])
        self.half = buffer.shape[-1]
        self.size = size

    def count(self, stage):
        return self.size >> (stage + 1)

    def offset(self, stage):
        return self.size - (self.size >> stage)

    def block_rows(self, half, number, mine):
        order = self.orders[half]
        first = bit_of(self.me, 0)
        index = first if mine else 1 - first
        later = order[1:]
        for place, bit in enumerate(later):
            index = index + ((number >> (len(later) - 1 - place)) & 1) * (1 << bit)
        return rows_at(index, self.rows)

    def columns(self, half):
        return slice(half * self.half, (half + 1) * self.half)

    def load(self, half, number):
        return pltpu.make_async_copy(
            self.grad.at[self.block_rows(half, number, True), self.columns(half)],
            self.keep.at[half, number],
            self.keep_sem.at[half, number],
        )

    def first_copy(self, half, number):
        return pltpu.make_async_remote_copy(
            src_ref=self.grad.at[self.block_rows(half, number, False), self.columns(half)],
            dst_ref=self.buffer.at[half, number],
            send_sem=self.send_sem.at[half, number],
            recv_sem=self.recv_sem.at[half, number],
            device_id={"dp": across(self.me, 0)},
            device_id_type=MESH,
        )

    def copy(self, half, stage):
        bit = self.orders[half][stage]
        count = self.count(stage)
        goes = (1 - bit_of(self.me, bit)) * count + self.offset(stage - 1)
        return pltpu.make_async_remote_copy(
            src_ref=self.buffer.at[half, pl.ds(goes, count)],
            dst_ref=self.buffer.at[half, pl.ds(self.offset(stage), count)],
            send_sem=self.send_sem.at[half, self.offset(stage)],
            recv_sem=self.recv_sem.at[half, self.offset(stage)],
            device_id={"dp": across(self.me, bit)},
            device_id_type=MESH,
        )

    def begin(self):
        for half in range(2):
            for number in range(self.count(0)):
                self.first_copy(half, number).start()
                self.load(half, number).start()

    def advance(self, stage):
        for half in range(2):
            if stage == 0:
                for number in range(self.count(0)):
                    self.first_copy(half, number).wait_recv()
                    self.load(half, number).wait()
            else:
                self.copy(half, stage).wait_recv()
            if stage == self.bits - 1:
                continue
            base = bit_of(self.me, self.orders[half][stage]) * self.count(stage)

            def add(number, carry, half=half, base=base):
                place = self.offset(stage) + number
                if stage == 0:
                    kept = self.keep[half, number]
                else:
                    kept = self.buffer[half, self.offset(stage - 1) + base + number]
                self.buffer[half, place] = (
                    self.buffer[half, place].astype(F32) + kept.astype(F32)
                ).astype(BF)
                return carry

            lax.fori_loop(0, self.count(stage), add, 0)
            self.copy(half, stage + 1).start()

    def result(self, half):
        stage = self.bits - 1
        base = bit_of(self.me, self.orders[half][stage])
        return self.buffer[half, self.offset(stage)].astype(F32) + self.buffer[
            half, self.offset(stage - 1) + base
        ].astype(F32)

    def drain(self):
        for half in range(2):
            for number in range(self.count(0)):
                self.first_copy(half, number).wait_send()
            for stage in range(1, self.bits):
                self.copy(half, stage).wait_send()


def last_kernel(
    n,
    dp,
    cells,
    out_heads,
    dqkv_ref,
    wqkv_ref,
    x_ref,
    dm_ref,
    gain_ref,
    dgain_two_ref,
    stat_one_ref,
    stat_two_ref,
    dw_hbm,
    dx_ref,
    gains_ref,
    rms_ref,
    grad_out_ref,
    grad_qkv_ref,
    part,
    sums,
    keep,
    blocks,
    vector,
    vectors,
    rs_send,
    rs_recv,
    keep_sem,
    dp_send,
    dp_recv,
    all_send,
    all_recv,
):
    z = lax.axis_index("tensor")
    me = lax.axis_index("dp")
    tokens, width = x_ref.shape
    dp_bits, z_bits = dp.bit_length() - 1, n.bit_length() - 1
    partners = [{"dp": across(me, bit)} for bit in range(dp_bits)]
    partners += [{"tensor": across(z, bit)} for bit in range(z_bits)]
    entry_barrier(n, partners[:dp_bits] + partners[dp_bits + 1 :])
    halving = Halving(dp, grad_out_ref.shape[0], dw_hbm, keep, blocks, keep_sem, dp_send, dp_recv)
    halving.begin()
    scatter = Scatter(n, sums, rs_send, rs_recv)

    def rows_of(target):
        rows = rows_at(target, tokens)
        for first in range(0, width, 512):
            part[:, first : first + 512] = nt(dqkv_ref[rows, :], wqkv_ref[first : first + 512, :])

    def turn_of(index, carry):
        step, side = index // 2 + 1, index % 2
        target, sends = scatter.turn(step, side)

        @pl.when(sends)
        def _():
            rows_of(target)
            scatter.push(step, side, lambda: part[...])

        return carry

    for step in range(1, n):
        lax.fori_loop(2 * (step - 1), 2 * step, turn_of, 0)
        if step <= dp_bits:
            halving.advance(step - 1)
    for stage in range(n - 1, dp_bits):
        halving.advance(stage)
    rows_of(z)
    for half in range(2):
        block = halving.result(half)
        first_head = half * (block.shape[1] // LANES)
        for index in range(block.shape[1] // LANES):
            values = block[:, index * LANES : index * LANES + HEAD_WIDTH]
            head = first_head + index
            if head < out_heads:
                grad_out_ref[:, head * HEAD_WIDTH : (head + 1) * HEAD_WIDTH] = values
            else:
                head -= out_heads
                grad_qkv_ref[:, head * HEAD_WIDTH : (head + 1) * HEAD_WIDTH] = values
    scatter.settle(part)
    gain = gain_ref[...]
    vector[...] = jnp.zeros_like(vector)
    vector[1:2, :] = dgain_two_ref[0:1, :]
    vector[2:3, :] = stat_one_ref[0:1, :]
    vector[3:4, :] = stat_two_ref[0:1, :]
    vector[4:5, :] = stat_one_ref[1:2, :]
    vector[5:6, :] = stat_two_ref[1:2, :]

    def finish(rows):
        values = x_ref[rows, :]
        dn = part[rows, :]
        inverse = lax.rsqrt(jnp.mean(values * values, axis=-1, keepdims=True) + norm_eps)
        scaled = dn * gain
        vector[0:1, :] += jnp.sum(dn * values * inverse, axis=0, keepdims=True)
        dx_ref[rows, :] = (
            inverse * scaled
            - values * inverse**3 * jnp.mean(scaled * values, axis=-1, keepdims=True)
            + dm_ref[rows, :]
        )

    by_rows(tokens, finish)

    def exchange(index):
        return pltpu.make_async_remote_copy(
            src_ref=vector if index == 0 else vectors.at[index - 1],
            dst_ref=vectors.at[index],
            send_sem=all_send.at[index],
            recv_sem=all_recv.at[index],
            device_id=partners[index],
            device_id_type=MESH,
        )

    for index in range(len(partners)):
        exchange(index).start()
        exchange(index).wait_recv()
        held = vector[...] if index == 0 else vectors[index - 1]
        vectors[index] += held
    for index in range(len(partners)):
        exchange(index).wait_send()
    total = vectors[len(partners) - 1]
    gains_ref[0] = total[0:2, :]
    squares = jnp.sqrt(jnp.sum(total, axis=1, keepdims=True) * (1.0 / cells))
    row = lax.broadcasted_iota(jnp.int32, (8, 4), 0)
    column = lax.broadcasted_iota(jnp.int32, (8, 4), 1)
    rms_ref[...] = jnp.sum(jnp.where(row == column + 2, squares, 0.0), axis=0, keepdims=True)
    halving.drain()
    scatter.drain()


def last(n, dqkv, wqkv, x, dm, gain, dgain_two, stat_one, stat_two, dw, out_columns, qkv_columns):
    tokens, width = x.shape
    dp = lax.axis_size("dp")
    owned = width // dp
    stages = (dp.bit_length() - 1) + (n.bit_length() - 1)
    half = dw.shape[1] // 2
    vmem = pl.BlockSpec(memory_space=pltpu.VMEM)
    return pl.pallas_call(
        functools.partial(last_kernel, n, dp, tokens * width * dp * n, out_columns // HEAD_WIDTH),
        out_shape=(
            jax.ShapeDtypeStruct((tokens, width), F32),
            jax.ShapeDtypeStruct((1, 2, width), F32),
            jax.ShapeDtypeStruct((1, 4), F32),
            jax.ShapeDtypeStruct((owned, out_columns), F32),
            jax.ShapeDtypeStruct((owned, qkv_columns), F32),
        ),
        in_specs=[vmem] * 8 + [pl.BlockSpec(memory_space=pl.ANY)],
        out_specs=(vmem,) * 5,
        scratch_shapes=[
            pltpu.VMEM((tokens, width), F32),
            pltpu.VMEM((2, n, tokens, width), BF),
            pltpu.VMEM((2, dp // 2, owned, half), BF),
            pltpu.VMEM((2, dp - 1, owned, half), BF),
            pltpu.VMEM((8, width), F32),
            pltpu.VMEM((stages, 8, width), F32),
            pltpu.SemaphoreType.DMA((2, n)),
            pltpu.SemaphoreType.DMA((2, n)),
            pltpu.SemaphoreType.DMA((2, dp // 2)),
            pltpu.SemaphoreType.DMA((2, dp)),
            pltpu.SemaphoreType.DMA((2, dp)),
            pltpu.SemaphoreType.DMA((stages,)),
            pltpu.SemaphoreType.DMA((stages,)),
        ],
        compiler_params=pltpu.CompilerParams(
            collective_id=5, has_side_effects=True, vmem_limit_bytes=VMEM_LIMIT
        ),
        cost_estimate=pl.CostEstimate(
            flops=2 * dqkv.size * width, bytes_accessed=150 * tokens * width * 2, transcendentals=0
        ),
        name="input_gradient",
    )(dqkv, wqkv, x, dm, gain, dgain_two, stat_one, stat_two, dw)


def pad_heads(values):
    rows, columns = values.shape
    heads = columns // HEAD_WIDTH
    padded = jnp.pad(
        values.reshape(rows, heads, HEAD_WIDTH), ((0, 0), (0, 0), (0, LANES - HEAD_WIDTH))
    )
    return padded.reshape(rows, heads * LANES)


def per_device(inputs, norm_gains, w_qkv, w_gate_up, w_out, w_down, segments, positions, cotangent):
    n = lax.axis_size("tensor")
    tokens, width = inputs.shape
    group_len = segments.shape[0]
    kv_local = w_out.shape[2] // (REPEAT * HEAD_WIDTH)
    ff_local = w_down.shape[2]
    chunks = 2
    half = HEAD_WIDTH // 2

    def whole(shard):
        return lax.all_gather(shard, "dp", axis=0, tiled=True)

    def owned(grad):
        return lax.psum_scatter(grad, "dp", scatter_dimension=0, tiled=True)

    wqkv = whole(pad_heads(w_qkv[0]))
    wout = whole(pad_heads(w_out[0]))
    wgu = whole(jnp.concatenate([w_gate_up[0, :, 0], w_gate_up[0, :, 1]], axis=1))
    wd = whole(w_down[0])

    lane = jnp.arange(LANES)
    freq_steps = jnp.arange(half, dtype=F32) * (2.0 / HEAD_WIDTH)
    inverse = jnp.power(rope_base, -freq_steps)
    lane_inverse = jnp.concatenate([inverse, inverse, jnp.zeros((LANES - HEAD_WIDTH,), F32)])
    angles = positions.astype(F32)[:, None] * lane_inverse[None, :]
    cosine, sine = jnp.cos(angles), jnp.sin(angles)
    tables = (
        cosine,
        jnp.where(lane < half, -sine, 0.0),
        jnp.where((lane >= half) & (lane < HEAD_WIDTH), sine, 0.0),
    )
    keys = (segments.reshape(group_len, 1), positions.reshape(group_len, 1))
    queries = (segments.reshape(n, 1, tokens), positions.reshape(n, 1, tokens))
    gain_one, gain_two = norm_gains[0, 0:1], norm_gains[0, 1:2]

    g1 = spread(n, inputs, gain_one)
    q, k, v, o, prob, gf_all, m, n2, stat_one = attend(
        n, kv_local, g1, wqkv, wout, cotangent, inputs, gain_two, tables, keys, queries
    )
    z_all, dm, ga, dgain_two, dwgu = feed(n, chunks, n2, gf_all, wgu, wd, m, gain_two, cotangent)
    grad_gu = owned(dwgu)
    output, stat_two, dqkv, dwd, dw = attend_back(
        n, kv_local, chunks, ga, wout, wd, z_all, prob, g1, gf_all, m, q, k, v, o, tables
    )
    dwd, grad_gu = lax.optimization_barrier((dwd, grad_gu))
    grad_down = owned(dwd)
    input_grad, gain_total, rms, grad_out, grad_qkv = last(
        n,
        dqkv,
        wqkv,
        inputs,
        dm,
        gain_one,
        dgain_two,
        stat_one,
        stat_two,
        dw,
        w_out.shape[2],
        w_qkv.shape[2],
    )
    return (
        output,
        input_grad,
        grad_qkv[None],
        grad_gu.reshape(-1, 2, ff_local)[None].astype(F32),
        grad_out[None],
        grad_down[None].astype(F32),
        gain_total,
        rms,
    )


def solution(mesh):
    rows = P(("dp", "tensor"), None)
    weights = P(None, "dp", "tensor")
    pairs = P(None, "dp", None, "tensor")
    return jax.shard_map(
        per_device,
        mesh=mesh,
        in_specs=(rows, P(), weights, pairs, weights, weights, P("dp"), P("dp"), rows),
        out_specs=(rows, rows, weights, pairs, weights, weights, P(), P()),
        check_vma=False,
    )
```

```python
import functools

import jax
import jax.numpy as jnp
from jax import lax
from jax.experimental import pallas as pl
from jax.experimental.pallas import tpu as pltpu
from jax.sharding import PartitionSpec as P

HEADS = 16
KV_HEADS = 8
HEAD_WIDTH = 96
REPEAT = HEADS // KV_HEADS
LANES = 128

norm_eps = 1e-05
rope_base = 100000.0
MESH = pl.DeviceIdType.MESH
BF = jnp.bfloat16
F32 = jnp.float32
VMEM_LIMIT = 60 * 2**20


def nn(a, b):
    return lax.dot_general(a, b, (((1,), (0,)), ((), ())), preferred_element_type=F32)


def nt(a, b):
    return lax.dot_general(a, b, (((1,), (1,)), ((), ())), preferred_element_type=F32)


def tn(a, b):
    return lax.dot_general(a, b, (((0,), (0,)), ((), ())), preferred_element_type=F32)


def rows_at(index, size):
    return pl.ds(pl.multiple_of(index * size, size), size)


def entry_barrier(n, others=()):
    z = lax.axis_index("tensor")
    barrier = pltpu.get_barrier_semaphore()

    @pl.when(z > 0)
    def _():
        pl.semaphore_signal(barrier, inc=1, device_id={"tensor": z - 1}, device_id_type=MESH)

    @pl.when(z < n - 1)
    def _():
        pl.semaphore_signal(barrier, inc=1, device_id={"tensor": z + 1}, device_id_type=MESH)

    for other in others:
        pl.semaphore_signal(barrier, inc=1, device_id=other, device_id_type=MESH)

    @pl.when((z > 0) & (z < n - 1))
    def _():
        pl.semaphore_wait(barrier, 2 + len(others))

    @pl.when((z == 0) | (z == n - 1))
    def _():
        pl.semaphore_wait(barrier, 1 + len(others))


def bit_of(index, bit):
    return (index // (1 << bit)) % 2


def across(index, bit):
    return index + (1 << bit) * (1 - 2 * bit_of(index, bit))


class Gather:
    def __init__(self, n, at, send_sem, recv_sem):
        self.n, self.at, self.send_sem, self.recv_sem = n, at, send_sem, recv_sem
        self.z = lax.axis_index("tensor")

    def copy(self, slot, step, side, source=None):
        block = self.at(slot)
        return pltpu.make_async_remote_copy(
            src_ref=block if source is None else source,
            dst_ref=block,
            send_sem=self.send_sem.at[side, step],
            recv_sem=self.recv_sem.at[side, step],
            device_id={"tensor": self.z + 1 - 2 * side},
            device_id_type=MESH,
        )

    def sends(self, step, side):
        z, n = self.z, self.n
        slot = z - (1 - 2 * side) * (step - 1)
        target = z + 1 - 2 * side
        return slot, (slot >= 0) & (slot < n) & (target >= 0) & (target < n)

    def send(self, step, side, source=None):
        slot, valid = self.sends(step, side)

        @pl.when(valid)
        def _():
            self.copy(slot, step, side, source).start()

    def begin(self, source=None):
        self.send(1, 0, source)
        self.send(1, 1, source)

    def arrive(self, step, side, forward=True):
        z, n = self.z, self.n
        slot = z - (1 - 2 * side) * step

        @pl.when((slot >= 0) & (slot < n))
        def _():
            self.copy(slot, step, side).wait_recv()

        if forward is True:
            self.send(step + 1, side)
        return slot, (slot >= 0) & (slot < n)

    def drain(self, source=None):
        for step in range(1, self.n):
            for side in range(2):
                slot, valid = self.sends(step, side)

                @pl.when(valid)
                def _(slot=slot, step=step, side=side):
                    self.copy(slot, step, side, source if step == 1 else None).wait_send()


class Scatter:
    def __init__(self, n, buffer, send_sem, recv_sem):
        self.n, self.buffer, self.send_sem, self.recv_sem = n, buffer, send_sem, recv_sem
        self.z = lax.axis_index("tensor")

    def copy(self, step, side):
        return pltpu.make_async_remote_copy(
            src_ref=self.buffer.at[side, step - 1],
            dst_ref=self.buffer.at[side, step],
            send_sem=self.send_sem.at[side, step],
            recv_sem=self.recv_sem.at[side, step],
            device_id={"tensor": self.z + 1 - 2 * side},
            device_id_type=MESH,
        )

    def turn(self, step, side):
        z, n = self.z, self.n
        return z + (1 - 2 * side) * (n - step), step >= 1 + z + side * (n - 1 - 2 * z)

    def has_source(self, side):
        source = self.z - (1 - 2 * side)
        return (source >= 0) & (source < self.n)

    def push(self, step, side, part):
        slot = self.buffer.at[side, step - 1]
        has_source = self.has_source(side)

        @pl.when(has_source)
        def _():
            self.copy(step - 1, side).wait_recv()
            slot[...] = (part() + slot[...].astype(F32)).astype(BF)

        @pl.when(jnp.logical_not(has_source))
        def _():
            slot[...] = part().astype(BF)

        self.copy(step, side).start()

    def settle(self, total_ref):
        for side in range(2):

            @pl.when(self.has_source(side))
            def _(side=side):
                self.copy(self.n - 1, side).wait_recv()
                total_ref[...] += self.buffer[side, self.n - 1].astype(F32)

    def drain(self):
        for step in range(1, self.n):
            for side in range(2):

                @pl.when(self.turn(step, side)[1])
                def _(step=step, side=side):
                    self.copy(step, side).wait_send()


def by_rows(rows, body, block=32):
    def step(index, carry):
        body(rows_at(index, block))
        return carry

    lax.fori_loop(0, rows // block, step, 0)


def norm_rows(values, gain):
    inverse = lax.rsqrt(jnp.mean(values * values, axis=-1, keepdims=True) + norm_eps)
    return values * inverse * gain, inverse


class Doubling:
    def __init__(self, size, source, target, keep_sem, send_sem, recv_sem):
        self.source, self.target = source, target
        self.keep_sem, self.send_sem, self.recv_sem = keep_sem, send_sem, recv_sem
        self.rows, columns = source.shape
        self.half = columns // 2
        self.me = lax.axis_index("dp")
        self.bits = size.bit_length() - 1
        rest = list(range(1, self.bits))
        self.orders = (rest + [0], rest[::-1] + [0])

    def index(self, order, stage, number):
        index = self.me
        for place in range(stage):
            if (number >> place) & 1:
                index = across(index, order[place])
        return index

    def copy(self, half, stage, number):
        order = self.orders[half]
        columns = slice(half * self.half, (half + 1) * self.half)
        place = self.target.at[rows_at(self.index(order, stage, number), self.rows), columns]
        return pltpu.make_async_remote_copy(
            src_ref=self.source.at[:, columns] if number == 0 else place,
            dst_ref=place,
            send_sem=self.send_sem.at[half, (1 << stage) + number],
            recv_sem=self.recv_sem.at[half, (1 << stage) + number],
            device_id={"dp": across(self.me, order[stage])},
            device_id_type=MESH,
        )

    def arrival(self, half, stage, number):
        order = self.orders[half]
        columns = slice(half * self.half, (half + 1) * self.half)
        index = across(self.index(order, stage, number), order[stage])
        place = self.target.at[rows_at(index, self.rows), columns]
        return pltpu.make_async_remote_copy(
            src_ref=place,
            dst_ref=place,
            send_sem=self.send_sem.at[half, (1 << stage) + number],
            recv_sem=self.recv_sem.at[half, (1 << stage) + number],
            device_id={"dp": across(self.me, order[stage])},
            device_id_type=MESH,
        )

    def own(self):
        return pltpu.make_async_copy(
            self.source, self.target.at[rows_at(self.me, self.rows)], self.keep_sem
        )

    def start(self, stage):
        for half in range(2):
            for number in range(1 << stage):
                self.copy(half, stage, number).start()

    def begin(self):
        self.own().start()
        self.start(0)

    def advance(self, stage):
        for half in range(2):
            for number in range(1 << stage):
                self.arrival(half, stage, number).wait_recv()
        if stage + 1 < self.bits:
            self.start(stage + 1)

    def drain(self, own=True):
        if own:
            self.own().wait()
        for half in range(2):
            for stage in range(self.bits):
                for number in range(1 << stage):
                    self.copy(half, stage, number).wait_send()


class Halving:
    def __init__(self, size, rows, grad, keep, buffer, keep_sem, send_sem, recv_sem):
        self.rows, self.grad, self.keep, self.buffer = rows, grad, keep, buffer
        self.keep_sem, self.send_sem, self.recv_sem = keep_sem, send_sem, recv_sem
        self.me = lax.axis_index("dp")
        self.bits = size.bit_length() - 1
        rest = list(range(1, self.bits))
        self.orders = ([0] + rest, [0] + rest[::-1])
        self.half = buffer.shape[-1]
        self.size = size

    def count(self, stage):
        return self.size >> (stage + 1)

    def offset(self, stage):
        return self.size - (self.size >> stage)

    def block_rows(self, half, number, mine):
        order = self.orders[half]
        first = bit_of(self.me, 0)
        index = first if mine else 1 - first
        later = order[1:]
        for place, bit in enumerate(later):
            index = index + ((number >> (len(later) - 1 - place)) & 1) * (1 << bit)
        return rows_at(index, self.rows)

    def columns(self, half):
        return slice(half * self.half, (half + 1) * self.half)

    def load(self, half, number):
        return pltpu.make_async_copy(
            self.grad.at[self.block_rows(half, number, True), self.columns(half)],
            self.keep.at[half, number],
            self.keep_sem.at[half, number],
        )

    def first_copy(self, half, number):
        return pltpu.make_async_remote_copy(
            src_ref=self.grad.at[self.block_rows(half, number, False), self.columns(half)],
            dst_ref=self.buffer.at[half, number],
            send_sem=self.send_sem.at[half, number],
            recv_sem=self.recv_sem.at[half, number],
            device_id={"dp": across(self.me, 0)},
            device_id_type=MESH,
        )

    def copy(self, half, stage):
        bit = self.orders[half][stage]
        count = self.count(stage)
        goes = (1 - bit_of(self.me, bit)) * count + self.offset(stage - 1)
        return pltpu.make_async_remote_copy(
            src_ref=self.buffer.at[half, pl.ds(goes, count)],
            dst_ref=self.buffer.at[half, pl.ds(self.offset(stage), count)],
            send_sem=self.send_sem.at[half, self.offset(stage)],
            recv_sem=self.recv_sem.at[half, self.offset(stage)],
            device_id={"dp": across(self.me, bit)},
            device_id_type=MESH,
        )

    def begin(self):
        for half in range(2):
            for number in range(self.count(0)):
                self.first_copy(half, number).start()
                self.load(half, number).start()

    def advance(self, stage):
        for half in range(2):
            if stage == 0:
                for number in range(self.count(0)):
                    self.first_copy(half, number).wait_recv()
                    self.load(half, number).wait()
            else:
                self.copy(half, stage).wait_recv()
            if stage == self.bits - 1:
                continue
            base = bit_of(self.me, self.orders[half][stage]) * self.count(stage)

            def add(number, carry, half=half, base=base):
                place = self.offset(stage) + number
                if stage == 0:
                    kept = self.keep[half, number]
                else:
                    kept = self.buffer[half, self.offset(stage - 1) + base + number]
                self.buffer[half, place] = (
                    self.buffer[half, place].astype(F32) + kept.astype(F32)
                ).astype(BF)
                return carry

            lax.fori_loop(0, self.count(stage), add, 0)
            self.copy(half, stage + 1).start()

    def result(self, half):
        stage = self.bits - 1
        base = bit_of(self.me, self.orders[half][stage])
        return self.buffer[half, self.offset(stage)].astype(F32) + self.buffer[
            half, self.offset(stage - 1) + base
        ].astype(F32)

    def drain(self):
        for half in range(2):
            for number in range(self.count(0)):
                self.first_copy(half, number).wait_send()
            for stage in range(1, self.bits):
                self.copy(half, stage).wait_send()


def forward_kernel(
    n,
    dp,
    kv_local,
    x_ref,
    gains_ref,
    wq_ref,
    wgu_ref,
    wo_ref,
    wd_ref,
    cot_ref,
    seg_ref,
    pos_ref,
    freq_ref,
    wqkv_hbm,
    wout_hbm,
    wgu_hbm,
    wd_hbm,
    g1_hbm,
    q_hbm,
    k_hbm,
    v_hbm,
    o_hbm,
    cos_hbm,
    low_hbm,
    high_hbm,
    prob_hbm,
    gf_all,
    m_ref,
    n2_ref,
    stat_ref,
    g1,
    wqkv,
    wout,
    own_qkv,
    own_out,
    own_gu,
    q_ref,
    k_ref,
    v_ref,
    o_ref,
    cos_ref,
    low_ref,
    high_ref,
    v_t,
    key_seg,
    key_pos,
    bias,
    prob,
    part,
    sums,
    load_sem,
    out_sem,
    prob_sem,
    own_sem,
    n1_send,
    n1_recv,
    ag_send,
    ag_recv,
    rs_send,
    rs_recv,
    keep_sem,
    dp_send,
    dp_recv,
):
    z = lax.axis_index("tensor")
    me = lax.axis_index("dp")
    tokens, width = x_ref.shape
    heads = REPEAT * kv_local
    ff = wd_ref.shape[2]
    half_head = HEAD_WIDTH // 2
    dp_bits = dp.bit_length() - 1
    gain_one, gain_two = gains_ref[0, 0:1, :], gains_ref[0, 1:2, :]
    first_row = pl.multiple_of(z * tokens, tokens)

    def normalize(rows):
        place = pl.ds(pl.multiple_of(first_row + rows.start, rows.size), rows.size)
        g1[place, :] = norm_rows(x_ref[rows, :], gain_one)[0].astype(BF)

    by_rows(tokens, normalize)
    for padded, shard in ((own_qkv, wq_ref), (own_out, wo_ref)):
        padded[...] = jnp.zeros_like(padded)
        for head in range(padded.shape[1] // LANES):
            padded[:, head * LANES : head * LANES + HEAD_WIDTH] = shard[
                0, :, head * HEAD_WIDTH : (head + 1) * HEAD_WIDTH
            ]
    entry_barrier(n, [{"dp": across(me, bit)} for bit in range(dp_bits)])
    spread = Gather(n, lambda slot: g1.at[rows_at(slot, tokens)], n1_send, n1_recv)
    spread.begin()
    shards = [
        Doubling(dp, source, target, keep_sem.at[k], dp_send.at[k], dp_recv.at[k])
        for k, (source, target) in enumerate(
            [
                (own_qkv, wqkv_hbm),
                (own_out, wout_hbm),
                (own_gu, wgu_hbm),
                (wd_ref.at[0], wd_hbm),
            ]
        )
    ]
    early, late = shards[:2], shards[2:]
    for shard in early:
        shard.begin()
    own_gu[:, :ff] = wgu_ref[0, :, 0, :]
    own_gu[:, ff:] = wgu_ref[0, :, 1, :]

    def tables(slot, carry):
        rows = rows_at(slot, tokens)

        def column(row):
            return jnp.broadcast_to(row.astype(F32), (LANES, tokens)).T

        places = column(pos_ref[slot])
        key_pos[rows, :] = places
        key_seg[rows, :] = column(seg_ref[slot])
        angles = places * freq_ref[...]
        sine = jnp.sin(angles)
        lane = lax.broadcasted_iota(jnp.int32, sine.shape, 1)
        cos_ref[rows, :] = jnp.cos(angles)
        low_ref[rows, :] = jnp.where(lane < half_head, -sine, 0.0)
        high_ref[rows, :] = jnp.where((lane >= half_head) & (lane < HEAD_WIDTH), sine, 0.0)
        return carry

    lax.fori_loop(0, n, tables, 0)
    for shard in early:
        shard.advance(0)
    for shard in late:
        shard.begin()
    for stage in range(1, dp_bits):
        for shard in early:
            shard.advance(stage)
    for shard in early:
        shard.own().wait()
    loads = [
        pltpu.make_async_copy(wqkv_hbm, wqkv, load_sem.at[0]),
        pltpu.make_async_copy(wout_hbm, wout, load_sem.at[1]),
    ]
    for load in loads:
        load.start()
    gather = Gather(n, lambda slot: gf_all.at[rows_at(slot, tokens)], ag_send, ag_recv)
    keep = pltpu.make_async_copy(cot_ref, gf_all.at[rows_at(z, tokens)], own_sem)
    keep.start()
    loads[0].wait()
    group_width = (REPEAT + 2) * LANES

    def project(slot):
        rows = rows_at(slot, tokens)
        cosine, low, high = cos_ref[rows, :], low_ref[rows, :], high_ref[rows, :]

        def turn(values):
            return (
                values * cosine
                + pltpu.roll(values, LANES - half_head, 1) * low
                + pltpu.roll(values, half_head, 1) * high
            ).astype(BF)

        for group in range(kv_local):
            joined = nn(g1[rows, :], wqkv[:, group * group_width : (group + 1) * group_width])
            for member in range(REPEAT):
                q_ref[group * REPEAT + member, rows, :] = turn(
                    joined[:, member * LANES : (member + 1) * LANES]
                )
            k_ref[group, rows, :] = turn(joined[:, REPEAT * LANES : (REPEAT + 1) * LANES])
            values = joined[:, (REPEAT + 1) * LANES :]
            v_ref[group, rows, :] = values.astype(BF)

    def project_of(index, carry):
        came, near = (index + 1) // 2, (index + 1) % 2
        slot = z - (1 - 2 * near) * came

        @pl.when(index > 0)
        def _():
            spread.arrive(came, near, forward=None)

        @pl.when((index > 0) & (came < n - 1))
        def _():
            spread.send(came + 1, near)

        @pl.when(index == 2 * (n - 2))
        def _():
            gather.begin(cot_ref)

        for stage in range(min(2, dp_bits)):

            @pl.when(index == 3 + 2 * stage)
            def _(stage=stage):
                for shard in late:
                    shard.advance(stage)

        @pl.when((slot >= 0) & (slot < n))
        def _():
            project(slot)

        return carry

    lax.fori_loop(0, 2 * n - 1, project_of, 0)
    outs = [
        pltpu.make_async_copy(source, target, out_sem.at[k])
        for k, (source, target) in enumerate(
            [
                (q_ref, q_hbm),
                (k_ref, k_hbm),
                (v_ref, v_hbm),
                (cos_ref, cos_hbm),
                (low_ref, low_hbm),
                (high_ref, high_hbm),
                (g1, g1_hbm),
                (o_ref, o_hbm),
            ]
        )
    ]
    for out in outs[:-1]:
        out.start()
    for group in range(kv_local):
        v_t[group] = v_ref[group].astype(F32).T.astype(BF)
    loads[1].wait()
    scatter = Scatter(n, sums, rs_send, rs_recv)
    log2_scale = HEAD_WIDTH ** (-0.5) * 1.4426950408889634

    def attend(target):
        rows = rows_at(target, tokens)
        for first in range(0, tokens, LANES):
            lanes = slice(first, first + LANES)
            seen = (key_seg[...] == 0.0) | (
                key_seg[...] == seg_ref[target, :, lanes].astype(F32)
            )
            seen = seen & (key_pos[...] <= pos_ref[target, :, lanes].astype(F32))
            bias[:, lanes] = jnp.where(seen, 0.0, -1e30)

        def one_head(head, carry):
            group = head // REPEAT
            scores = nt(k_ref[group], q_ref[head, rows, :]) * log2_scale + bias[...]
            top = jnp.max(scores, axis=0, keepdims=True)
            weights = jnp.exp2(scores - top)
            total = jnp.sum(weights, axis=0, keepdims=True)
            prob[head] = (weights * (1.0 / total)).astype(BF)
            mixed = nn(v_t[group], prob[head])
            o_ref[rows, rows_at(head, LANES)] = mixed.T.astype(BF)
            return carry

        lax.fori_loop(0, heads, one_head, 0)
        out = pltpu.make_async_copy(prob, prob_hbm.at[target], prob_sem)
        out.start()
        for first in range(0, width, 512):
            part[:, first : first + 512] = nt(o_ref[rows, :], wout[first : first + 512, :])
        out.wait()

    def turn_of(index, carry):
        step, side = index // 2 + 1, index % 2
        target, valid = scatter.turn(step, side)

        @pl.when(valid)
        def _():
            attend(target)

            @pl.when(step < n)
            def _():
                scatter.push(step, side, lambda: part[...])

        for stage in range(2, dp_bits):

            @pl.when(index == 2 * (stage - 2) + 1)
            def _(stage=stage):
                for shard in late:
                    shard.advance(stage)

        @pl.when(step < n)
        def _():
            gather.arrive(step, side, forward=None)

        @pl.when(step < n - 1)
        def _():
            gather.send(step + 1, side)

        return carry

    lax.fori_loop(0, 2 * (n - 1) + 1, turn_of, 0)
    outs[-1].start()
    scatter.settle(part)
    stat_ref[...] = jnp.zeros_like(stat_ref)

    def finish(rows):
        branch = part[rows, :]
        middle = x_ref[rows, :] + branch
        m_ref[rows, :] = middle
        n2_ref[rows, :] = norm_rows(middle, gain_two)[0].astype(BF)
        stat_ref[0:1, :] += jnp.sum(middle * middle, axis=0, keepdims=True)
        stat_ref[1:2, :] += jnp.sum(branch * branch, axis=0, keepdims=True)

    by_rows(tokens, finish)
    keep.wait()
    for out in outs:
        out.wait()
    spread.drain()
    gather.drain(cot_ref)
    scatter.drain()
    for shard in early:
        shard.drain(own=False)
    for shard in late:
        shard.drain()


def forward(n, dp, kv_local, x, gains, w_qkv, w_gate_up, w_out, w_down, cot, seg, pos, freq):
    tokens, width = x.shape
    group_len = n * tokens
    heads = REPEAT * kv_local
    owned = w_qkv.shape[1]
    ff = w_down.shape[2]
    lanes, out_lanes = (REPEAT + 2) * kv_local * LANES, heads * LANES
    vmem = pl.BlockSpec(memory_space=pltpu.VMEM)
    hbm = pl.BlockSpec(memory_space=pl.ANY)
    kept = [
        ((heads, group_len, LANES), BF),
        ((kv_local, group_len, LANES), BF),
        ((kv_local, group_len, LANES), BF),
        ((group_len, out_lanes), BF),
        ((group_len, LANES), F32),
        ((group_len, LANES), F32),
        ((group_len, LANES), F32),
    ]
    flops = 2 * group_len * (
        width * lanes + width * out_lanes + 2 * heads * group_len * LANES
    )
    return pl.pallas_call(
        functools.partial(forward_kernel, n, dp, kv_local),
        out_shape=(
            jax.ShapeDtypeStruct((width, lanes), BF),
            jax.ShapeDtypeStruct((width, out_lanes), BF),
            jax.ShapeDtypeStruct((width, 2 * ff), BF),
            jax.ShapeDtypeStruct((width, ff), BF),
            jax.ShapeDtypeStruct((group_len, width), BF),
            *[jax.ShapeDtypeStruct(shape, kind) for shape, kind in kept],
            jax.ShapeDtypeStruct((n, heads, group_len, tokens), BF),
            jax.ShapeDtypeStruct((group_len, width), BF),
            jax.ShapeDtypeStruct((tokens, width), F32),
            jax.ShapeDtypeStruct((tokens, width), BF),
            jax.ShapeDtypeStruct((8, width), F32),
        ),
        in_specs=[vmem] * 10,
        out_specs=(hbm,) * 14 + (vmem,) * 3,
        scratch_shapes=[
            pltpu.VMEM((group_len, width), BF),
            pltpu.VMEM((width, lanes), BF),
            pltpu.VMEM((width, out_lanes), BF),
            pltpu.VMEM((owned, lanes), BF),
            pltpu.VMEM((owned, out_lanes), BF),
            pltpu.VMEM((owned, 2 * ff), BF),
            *[pltpu.VMEM(shape, kind) for shape, kind in kept],
            pltpu.VMEM((kv_local, LANES, group_len), BF),
            pltpu.VMEM((group_len, LANES), F32),
            pltpu.VMEM((group_len, LANES), F32),
            pltpu.VMEM((group_len, tokens), F32),
            pltpu.VMEM((heads, group_len, tokens), BF),
            pltpu.VMEM((tokens, width), F32),
            pltpu.VMEM((2, n, tokens, width), BF),
            pltpu.SemaphoreType.DMA((2,)),
            pltpu.SemaphoreType.DMA((8,)),
            pltpu.SemaphoreType.DMA,
            pltpu.SemaphoreType.DMA,
            *[pltpu.SemaphoreType.DMA((2, n))] * 6,
            pltpu.SemaphoreType.DMA((4,)),
            pltpu.SemaphoreType.DMA((4, 2, dp)),
            pltpu.SemaphoreType.DMA((4, 2, dp)),
        ],
        compiler_params=pltpu.CompilerParams(
            collective_id=1, has_side_effects=True, vmem_limit_bytes=VMEM_LIMIT
        ),
        cost_estimate=pl.CostEstimate(
            flops=flops, bytes_accessed=200 * tokens * width * 2, transcendentals=0
        ),
        name="attend_forward",
    )(x, gains, w_qkv, w_gate_up, w_out, w_down, cot, seg, pos, freq)


def feed_kernel(
    n,
    chunks,
    n2_ref,
    gf_hbm,
    wgu_hbm,
    wd_hbm,
    m_ref,
    gain_ref,
    cot_ref,
    z_hbm,
    dm_ref,
    ga_ref,
    dgain_ref,
    dwgu_hbm,
    dwgu_ref,
    n2_all,
    gf_all,
    z_all,
    dgu,
    wgu,
    wd,
    part,
    dn2,
    sums,
    load_sem,
    gf_sem,
    z_sem,
    dw_sem,
    ag_send,
    ag_recv,
    rs_send,
    rs_recv,
):
    z = lax.axis_index("tensor")
    tokens, width = n2_ref.shape
    ff = wd_hbm.shape[1]
    piece = tokens // chunks
    rows_chunk = n * piece
    load_gu = pltpu.make_async_copy(wgu_hbm, wgu, load_sem.at[0])
    load_d = pltpu.make_async_copy(wd_hbm, wd, load_sem.at[1])

    def load_gf(chunk, slot):
        return pltpu.make_async_copy(
            gf_hbm.at[pl.ds(pl.multiple_of(slot * tokens + chunk * piece, piece), piece)],
            gf_all.at[pl.ds(pl.multiple_of(chunk * rows_chunk + slot * piece, piece), piece)],
            gf_sem.at[chunk, slot],
        )

    load_gu.start()
    load_d.start()
    for chunk in range(chunks):
        for slot in range(n):
            load_gf(chunk, slot).start()
        n2_all[pl.ds(pl.multiple_of(chunk * rows_chunk + z * piece, piece), piece), :] = n2_ref[
            chunk * piece : (chunk + 1) * piece, :
        ]
    entry_barrier(n)

    def gather_of(chunk):
        return Gather(
            n,
            lambda slot: n2_all.at[
                pl.ds(pl.multiple_of(chunk * rows_chunk + slot * piece, piece), piece)
            ],
            ag_send.at[chunk],
            ag_recv.at[chunk],
        )

    def scatter_of(chunk):
        return Scatter(n, sums.at[chunk], rs_send.at[chunk], rs_recv.at[chunk])

    gather_of(0).begin()

    def scatter_end(chunk):
        own = dn2.at[rows_at(chunk, piece)]
        own[...] = part[chunk, rows_at(z, piece), :]
        scatter_of(chunk).settle(own)

    block = 256
    hidden_blocks = ff // block
    out_blocks = width // 512

    def hidden_block(chunk, index):
        rows = rows_at(chunk, rows_chunk)
        cols = rows_at(index, block)
        up_cols = pl.ds(pl.multiple_of(ff + index * block, block), block)
        gate = nn(n2_all[rows, :], wgu[:, cols])
        up = nn(n2_all[rows, :], wgu[:, up_cols])
        dz = nn(gf_all[rows, :], wd[:, cols])
        s = 1.0 / (1.0 + jnp.exp(-gate))
        act = gate * s
        z_all[rows, cols] = (act * up).astype(BF)
        dgu[rows, cols] = (dz * up * (s * (1.0 + gate * (1.0 - s)))).astype(BF)
        dgu[rows, up_cols] = (dz * act).astype(BF)

    def out_block(chunk, index):
        rows = rows_at(chunk, rows_chunk)
        cols = rows_at(index, 512)
        part[chunk, :, cols] = nt(dgu[rows, :], wgu[cols, :])

    def z_out(chunk):
        rows = rows_at(chunk, rows_chunk)
        return pltpu.make_async_copy(z_all.at[rows], z_hbm.at[rows], z_sem.at[chunk])

    def compute(chunk):
        for slot in range(n):
            load_gf(chunk, slot).wait()

        def hidden(index, carry):
            hidden_block(chunk, index)
            return carry

        def out(index, carry):
            out_block(chunk, index)
            return carry

        lax.fori_loop(0, hidden_blocks, hidden, 0)
        lax.fori_loop(0, out_blocks, out, 0)
        z_out(chunk).start()

    def grad_gu(index, carry):
        cols = rows_at(index, 256)
        dwgu_ref[:, cols] = tn(n2_all[...], dgu[:, cols]).astype(BF)
        dw_out(index).start()
        return carry

    def dw_out(index):
        cols = rows_at(index, 256)
        return pltpu.make_async_copy(dwgu_ref.at[:, cols], dwgu_hbm.at[:, cols], dw_sem.at[index])

    blocks = 2 * ff // 256

    def within(chunk):
        return (chunk >= 0) & (chunk < chunks)

    def stage(index, carry):
        for step in range(n - 1, 0, -1):
            chunk = index - (step - 1)

            @pl.when(within(chunk))
            def _(step=step, chunk=chunk):
                for side in range(2):
                    gather_of(chunk).arrive(step, side, forward=step < n - 1)

        @pl.when(index + 1 < chunks)
        def _():
            gather_of(index + 1).begin()

        ready = index - (n - 2)

        @pl.when(within(ready - (n - 1)))
        def _():
            scatter_end(ready - (n - 1))

        def push(chunk, step):
            scatter = scatter_of(chunk)
            for side in range(2):
                target, valid = scatter.turn(step, side)

                @pl.when(valid)
                def _(side=side, target=target):
                    scatter.push(step, side, lambda: part[chunk, rows_at(target, piece), :])

        for step in range(n - 1, 1, -1):
            chunk = ready - (step - 1)

            @pl.when(within(chunk))
            def _(step=step, chunk=chunk):
                push(chunk, step)

        @pl.when(ready == 0)
        def _():
            load_gu.wait()
            load_d.wait()

        @pl.when(within(ready))
        def _():
            compute(ready)
            push(ready, 1)

        @pl.when(ready >= chunks)
        def _():
            late = ready - chunks
            lax.fori_loop(blocks * late // (n - 1), blocks * (late + 1) // (n - 1), grad_gu, 0)

        return carry

    lax.fori_loop(0, chunks + 2 * n - 3, stage, 0)
    gain = gain_ref[0, 1:2, :]
    dgain_ref[...] = jnp.zeros_like(dgain_ref)

    def finish(rows):
        middle = m_ref[rows, :]
        dn = dn2[rows, :]
        inverse = lax.rsqrt(jnp.mean(middle * middle, axis=-1, keepdims=True) + norm_eps)
        scaled = dn * gain
        dgain_ref[0:1, :] += jnp.sum(dn * middle * inverse, axis=0, keepdims=True)
        dm = (
            inverse * scaled
            - middle * inverse**3 * jnp.mean(scaled * middle, axis=-1, keepdims=True)
            + cot_ref[rows, :].astype(F32)
        )
        dm_ref[rows, :] = dm
        ga_ref[rows, :] = dm.astype(BF)

    by_rows(tokens, finish)
    for index in range(blocks):
        dw_out(index).wait()
    for chunk in range(chunks):
        z_out(chunk).wait()
        gather_of(chunk).drain()
        scatter_of(chunk).drain()


def feed(n, chunks, n2, gf_all, wgu, wd, m, gain, cot):
    tokens, width = n2.shape
    group_len = n * tokens
    ff = wd.shape[1]
    vmem = pl.BlockSpec(memory_space=pltpu.VMEM)
    hbm = pl.BlockSpec(memory_space=pl.ANY)
    return pl.pallas_call(
        functools.partial(feed_kernel, n, chunks),
        out_shape=(
            jax.ShapeDtypeStruct((group_len, ff), BF),
            jax.ShapeDtypeStruct((tokens, width), F32),
            jax.ShapeDtypeStruct((tokens, width), BF),
            jax.ShapeDtypeStruct((8, width), F32),
            jax.ShapeDtypeStruct((width, 2 * ff), BF),
        ),
        in_specs=[vmem, hbm, hbm, hbm, vmem, vmem, vmem],
        out_specs=(hbm, vmem, vmem, vmem, hbm),
        scratch_shapes=[
            pltpu.VMEM((width, 2 * ff), BF),
            pltpu.VMEM((group_len, width), BF),
            pltpu.VMEM((group_len, width), BF),
            pltpu.VMEM((group_len, ff), BF),
            pltpu.VMEM((group_len, 2 * ff), BF),
            pltpu.VMEM((width, 2 * ff), BF),
            pltpu.VMEM((width, ff), BF),
            pltpu.VMEM((chunks, group_len // chunks, width), F32),
            pltpu.VMEM((tokens, width), F32),
            pltpu.VMEM((chunks, 2, n, tokens // chunks, width), BF),
            pltpu.SemaphoreType.DMA((2,)),
            pltpu.SemaphoreType.DMA((chunks, n)),
            pltpu.SemaphoreType.DMA((chunks,)),
            pltpu.SemaphoreType.DMA((2 * ff // 256,)),
            pltpu.SemaphoreType.DMA((chunks, 2, n)),
            pltpu.SemaphoreType.DMA((chunks, 2, n)),
            pltpu.SemaphoreType.DMA((chunks, 2, n)),
            pltpu.SemaphoreType.DMA((chunks, 2, n)),
        ],
        compiler_params=pltpu.CompilerParams(
            collective_id=3, has_side_effects=True, vmem_limit_bytes=VMEM_LIMIT
        ),
        cost_estimate=pl.CostEstimate(
            flops=18 * group_len * width * ff, bytes_accessed=250 * tokens * width * 2, transcendentals=0
        ),
        name="feed_both",
    )(n2, gf_all, wgu, wd, m, gain, cot)


def attend_back_kernel(
    n,
    dp,
    kv_local,
    chunks,
    ga_ref,
    wout_hbm,
    wd_hbm,
    z_hbm,
    prob_hbm,
    g1_hbm,
    gf_hbm,
    dwgu_hbm,
    m_ref,
    q_ref,
    k_ref,
    v_ref,
    o_ref,
    cos_ref,
    sin_low_ref,
    sin_high_ref,
    out_ref,
    stat_ref,
    dqkv_ref,
    dw_hbm,
    grad_gu_ref,
    dw_ref,
    keep,
    held,
    ga_all,
    g1,
    gf,
    wout,
    wd,
    z_all,
    k_t,
    prob,
    d_out,
    dk,
    dv,
    part,
    sums,
    load_sem,
    gf_sem,
    prob_sem,
    dw_sem,
    ag_send,
    ag_recv,
    rs_send,
    rs_recv,
    keep_sem,
    dp_send,
    dp_recv,
):
    z = lax.axis_index("tensor")
    tokens, width = ga_ref.shape
    heads = REPEAT * kv_local
    group_len = n * tokens
    piece = tokens // chunks
    scale = HEAD_WIDTH ** (-0.5)
    loads = [
        pltpu.make_async_copy(source, target, load_sem.at[index])
        for index, (source, target) in enumerate(
            [(wout_hbm, wout), (z_hbm, z_all), (wd_hbm, wd), (g1_hbm, g1)]
        )
    ]
    for load in loads:
        load.start()
    load_out, load_z, load_d, load_g1 = loads

    def load_gf(chunk, slot):
        return pltpu.make_async_copy(
            gf_hbm.at[pl.ds(pl.multiple_of(slot * tokens + chunk * piece, piece), piece)],
            gf.at[pl.ds(pl.multiple_of((chunk * n + slot) * piece, piece), piece)],
            gf_sem.at[chunk, slot],
        )

    for chunk in range(chunks):
        for slot in range(n):
            load_gf(chunk, slot).start()

    def load_prob(slot):
        return pltpu.make_async_copy(prob_hbm.at[slot], prob, prob_sem)

    ga_all[rows_at(z, tokens), :] = ga_ref[...]
    me = lax.axis_index("dp")
    dp_bits = dp.bit_length() - 1
    entry_barrier(n, [{"dp": across(me, bit)} for bit in range(dp_bits)])
    gather = Gather(n, lambda slot: ga_all.at[rows_at(slot, tokens)], ag_send, ag_recv)
    gather.begin()
    halving = Halving(
        dp, grad_gu_ref.shape[0], dwgu_hbm, keep, held, keep_sem, dp_send, dp_recv
    )
    halving.begin()
    scatter = Scatter(n, sums, rs_send, rs_recv)
    for group in range(kv_local):
        k_t[group] = k_ref[group].astype(F32).T.astype(BF)
    dk[...] = jnp.zeros_like(dk)
    dv[...] = jnp.zeros_like(dv)
    load_out.wait()
    load_z.wait()
    load_d.wait()
    group_lanes = (REPEAT + 2) * LANES

    def turn_back(values, rows):
        return (
            values * cos_ref[rows, :]
            - pltpu.roll(values, LANES - HEAD_WIDTH // 2, 1) * sin_low_ref[rows, :]
            - pltpu.roll(values, HEAD_WIDTH // 2, 1) * sin_high_ref[rows, :]
        )

    def back(slot):
        rows = rows_at(slot, tokens)
        d_o = nn(ga_all[rows, :], wout[...])
        d_out[...] = d_o.astype(BF)

        def one_head(head, carry):
            group = head // REPEAT
            lanes = rows_at(head, LANES)
            do_h = d_out[:, lanes]
            both = do_h.astype(F32) * o_ref[rows, lanes].astype(F32)
            delta = jnp.sum(both.T, axis=0, keepdims=True)
            dprob = nt(v_ref[group], do_h)
            weights = prob[head]
            ds = (weights.astype(F32) * (dprob - delta)).astype(BF)
            dv[group] += nn(weights, do_h)
            dk[group] += nn(ds, q_ref[head, rows, :])
            dq = nn(k_t[group], ds).T * scale
            first = group * (REPEAT + 2) + head % REPEAT
            dqkv_ref[rows, rows_at(first, LANES)] = turn_back(dq, rows).astype(BF)
            return carry

        lax.fori_loop(0, heads, one_head, 0)

    def feed_rows(target):
        pieces = [
            z_all[
                pl.ds(
                    pl.multiple_of(chunk * n * piece + target * piece, piece), piece
                ),
                :,
            ]
            for chunk in range(chunks)
        ]
        rows = jnp.concatenate(pieces, axis=0) if chunks > 1 else pieces[0]
        for first in range(0, width, 512):
            part[:, first : first + 512] = nt(rows, wd[first : first + 512, :])

    def turn_of(index, carry):
        came, near = (index + 1) // 2, (index + 1) % 2
        slot = z - (1 - 2 * near) * came
        valid = (slot >= 0) & (slot < n)

        @pl.when(valid)
        def _():
            load_prob(slot).start()

        @pl.when(index > 0)
        def _():
            gather.arrive(came, near, forward=None)

        @pl.when((index > 0) & (came < n - 1))
        def _():
            gather.send(came + 1, near)

        step, side = index // 2 + 1, index % 2
        target, sends = scatter.turn(step, side)

        @pl.when(sends & (step < n))
        def _():
            feed_rows(target)
            scatter.push(step, side, lambda: part[...])

        @pl.when(valid)
        def _():
            load_prob(slot).wait()
            back(slot)

        return carry

    for chunk in range(chunks):
        for slot in range(n):
            load_gf(chunk, slot).wait()
    ff = wd_hbm.shape[1]
    down_blocks = ff // 256
    down_first = heads * LANES + dqkv_ref.shape[1]

    def grad_down(first, last):
        def body(index, carry):
            cols = rows_at(index, 256)
            place = pl.ds(pl.multiple_of(down_first + index * 256, 256), 256)
            dw_ref[:, place] = tn(gf[...], z_all[:, cols]).astype(BF)
            return carry

        lax.fori_loop(first, last, body, 0)

    turns = 2 * n - 1

    def turn_and_grad(index, carry):
        turn_of(index, 0)
        grad_down(down_blocks * index // turns, down_blocks * (index + 1) // turns)
        for stage in range(dp_bits):

            @pl.when(index == 2 * stage + 1)
            def _(stage=stage):
                halving.advance(stage)

        return carry

    lax.fori_loop(0, turns, turn_and_grad, 0)

    def finish_keys(slot, carry):
        rows = rows_at(slot, tokens)
        for group in range(kv_local):
            first = group * group_lanes + REPEAT * LANES
            dqkv_ref[rows, first : first + LANES] = turn_back(
                dk[group, rows, :] * scale, rows
            ).astype(BF)
            dqkv_ref[rows, first + LANES : first + 2 * LANES] = dv[group, rows, :].astype(BF)
        return carry

    lax.fori_loop(0, n, finish_keys, 0)
    load_g1.wait()
    out_lanes = heads * LANES

    def dw_out(which):
        first, size = (
            (down_first, ff),
            (out_lanes, dqkv_ref.shape[1]),
            (0, out_lanes),
        )[which]
        cols = slice(first, first + size)
        return pltpu.make_async_copy(dw_ref.at[:, cols], dw_hbm.at[:, cols], dw_sem.at[which])

    dw_out(0).start()

    def grad_qkv(index, carry):
        cols = rows_at(index, 256)
        place = pl.ds(pl.multiple_of(out_lanes + index * 256, 256), 256)
        dw_ref[:, place] = tn(g1[...], dqkv_ref[:, cols]).astype(BF)
        return carry

    lax.fori_loop(0, dqkv_ref.shape[1] // 256, grad_qkv, 0)
    dw_out(1).start()

    def grad_out(index, carry):
        cols = rows_at(index, 256)
        dw_ref[:, cols] = tn(ga_all[...], o_ref[:, cols]).astype(BF)
        return carry

    lax.fori_loop(0, out_lanes // 256, grad_out, 0)
    dw_out(2).start()
    for half in range(2):
        grad_gu_ref[:, half, :] = halving.result(half)
    feed_rows(z)
    scatter.settle(part)
    stat_ref[...] = jnp.zeros_like(stat_ref)

    def finish(rows):
        branch = part[rows, :]
        result = m_ref[rows, :] + branch
        out_ref[rows, :] = result
        stat_ref[0:1, :] += jnp.sum(result * result, axis=0, keepdims=True)
        stat_ref[1:2, :] += jnp.sum(branch * branch, axis=0, keepdims=True)

    by_rows(tokens, finish)
    for which in range(3):
        dw_out(which).wait()
    gather.drain()
    scatter.drain()
    halving.drain()


def attend_back(n, dp, kv_local, chunks, ga, wout, wd, z_all, prob, g1, gf, dwgu, m, q, k, v, o, tables):
    tokens, width = ga.shape
    group_len = n * tokens
    heads = REPEAT * kv_local
    ff = wd.shape[1]
    owned = width // dp
    lanes = (REPEAT + 2) * kv_local * LANES
    vmem = pl.BlockSpec(memory_space=pltpu.VMEM)
    hbm = pl.BlockSpec(memory_space=pl.ANY)
    return pl.pallas_call(
        functools.partial(attend_back_kernel, n, dp, kv_local, chunks),
        out_shape=(
            jax.ShapeDtypeStruct((tokens, width), F32),
            jax.ShapeDtypeStruct((8, width), F32),
            jax.ShapeDtypeStruct((group_len, lanes), BF),
            jax.ShapeDtypeStruct((width, heads * LANES + lanes + ff), BF),
            jax.ShapeDtypeStruct((owned, 2, ff), F32),
        ),
        in_specs=[vmem] + [hbm] * 7 + [vmem] * 8,
        out_specs=(vmem, vmem, vmem, hbm, vmem),
        scratch_shapes=[
            pltpu.VMEM((width, heads * LANES + lanes + ff), BF),
            pltpu.VMEM((2, dp // 2, owned, ff), BF),
            pltpu.VMEM((2, dp - 1, owned, ff), BF),
            pltpu.VMEM((group_len, width), BF),
            pltpu.VMEM((group_len, width), BF),
            pltpu.VMEM((group_len, width), BF),
            pltpu.VMEM(wout.shape, BF),
            pltpu.VMEM(wd.shape, BF),
            pltpu.VMEM((group_len, ff), BF),
            pltpu.VMEM((kv_local, LANES, group_len), BF),
            pltpu.VMEM((heads, group_len, tokens), BF),
            pltpu.VMEM((tokens, heads * LANES), BF),
            pltpu.VMEM((kv_local, group_len, LANES), F32),
            pltpu.VMEM((kv_local, group_len, LANES), F32),
            pltpu.VMEM((tokens, width), F32),
            pltpu.VMEM((2, n, tokens, width), BF),
            pltpu.SemaphoreType.DMA((4,)),
            pltpu.SemaphoreType.DMA((chunks, n)),
            pltpu.SemaphoreType.DMA,
            pltpu.SemaphoreType.DMA((3,)),
            pltpu.SemaphoreType.DMA((2, n)),
            pltpu.SemaphoreType.DMA((2, n)),
            pltpu.SemaphoreType.DMA((2, n)),
            pltpu.SemaphoreType.DMA((2, n)),
            pltpu.SemaphoreType.DMA((2, dp // 2)),
            pltpu.SemaphoreType.DMA((2, dp)),
            pltpu.SemaphoreType.DMA((2, dp)),
        ],
        compiler_params=pltpu.CompilerParams(
            collective_id=4, has_side_effects=True, vmem_limit_bytes=VMEM_LIMIT
        ),
        cost_estimate=pl.CostEstimate(
            flops=8 * group_len * width * ff, bytes_accessed=200 * tokens * width * 2, transcendentals=0
        ),
        name="attend_backward",
    )(ga, wout, wd, z_all, prob, g1, gf, dwgu, m, q, k, v, o, *tables)


def last_kernel(
    n,
    dp,
    cells,
    out_heads,
    qkv_heads,
    dqkv_ref,
    wqkv_ref,
    x_ref,
    dm_ref,
    gain_ref,
    dgain_two_ref,
    stat_one_ref,
    stat_two_ref,
    g1_hbm,
    dw_hbm,
    dx_ref,
    gains_ref,
    rms_ref,
    grad_out_ref,
    grad_qkv_ref,
    grad_down_ref,
    g1,
    part,
    sums,
    keep,
    blocks,
    vector,
    vectors,
    rs_send,
    rs_recv,
    g1_sem,
    keep_sem,
    dp_send,
    dp_recv,
    all_send,
    all_recv,
):
    z = lax.axis_index("tensor")
    me = lax.axis_index("dp")
    tokens, width = x_ref.shape
    load_g1 = pltpu.make_async_copy(g1_hbm, g1, g1_sem)
    load_g1.start()
    dp_bits, z_bits = dp.bit_length() - 1, n.bit_length() - 1
    partners = [{"dp": across(me, bit)} for bit in range(dp_bits)]
    partners += [{"tensor": across(z, bit)} for bit in range(z_bits)]
    entry_barrier(n, partners[:dp_bits] + partners[dp_bits + 1 :])
    halving = Halving(dp, grad_out_ref.shape[0], dw_hbm, keep, blocks, keep_sem, dp_send, dp_recv)
    halving.begin()
    scatter = Scatter(n, sums, rs_send, rs_recv)
    gain = gain_ref[0, 0:1, :]
    vector[...] = jnp.zeros_like(vector)
    vector[1:2, :] = dgain_two_ref[0:1, :]
    vector[2:3, :] = stat_one_ref[0:1, :]
    vector[3:4, :] = stat_two_ref[0:1, :]
    vector[4:5, :] = stat_one_ref[1:2, :]
    vector[5:6, :] = stat_two_ref[1:2, :]
    load_g1.wait()

    def compute(index, carry):
        step, side = index // 2 + 1, index % 2
        target, due = scatter.turn(step, side)

        @pl.when(due)
        def _():
            rows = rows_at(target, tokens)

            def block(number, carry):
                cols = rows_at(number, 256)
                values = nt(dqkv_ref[rows, :], wqkv_ref[cols, :])
                part[rows, cols] = values
                vector[0:1, cols] += jnp.sum(
                    values * g1[rows, cols].astype(F32), axis=0, keepdims=True
                )
                return carry

            lax.fori_loop(0, width // 256, block, 0)

            @pl.when((step < n) & jnp.logical_not(scatter.has_source(side)))
            def _():
                scatter.push(step, side, lambda: part[rows, :])

        return carry

    lax.fori_loop(0, 2 * n - 1, compute, 0)
    vector[0:1, :] = vector[0:1, :] / gain

    def exchange(index):
        return pltpu.make_async_remote_copy(
            src_ref=vector if index == 0 else vectors.at[index - 1],
            dst_ref=vectors.at[index],
            send_sem=all_send.at[index],
            recv_sem=all_recv.at[index],
            device_id=partners[index],
            device_id_type=MESH,
        )

    def meet(index):
        exchange(index).wait_recv()
        held = vector[...] if index == 0 else vectors[index - 1]
        vectors[index] += held
        if index + 1 < len(partners):
            exchange(index + 1).start()

    exchange(0).start()
    stages = max(len(partners), dp_bits)
    for step in range(1, n):
        for side in range(2):
            target, sends = scatter.turn(step, side)

            @pl.when(sends & scatter.has_source(side))
            def _(step=step, side=side, target=target):
                rows = rows_at(target, tokens)
                scatter.push(step, side, lambda: part[rows, :])

        for index in range(stages * (step - 1) // (n - 1), stages * step // (n - 1)):
            if index < len(partners):
                meet(index)
        for index in range(dp_bits * (step - 1) // (n - 1), dp_bits * step // (n - 1)):
            halving.advance(index)
    place = 0
    for half in range(2):
        block = halving.result(half)
        for index in range(block.shape[1] // LANES):
            values = block[:, index * LANES : (index + 1) * LANES]
            if place < out_heads:
                grad_out_ref[:, place * HEAD_WIDTH : (place + 1) * HEAD_WIDTH] = values[
                    :, :HEAD_WIDTH
                ]
            elif place < out_heads + qkv_heads:
                head = place - out_heads
                grad_qkv_ref[:, head * HEAD_WIDTH : (head + 1) * HEAD_WIDTH] = values[
                    :, :HEAD_WIDTH
                ]
            else:
                first = (place - out_heads - qkv_heads) * LANES
                grad_down_ref[:, first : first + LANES] = values
            place += 1
    total = vectors[len(partners) - 1]
    gains_ref[0] = total[0:2, :]
    squares = jnp.sqrt(jnp.sum(total, axis=1, keepdims=True) * (1.0 / cells))
    row = lax.broadcasted_iota(jnp.int32, (8, 4), 0)
    column = lax.broadcasted_iota(jnp.int32, (8, 4), 1)
    rms_ref[...] = jnp.sum(jnp.where(row == column + 2, squares, 0.0), axis=0, keepdims=True)
    own = part.at[rows_at(z, tokens)]
    scatter.settle(own)

    def finish(rows):
        values = x_ref[rows, :]
        dn = own[rows, :]
        inverse = lax.rsqrt(jnp.mean(values * values, axis=-1, keepdims=True) + norm_eps)
        scaled = dn * gain
        dx_ref[rows, :] = (
            inverse * scaled
            - values * inverse**3 * jnp.mean(scaled * values, axis=-1, keepdims=True)
            + dm_ref[rows, :]
        )

    by_rows(tokens, finish)
    for index in range(len(partners)):
        exchange(index).wait_send()
    halving.drain()
    scatter.drain()


def last(n, dqkv, wqkv, x, dm, gain, dgain_two, stat_one, stat_two, g1, dw, out_columns, qkv_columns, ff):
    tokens, width = x.shape
    dp = lax.axis_size("dp")
    owned = width // dp
    stages = (dp.bit_length() - 1) + (n.bit_length() - 1)
    half = dw.shape[1] // 2
    vmem = pl.BlockSpec(memory_space=pltpu.VMEM)
    hbm = pl.BlockSpec(memory_space=pl.ANY)
    return pl.pallas_call(
        functools.partial(
            last_kernel,
            n,
            dp,
            tokens * width * dp * n,
            out_columns // HEAD_WIDTH,
            qkv_columns // HEAD_WIDTH,
        ),
        out_shape=(
            jax.ShapeDtypeStruct((tokens, width), F32),
            jax.ShapeDtypeStruct((1, 2, width), F32),
            jax.ShapeDtypeStruct((1, 4), F32),
            jax.ShapeDtypeStruct((owned, out_columns), F32),
            jax.ShapeDtypeStruct((owned, qkv_columns), F32),
            jax.ShapeDtypeStruct((owned, ff), F32),
        ),
        in_specs=[vmem] * 8 + [hbm] * 2,
        out_specs=(vmem,) * 6,
        scratch_shapes=[
            pltpu.VMEM((n * tokens, width), BF),
            pltpu.VMEM((n * tokens, width), F32),
            pltpu.VMEM((2, n, tokens, width), BF),
            pltpu.VMEM((2, dp // 2, owned, half), BF),
            pltpu.VMEM((2, dp - 1, owned, half), BF),
            pltpu.VMEM((8, width), F32),
            pltpu.VMEM((stages, 8, width), F32),
            pltpu.SemaphoreType.DMA((2, n)),
            pltpu.SemaphoreType.DMA((2, n)),
            pltpu.SemaphoreType.DMA,
            pltpu.SemaphoreType.DMA((2, dp // 2)),
            pltpu.SemaphoreType.DMA((2, dp)),
            pltpu.SemaphoreType.DMA((2, dp)),
            pltpu.SemaphoreType.DMA((stages,)),
            pltpu.SemaphoreType.DMA((stages,)),
        ],
        compiler_params=pltpu.CompilerParams(
            collective_id=5, has_side_effects=True, vmem_limit_bytes=VMEM_LIMIT
        ),
        cost_estimate=pl.CostEstimate(
            flops=2 * dqkv.size * width, bytes_accessed=150 * tokens * width * 2, transcendentals=0
        ),
        name="input_gradient",
    )(dqkv, wqkv, x, dm, gain, dgain_two, stat_one, stat_two, g1, dw)


def per_device(inputs, norm_gains, w_qkv, w_gate_up, w_out, w_down, segments, positions, cotangent):
    n, dp = lax.axis_size("tensor"), lax.axis_size("dp")
    tokens, width = inputs.shape
    kv_local = w_out.shape[2] // (REPEAT * HEAD_WIDTH)
    ff_local = w_down.shape[2]
    chunks = 4
    half = HEAD_WIDTH // 2
    freq_steps = jnp.arange(half, dtype=F32) * (2.0 / HEAD_WIDTH)
    inverse = jnp.power(rope_base, -freq_steps)
    freq = jnp.concatenate([inverse, inverse, jnp.zeros((LANES - HEAD_WIDTH,), F32)])[None]

    (
        wqkv,
        wout,
        wgu,
        wd,
        g1,
        q,
        k,
        v,
        o,
        cosine,
        low,
        high,
        prob,
        gf_all,
        m,
        n2,
        stat_one,
    ) = forward(
        n,
        dp,
        kv_local,
        inputs,
        norm_gains,
        w_qkv,
        w_gate_up,
        w_out,
        w_down,
        cotangent,
        segments.reshape(n, 1, tokens),
        positions.reshape(n, 1, tokens),
        freq,
    )
    z_all, dm, ga, dgain_two, dwgu = feed(n, chunks, n2, gf_all, wgu, wd, m, norm_gains, cotangent)
    output, stat_two, dqkv, dw, grad_gu = attend_back(
        n,
        dp,
        kv_local,
        chunks,
        ga,
        wout,
        wd,
        z_all,
        prob,
        g1,
        gf_all,
        dwgu,
        m,
        q,
        k,
        v,
        o,
        (cosine, low, high),
    )
    input_grad, gain_total, rms, grad_out, grad_qkv, grad_down = last(
        n,
        dqkv,
        wqkv,
        inputs,
        dm,
        norm_gains,
        dgain_two,
        stat_one,
        stat_two,
        g1,
        dw,
        w_out.shape[2],
        w_qkv.shape[2],
        ff_local,
    )
    return (
        output,
        input_grad,
        grad_qkv[None],
        grad_gu[None],
        grad_out[None],
        grad_down[None],
        gain_total,
        rms,
    )


def solution(mesh):
    rows = P(("dp", "tensor"), None)
    weights = P(None, "dp", "tensor")
    pairs = P(None, "dp", None, "tensor")
    return jax.shard_map(
        per_device,
        mesh=mesh,
        in_specs=(rows, P(), weights, pairs, weights, weights, P("dp"), P("dp"), rows),
        out_specs=(rows, rows, weights, pairs, weights, weights, P(), P()),
        check_vma=False,
    )
```

```python
import functools

import jax
import jax.numpy as jnp
from jax import lax
from jax.experimental import pallas as pl
from jax.experimental.pallas import tpu as pltpu
from jax.sharding import PartitionSpec as P

HEADS = 16
KV_HEADS = 8
HEAD_WIDTH = 96
REPEAT = HEADS // KV_HEADS
LANES = 128

norm_eps = 1e-05
rope_base = 100000.0
MESH = pl.DeviceIdType.MESH
BF = jnp.bfloat16
F32 = jnp.float32
VMEM_LIMIT = 60 * 2**20
PIECES = 1
LAG = 2


def nn(a, b):
    return lax.dot_general(a, b, (((1,), (0,)), ((), ())), preferred_element_type=F32)


def nt(a, b):
    return lax.dot_general(a, b, (((1,), (1,)), ((), ())), preferred_element_type=F32)


def tn(a, b):
    return lax.dot_general(a, b, (((0,), (0,)), ((), ())), preferred_element_type=F32)


def rows_at(index, size):
    return pl.ds(pl.multiple_of(index * size, size), size)


def greet(n, others=()):
    z = lax.axis_index("tensor")
    barrier = pltpu.get_barrier_semaphore()

    @pl.when(z > 0)
    def _():
        pl.semaphore_signal(barrier, inc=1, device_id={"tensor": z - 1}, device_id_type=MESH)

    @pl.when(z < n - 1)
    def _():
        pl.semaphore_signal(barrier, inc=1, device_id={"tensor": z + 1}, device_id_type=MESH)

    for other in others:
        pl.semaphore_signal(barrier, inc=1, device_id=other, device_id_type=MESH)


def greeted(n, others=()):
    z = lax.axis_index("tensor")
    barrier = pltpu.get_barrier_semaphore()

    @pl.when((z > 0) & (z < n - 1))
    def _():
        pl.semaphore_wait(barrier, 2 + len(others))

    @pl.when((z == 0) | (z == n - 1))
    def _():
        pl.semaphore_wait(barrier, 1 + len(others))


def bit_of(index, bit):
    return (index // (1 << bit)) % 2


def across(index, bit):
    return index + (1 << bit) * (1 - 2 * bit_of(index, bit))


class Gather:
    def __init__(self, n, at, send_sem, recv_sem):
        self.n, self.at, self.send_sem, self.recv_sem = n, at, send_sem, recv_sem
        self.z = lax.axis_index("tensor")
        self.pieces = send_sem.shape[-1]

    def copy(self, slot, step, side, piece, source=None):
        block = self.at(slot)
        size = block.shape[0] // self.pieces
        rows = pl.ds(piece * size, size)
        return pltpu.make_async_remote_copy(
            src_ref=(block if source is None else source).at[rows],
            dst_ref=block.at[rows],
            send_sem=self.send_sem.at[side, step, piece],
            recv_sem=self.recv_sem.at[side, step, piece],
            device_id={"tensor": self.z + 1 - 2 * side},
            device_id_type=MESH,
        )

    def sends(self, step, side):
        z, n = self.z, self.n
        slot = z - (1 - 2 * side) * (step - 1)
        target = z + 1 - 2 * side
        return slot, (slot >= 0) & (slot < n) & (target >= 0) & (target < n)

    def send(self, step, side, piece, source=None, where=True):
        slot, valid = self.sends(step, side)

        @pl.when(valid if where is True else valid & where)
        def _():
            self.copy(slot, step, side, piece, source).start()

    def begin(self, source=None):
        for piece in range(self.pieces):
            for side in range(2):
                self.send(1, side, piece, source)

    def begin_where(self, passes_on):
        for side in range(2):
            source = self.z - (1 - 2 * side)
            other = (source >= 0) & (source < self.n)
            for piece in range(self.pieces):
                self.send(1, side, piece, where=other if passes_on else jnp.logical_not(other))

    def arrive(self, step, side, forward):
        z, n = self.z, self.n
        slot = z - (1 - 2 * side) * step
        for piece in range(self.pieces):

            @pl.when((slot >= 0) & (slot < n))
            def _(piece=piece):
                self.copy(slot, step, side, piece).wait_recv()

            if forward is not False:
                self.send(step + 1, side, piece, where=forward)

    def drain(self, source=None):
        for step in range(1, self.n):
            for side in range(2):
                slot, valid = self.sends(step, side)
                for piece in range(self.pieces):

                    @pl.when(valid)
                    def _(slot=slot, step=step, side=side, piece=piece):
                        self.copy(
                            slot, step, side, piece, source if step == 1 else None
                        ).wait_send()


class Scatter:
    def __init__(self, n, buffer, send_sem, recv_sem):
        self.n, self.buffer, self.send_sem, self.recv_sem = n, buffer, send_sem, recv_sem
        self.z = lax.axis_index("tensor")
        self.pieces = send_sem.shape[-1]
        self.size = buffer.shape[2] // self.pieces

    def rows(self, piece):
        return pl.ds(piece * self.size, self.size)

    def copy(self, step, side, piece):
        return pltpu.make_async_remote_copy(
            src_ref=self.buffer.at[side, step - 1, self.rows(piece)],
            dst_ref=self.buffer.at[side, step, self.rows(piece)],
            send_sem=self.send_sem.at[side, step, piece],
            recv_sem=self.recv_sem.at[side, step, piece],
            device_id={"tensor": self.z + 1 - 2 * side},
            device_id_type=MESH,
        )

    def turn(self, step, side):
        z, n = self.z, self.n
        return z + (1 - 2 * side) * (n - step), step >= 1 + z + side * (n - 1 - 2 * z)

    def has_source(self, side):
        source = self.z - (1 - 2 * side)
        return (source >= 0) & (source < self.n)

    def push(self, step, side, part, first=0):
        has_source = self.has_source(side)
        for piece in range(self.pieces):
            slot = self.buffer.at[side, step - 1, self.rows(piece)]
            rows = pl.ds(pl.multiple_of(first + piece * self.size, self.size), self.size)

            @pl.when(has_source)
            def _(piece=piece, slot=slot, rows=rows):
                self.copy(step - 1, side, piece).wait_recv()
                slot[...] = (part[rows, :] + slot[...].astype(F32)).astype(BF)

            @pl.when(jnp.logical_not(has_source))
            def _(slot=slot, rows=rows):
                slot[...] = part[rows, :].astype(BF)

            self.copy(step, side, piece).start()

    def settle(self, total_ref, then=None):
        for piece in range(self.pieces):
            for side in range(2):

                @pl.when(self.has_source(side))
                def _(side=side, piece=piece):
                    rows = self.rows(piece)
                    self.copy(self.n - 1, side, piece).wait_recv()
                    total_ref[rows, :] += self.buffer[side, self.n - 1, rows, :].astype(F32)

            if then is not None:
                then(piece, piece * self.size, self.size)

    def drain(self):
        for step in range(1, self.n):
            for side in range(2):
                for piece in range(self.pieces):

                    @pl.when(self.turn(step, side)[1])
                    def _(step=step, side=side, piece=piece):
                        self.copy(step, side, piece).wait_send()


def by_rows(rows, body, first=0, block=32):
    def step(index, carry):
        body(pl.ds(pl.multiple_of(first + index * block, block), block))
        return carry

    lax.fori_loop(0, rows // block, step, 0)


def norm_rows(values, gain):
    inverse = lax.rsqrt(jnp.mean(values * values, axis=-1, keepdims=True) + norm_eps)
    return values * inverse * gain, inverse


class Doubling:
    def __init__(self, size, source, target, keep_sem, send_sem, recv_sem):
        self.source, self.target = source, target
        self.keep_sem, self.send_sem, self.recv_sem = keep_sem, send_sem, recv_sem
        self.rows, columns = source.shape
        self.half = columns // 2
        self.me = lax.axis_index("dp")
        self.bits = size.bit_length() - 1
        rest = list(range(1, self.bits))
        self.orders = (rest + [0], rest[::-1] + [0])

    def index(self, order, stage, number):
        index = self.me
        for place in range(stage):
            if (number >> place) & 1:
                index = across(index, order[place])
        return index

    def copy(self, half, stage, number):
        order = self.orders[half]
        columns = slice(half * self.half, (half + 1) * self.half)
        place = self.target.at[rows_at(self.index(order, stage, number), self.rows), columns]
        return pltpu.make_async_remote_copy(
            src_ref=self.source.at[:, columns] if number == 0 else place,
            dst_ref=place,
            send_sem=self.send_sem.at[half, (1 << stage) + number],
            recv_sem=self.recv_sem.at[half, (1 << stage) + number],
            device_id={"dp": across(self.me, order[stage])},
            device_id_type=MESH,
        )

    def arrival(self, half, stage, number):
        order = self.orders[half]
        columns = slice(half * self.half, (half + 1) * self.half)
        index = across(self.index(order, stage, number), order[stage])
        place = self.target.at[rows_at(index, self.rows), columns]
        return pltpu.make_async_remote_copy(
            src_ref=place,
            dst_ref=place,
            send_sem=self.send_sem.at[half, (1 << stage) + number],
            recv_sem=self.recv_sem.at[half, (1 << stage) + number],
            device_id={"dp": across(self.me, order[stage])},
            device_id_type=MESH,
        )

    def own(self):
        return pltpu.make_async_copy(
            self.source, self.target.at[rows_at(self.me, self.rows)], self.keep_sem
        )

    def start(self, stage):
        for half in range(2):
            for number in range(1 << stage):
                self.copy(half, stage, number).start()

    def begin(self):
        self.own().start()
        self.start(0)

    def advance(self, stage):
        for half in range(2):
            for number in range(1 << stage):
                self.arrival(half, stage, number).wait_recv()
        if stage + 1 < self.bits:
            self.start(stage + 1)

    def drain(self, own=True):
        if own:
            self.own().wait()
        for half in range(2):
            for stage in range(self.bits):
                for number in range(1 << stage):
                    self.copy(half, stage, number).wait_send()


class Halving:
    def __init__(self, size, rows, grad, keep, buffer, keep_sem, send_sem, recv_sem):
        self.rows, self.grad, self.keep, self.buffer = rows, grad, keep, buffer
        self.keep_sem, self.send_sem, self.recv_sem = keep_sem, send_sem, recv_sem
        self.me = lax.axis_index("dp")
        self.bits = size.bit_length() - 1
        rest = list(range(1, self.bits))
        self.orders = ([0] + rest, [0] + rest[::-1])
        self.half = buffer.shape[-1]
        self.size = size

    def count(self, stage):
        return self.size >> (stage + 1)

    def offset(self, stage):
        return self.size - (self.size >> stage)

    def block_rows(self, half, number, mine):
        order = self.orders[half]
        first = bit_of(self.me, 0)
        index = first if mine else 1 - first
        later = order[1:]
        for place, bit in enumerate(later):
            index = index + ((number >> (len(later) - 1 - place)) & 1) * (1 << bit)
        return rows_at(index, self.rows)

    def columns(self, half):
        return slice(half * self.half, (half + 1) * self.half)

    def load(self, half, number):
        return pltpu.make_async_copy(
            self.grad.at[self.block_rows(half, number, True), self.columns(half)],
            self.keep.at[half, number],
            self.keep_sem.at[half, number],
        )

    def first_copy(self, half, number):
        return pltpu.make_async_remote_copy(
            src_ref=self.grad.at[self.block_rows(half, number, False), self.columns(half)],
            dst_ref=self.buffer.at[half, number],
            send_sem=self.send_sem.at[half, number],
            recv_sem=self.recv_sem.at[half, number],
            device_id={"dp": across(self.me, 0)},
            device_id_type=MESH,
        )

    def copy(self, half, stage):
        bit = self.orders[half][stage]
        count = self.count(stage)
        goes = (1 - bit_of(self.me, bit)) * count + self.offset(stage - 1)
        return pltpu.make_async_remote_copy(
            src_ref=self.buffer.at[half, pl.ds(goes, count)],
            dst_ref=self.buffer.at[half, pl.ds(self.offset(stage), count)],
            send_sem=self.send_sem.at[half, self.offset(stage)],
            recv_sem=self.recv_sem.at[half, self.offset(stage)],
            device_id={"dp": across(self.me, bit)},
            device_id_type=MESH,
        )

    def begin(self):
        for half in range(2):
            for number in range(self.count(0)):
                self.first_copy(half, number).start()
                self.load(half, number).start()

    def advance(self, stage):
        for half in range(2):
            if stage == 0:
                for number in range(self.count(0)):
                    self.first_copy(half, number).wait_recv()
                    self.load(half, number).wait()
            else:
                self.copy(half, stage).wait_recv()
            if stage == self.bits - 1:
                continue
            base = bit_of(self.me, self.orders[half][stage]) * self.count(stage)

            def add(number, carry, half=half, base=base):
                place = self.offset(stage) + number
                if stage == 0:
                    kept = self.keep[half, number]
                else:
                    kept = self.buffer[half, self.offset(stage - 1) + base + number]
                self.buffer[half, place] = (
                    self.buffer[half, place].astype(F32) + kept.astype(F32)
                ).astype(BF)
                return carry

            lax.fori_loop(0, self.count(stage), add, 0)
            self.copy(half, stage + 1).start()

    def result(self, half):
        stage = self.bits - 1
        base = bit_of(self.me, self.orders[half][stage])
        return self.buffer[half, self.offset(stage)].astype(F32) + self.buffer[
            half, self.offset(stage - 1) + base
        ].astype(F32)

    def drain(self):
        for half in range(2):
            for number in range(self.count(0)):
                self.first_copy(half, number).wait_send()
            for stage in range(1, self.bits):
                self.copy(half, stage).wait_send()


def forward_kernel(
    n,
    dp,
    kv_local,
    x_ref,
    gains_ref,
    wq_ref,
    wgu_ref,
    wo_ref,
    wd_ref,
    cot_ref,
    seg_ref,
    pos_ref,
    freq_ref,
    wqkv_hbm,
    wout_hbm,
    wgu_hbm,
    wd_hbm,
    g1_hbm,
    q_hbm,
    k_hbm,
    v_hbm,
    o_hbm,
    cos_hbm,
    low_hbm,
    high_hbm,
    prob_hbm,
    gf_all,
    m_hbm,
    n2_hbm,
    stat_ref,
    m_ref,
    n2_ref,
    g1,
    wqkv,
    wout,
    own_qkv,
    own_out,
    own_gu,
    q_ref,
    k_ref,
    v_ref,
    o_ref,
    cos_ref,
    low_ref,
    high_ref,
    v_t,
    key_seg,
    key_pos,
    bias,
    prob,
    part,
    sums,
    load_sem,
    out_sem,
    piece_sem,
    prob_sem,
    own_sem,
    n1_send,
    n1_recv,
    ag_send,
    ag_recv,
    rs_send,
    rs_recv,
    keep_sem,
    dp_send,
    dp_recv,
):
    z = lax.axis_index("tensor")
    me = lax.axis_index("dp")
    tokens, width = x_ref.shape
    heads = REPEAT * kv_local
    ff = wd_ref.shape[2]
    half_head = HEAD_WIDTH // 2
    dp_bits = dp.bit_length() - 1
    gain_one, gain_two = gains_ref[0, 0:1, :], gains_ref[0, 1:2, :]
    others = [{"dp": across(me, bit)} for bit in range(dp_bits)]
    greet(n, others)
    first_row = pl.multiple_of(z * tokens, tokens)

    def normalize(rows):
        place = pl.ds(pl.multiple_of(first_row + rows.start, rows.size), rows.size)
        g1[place, :] = norm_rows(x_ref[rows, :], gain_one)[0].astype(BF)

    by_rows(tokens, normalize)
    greeted(n, others)
    spread = Gather(n, lambda slot: g1.at[rows_at(slot, tokens)], n1_send, n1_recv)
    spread.begin()
    shards = [
        Doubling(dp, source, target, keep_sem.at[k], dp_send.at[k], dp_recv.at[k])
        for k, (source, target) in enumerate(
            [
                (own_qkv, wqkv_hbm),
                (own_out, wout_hbm),
                (own_gu, wgu_hbm),
                (wd_ref.at[0], wd_hbm),
            ]
        )
    ]
    early, late = shards[:2], shards[2:]
    for padded, shard in ((own_qkv, wq_ref), (own_out, wo_ref)):
        padded[...] = jnp.zeros_like(padded)
        for head in range(padded.shape[1] // LANES):
            padded[:, head * LANES : head * LANES + HEAD_WIDTH] = shard[
                0, :, head * HEAD_WIDTH : (head + 1) * HEAD_WIDTH
            ]
    for shard in early:
        shard.begin()
    own_gu[:, :ff] = wgu_ref[0, :, 0, :]
    own_gu[:, ff:] = wgu_ref[0, :, 1, :]

    def tables(slot, carry):
        rows = rows_at(slot, tokens)

        def column(row):
            return jnp.broadcast_to(row.astype(F32), (LANES, tokens)).T

        places = column(pos_ref[slot])
        key_pos[rows, :] = places
        key_seg[rows, :] = column(seg_ref[slot])
        angles = places * freq_ref[...]
        sine = jnp.sin(angles)
        lane = lax.broadcasted_iota(jnp.int32, sine.shape, 1)
        cos_ref[rows, :] = jnp.cos(angles)
        low_ref[rows, :] = jnp.where(lane < half_head, -sine, 0.0)
        high_ref[rows, :] = jnp.where((lane >= half_head) & (lane < HEAD_WIDTH), sine, 0.0)
        return carry

    lax.fori_loop(0, n, tables, 0)
    for shard in early:
        shard.advance(0)
    for side in range(2):
        spread.arrive(1, side, n > 2)
    for stage in range(1, dp_bits):
        for shard in early:
            shard.advance(stage)
        if stage == max(dp_bits - 2, 1):
            for shard in late:
                shard.begin()
    for shard in early:
        shard.own().wait()
    loads = [
        pltpu.make_async_copy(wqkv_hbm, wqkv, load_sem.at[0]),
        pltpu.make_async_copy(wout_hbm, wout, load_sem.at[1]),
    ]
    for load in loads:
        load.start()
    gather = Gather(n, lambda slot: gf_all.at[rows_at(slot, tokens)], ag_send, ag_recv)
    keep = pltpu.make_async_copy(cot_ref, gf_all.at[rows_at(z, tokens)], own_sem)
    keep.start()
    loads[0].wait()
    group_width = (REPEAT + 2) * LANES

    def project(slot):
        rows = rows_at(slot, tokens)
        cosine, low, high = cos_ref[rows, :], low_ref[rows, :], high_ref[rows, :]

        def turn(values):
            return (
                values * cosine
                + pltpu.roll(values, LANES - half_head, 1) * low
                + pltpu.roll(values, half_head, 1) * high
            ).astype(BF)

        for group in range(kv_local):
            joined = nn(g1[rows, :], wqkv[:, group * group_width : (group + 1) * group_width])
            for member in range(REPEAT):
                q_ref[group * REPEAT + member, rows, :] = turn(
                    joined[:, member * LANES : (member + 1) * LANES]
                )
            k_ref[group, rows, :] = turn(joined[:, REPEAT * LANES : (REPEAT + 1) * LANES])
            values = joined[:, (REPEAT + 1) * LANES :]
            v_ref[group, rows, :] = values.astype(BF)

    def project_of(index, carry):
        came, near = (index + 1) // 2, (index + 1) % 2
        slot = z - (1 - 2 * near) * came

        @pl.when(came > 1)
        def _():
            spread.arrive(came, near, came < n - 1)

        @pl.when(index == 2 * (n - 2))
        def _():
            gather.begin(cot_ref)

        for stage in range(min(2, dp_bits)):

            @pl.when(index == 3 + 2 * stage)
            def _(stage=stage):
                for shard in late:
                    shard.advance(stage)

        @pl.when((slot >= 0) & (slot < n))
        def _():
            project(slot)

        return carry

    lax.fori_loop(0, 2 * n - 1, project_of, 0)
    outs = [
        pltpu.make_async_copy(source, target, out_sem.at[k])
        for k, (source, target) in enumerate(
            [
                (q_ref, q_hbm),
                (k_ref, k_hbm),
                (v_ref, v_hbm),
                (cos_ref, cos_hbm),
                (low_ref, low_hbm),
                (high_ref, high_hbm),
                (g1, g1_hbm),
                (o_ref, o_hbm),
            ]
        )
    ]
    for out in outs[:-1]:
        out.start()
    for group in range(kv_local):
        v_t[group] = v_ref[group].astype(F32).T.astype(BF)
    loads[1].wait()
    scatter = Scatter(n, sums, rs_send, rs_recv)
    log2_scale = HEAD_WIDTH ** (-0.5) * 1.4426950408889634

    def attend(target):
        rows = rows_at(target, tokens)
        for first in range(0, tokens, LANES):
            lanes = slice(first, first + LANES)
            seen = (key_seg[...] == 0.0) | (
                key_seg[...] == seg_ref[target, :, lanes].astype(F32)
            )
            seen = seen & (key_pos[...] <= pos_ref[target, :, lanes].astype(F32))
            bias[:, lanes] = jnp.where(seen, 0.0, -1e30)

        def one_head(head, carry):
            group = head // REPEAT
            scores = nt(k_ref[group], q_ref[head, rows, :]) * log2_scale + bias[...]
            top = jnp.max(scores, axis=0, keepdims=True)
            weights = jnp.exp2(scores - top)
            total = jnp.sum(weights, axis=0, keepdims=True)
            prob[head] = (weights * (1.0 / total)).astype(BF)
            mixed = nn(v_t[group], prob[head])
            o_ref[rows, rows_at(head, LANES)] = mixed.T.astype(BF)
            return carry

        lax.fori_loop(0, heads, one_head, 0)
        out = pltpu.make_async_copy(prob, prob_hbm.at[target], prob_sem)
        out.start()
        for first in range(0, width, 512):
            part[:, first : first + 512] = nt(o_ref[rows, :], wout[first : first + 512, :])
        out.wait()

    def turn_of(index, carry):
        step, side = index // 2 + 1, index % 2
        target, valid = scatter.turn(step, side)

        @pl.when(valid)
        def _():
            attend(target)

            @pl.when(step < n)
            def _():
                scatter.push(step, side, part)

        for stage in range(2, dp_bits):

            @pl.when(index == 2 * (stage - 2) + 1)
            def _(stage=stage):
                for shard in late:
                    shard.advance(stage)

        @pl.when(step < n)
        def _():
            gather.arrive(step, side, step < n - 1)

        return carry

    lax.fori_loop(0, 2 * (n - 1) + 1, turn_of, 0)
    outs[-1].start()
    stat_ref[...] = jnp.zeros_like(stat_ref)

    def finish(rows):
        branch = part[rows, :]
        middle = x_ref[rows, :] + branch
        m_ref[rows, :] = middle
        n2_ref[rows, :] = norm_rows(middle, gain_two)[0].astype(BF)
        stat_ref[0:1, :] += jnp.sum(middle * middle, axis=0, keepdims=True)
        stat_ref[1:2, :] += jnp.sum(branch * branch, axis=0, keepdims=True)

    def piece_out(piece):
        size = tokens // PIECES
        rows = pl.ds(piece * size, size)
        return [
            pltpu.make_async_copy(source.at[rows], target.at[rows], piece_sem.at[k, piece])
            for k, (source, target) in enumerate([(n2_ref, n2_hbm), (m_ref, m_hbm)])
        ]

    def settled(piece, first, rows):
        by_rows(rows, finish, first)
        for out in piece_out(piece):
            out.start()

    scatter.settle(part, settled)
    for piece in range(PIECES):
        for out in piece_out(piece):
            out.wait()
    keep.wait()
    for out in outs:
        out.wait()
    spread.drain()
    gather.drain(cot_ref)
    scatter.drain()
    for shard in early:
        shard.drain(own=False)
    for shard in late:
        shard.drain()


def forward(n, dp, kv_local, x, gains, w_qkv, w_gate_up, w_out, w_down, cot, seg, pos, freq):
    tokens, width = x.shape
    group_len = n * tokens
    heads = REPEAT * kv_local
    owned = w_qkv.shape[1]
    ff = w_down.shape[2]
    lanes, out_lanes = (REPEAT + 2) * kv_local * LANES, heads * LANES
    vmem = pl.BlockSpec(memory_space=pltpu.VMEM)
    hbm = pl.BlockSpec(memory_space=pl.ANY)
    kept = [
        ((heads, group_len, LANES), BF),
        ((kv_local, group_len, LANES), BF),
        ((kv_local, group_len, LANES), BF),
        ((group_len, out_lanes), BF),
        ((group_len, LANES), F32),
        ((group_len, LANES), F32),
        ((group_len, LANES), F32),
    ]
    flops = 2 * group_len * (
        width * lanes + width * out_lanes + 2 * heads * group_len * LANES
    )
    return pl.pallas_call(
        functools.partial(forward_kernel, n, dp, kv_local),
        out_shape=(
            jax.ShapeDtypeStruct((width, lanes), BF),
            jax.ShapeDtypeStruct((width, out_lanes), BF),
            jax.ShapeDtypeStruct((width, 2 * ff), BF),
            jax.ShapeDtypeStruct((width, ff), BF),
            jax.ShapeDtypeStruct((group_len, width), BF),
            *[jax.ShapeDtypeStruct(shape, kind) for shape, kind in kept],
            jax.ShapeDtypeStruct((n, heads, group_len, tokens), BF),
            jax.ShapeDtypeStruct((group_len, width), BF),
            jax.ShapeDtypeStruct((tokens, width), F32),
            jax.ShapeDtypeStruct((tokens, width), BF),
            jax.ShapeDtypeStruct((8, width), F32),
        ),
        in_specs=[vmem] * 10,
        out_specs=(hbm,) * 16 + (vmem,),
        scratch_shapes=[
            pltpu.VMEM((tokens, width), F32),
            pltpu.VMEM((tokens, width), BF),
            pltpu.VMEM((group_len, width), BF),
            pltpu.VMEM((width, lanes), BF),
            pltpu.VMEM((width, out_lanes), BF),
            pltpu.VMEM((owned, lanes), BF),
            pltpu.VMEM((owned, out_lanes), BF),
            pltpu.VMEM((owned, 2 * ff), BF),
            *[pltpu.VMEM(shape, kind) for shape, kind in kept],
            pltpu.VMEM((kv_local, LANES, group_len), BF),
            pltpu.VMEM((group_len, LANES), F32),
            pltpu.VMEM((group_len, LANES), F32),
            pltpu.VMEM((group_len, tokens), F32),
            pltpu.VMEM((heads, group_len, tokens), BF),
            pltpu.VMEM((tokens, width), F32),
            pltpu.VMEM((2, n, tokens, width), BF),
            pltpu.SemaphoreType.DMA((2,)),
            pltpu.SemaphoreType.DMA((8,)),
            pltpu.SemaphoreType.DMA((2, PIECES)),
            pltpu.SemaphoreType.DMA,
            pltpu.SemaphoreType.DMA,
            *[pltpu.SemaphoreType.DMA((2, n, PIECES))] * 6,
            pltpu.SemaphoreType.DMA((4,)),
            pltpu.SemaphoreType.DMA((4, 2, dp)),
            pltpu.SemaphoreType.DMA((4, 2, dp)),
        ],
        compiler_params=pltpu.CompilerParams(
            collective_id=1, has_side_effects=True, vmem_limit_bytes=VMEM_LIMIT
        ),
        cost_estimate=pl.CostEstimate(
            flops=flops, bytes_accessed=200 * tokens * width * 2, transcendentals=0
        ),
        name="attend_forward",
    )(x, gains, w_qkv, w_gate_up, w_out, w_down, cot, seg, pos, freq)


def feed_kernel(
    n,
    chunks,
    n2_hbm,
    gf_hbm,
    wgu_hbm,
    wd_hbm,
    m_hbm,
    gain_ref,
    cot_hbm,
    z_hbm,
    dm_ref,
    ga_ref,
    dgain_ref,
    dwgu_hbm,
    m_ref,
    cot_ref,
    dwgu_ref,
    n2_all,
    gf_all,
    z_all,
    dgu,
    wgu,
    wd,
    part,
    dn2,
    sums,
    load_sem,
    n2_sem,
    gf_sem,
    z_sem,
    dw_sem,
    ag_send,
    ag_recv,
    rs_send,
    rs_recv,
):
    z = lax.axis_index("tensor")
    greet(n)
    tokens, width = n2_hbm.shape
    ff = wd_hbm.shape[1]
    piece = tokens // chunks
    rows_chunk = n * piece
    load_gu = pltpu.make_async_copy(wgu_hbm, wgu, load_sem.at[0])
    load_d = pltpu.make_async_copy(wd_hbm, wd, load_sem.at[1])

    def load_gf(chunk, slot):
        return pltpu.make_async_copy(
            gf_hbm.at[pl.ds(pl.multiple_of(slot * tokens + chunk * piece, piece), piece)],
            gf_all.at[pl.ds(pl.multiple_of(chunk * rows_chunk + slot * piece, piece), piece)],
            gf_sem.at[chunk, slot],
        )


    def load_n2(chunk):
        return pltpu.make_async_copy(
            n2_hbm.at[chunk * piece : (chunk + 1) * piece],
            n2_all.at[pl.ds(pl.multiple_of(chunk * rows_chunk + z * piece, piece), piece)],
            n2_sem.at[chunk],
        )

    for chunk in range(chunks):
        load_n2(chunk).start()
    load_gu.start()
    load_d.start()
    for chunk in range(chunks):
        for slot in range(n):
            load_gf(chunk, slot).start()
    load_m = pltpu.make_async_copy(m_hbm, m_ref, load_sem.at[2])
    load_cot = pltpu.make_async_copy(cot_hbm, cot_ref, load_sem.at[3])
    load_m.start()
    load_cot.start()
    greeted(n)
    for chunk in range(chunks):
        load_n2(chunk).wait()

    def gather_of(chunk):
        return Gather(
            n,
            lambda slot: n2_all.at[
                pl.ds(pl.multiple_of(chunk * rows_chunk + slot * piece, piece), piece)
            ],
            ag_send.at[chunk],
            ag_recv.at[chunk],
        )

    def scatter_of(chunk):
        return Scatter(n, sums.at[chunk], rs_send.at[chunk], rs_recv.at[chunk])

    gather_of(0).begin_where(True)
    for chunk in range(chunks):
        gather_of(chunk).begin_where(False)

    def scatter_end(chunk):
        own = dn2.at[rows_at(chunk, piece)]
        own[...] = part[chunk, rows_at(z, piece), :]
        scatter_of(chunk).settle(own)

    block = 256
    hidden_blocks = ff // block
    out_blocks = width // 512

    def hidden_block(chunk, index):
        rows = rows_at(chunk, rows_chunk)
        cols = rows_at(index, block)
        up_cols = pl.ds(pl.multiple_of(ff + index * block, block), block)
        gate = nn(n2_all[rows, :], wgu[:, cols])
        up = nn(n2_all[rows, :], wgu[:, up_cols])
        dz = nn(gf_all[rows, :], wd[:, cols])
        s = 1.0 / (1.0 + jnp.exp(-gate))
        act = gate * s
        z_all[rows, cols] = (act * up).astype(BF)
        dgu[rows, cols] = (dz * up * (s * (1.0 + gate * (1.0 - s)))).astype(BF)
        dgu[rows, up_cols] = (dz * act).astype(BF)

    def out_block(chunk, index):
        rows = rows_at(chunk, rows_chunk)
        cols = rows_at(index, 512)
        part[chunk, :, cols] = nt(dgu[rows, :], wgu[cols, :])

    def z_out(chunk):
        rows = rows_at(chunk, rows_chunk)
        return pltpu.make_async_copy(z_all.at[rows], z_hbm.at[rows], z_sem.at[chunk])

    def compute(chunk):
        for slot in range(n):
            load_gf(chunk, slot).wait()

        def hidden(index, carry):
            hidden_block(chunk, index)
            return carry

        def out(index, carry):
            out_block(chunk, index)
            return carry

        lax.fori_loop(0, hidden_blocks, hidden, 0)
        lax.fori_loop(0, out_blocks, out, 0)
        z_out(chunk).start()

    def grad_gu(index, carry):
        cols = rows_at(index, 256)
        dwgu_ref[:, cols] = tn(n2_all[...], dgu[:, cols]).astype(BF)
        dw_out(index).start()
        return carry

    def dw_out(index):
        cols = rows_at(index, 256)
        return pltpu.make_async_copy(dwgu_ref.at[:, cols], dwgu_hbm.at[:, cols], dw_sem.at[index])

    blocks = 2 * ff // 256

    def within(chunk):
        return (chunk >= 0) & (chunk < chunks)

    def stage(index, carry):
        for step in range(n - 1, 0, -1):
            chunk = index - (step - 1)

            @pl.when(within(chunk))
            def _(step=step, chunk=chunk):
                for side in range(2):
                    gather_of(chunk).arrive(step, side, step < n - 1)

        @pl.when(index + 1 < chunks)
        def _():
            gather_of(index + 1).begin_where(True)

        ready = index - (n - 2)

        def push(chunk, step, starts):
            scatter = scatter_of(chunk)
            for side in range(2):
                target, valid = scatter.turn(step, side)
                other = scatter.has_source(side)

                @pl.when(valid & (jnp.logical_not(other) if starts else other))
                def _(side=side, target=target):
                    scatter.push(step, side, part.at[chunk], target * piece)

        for step in range(n - 1, 1, -1):
            chunk = ready - LAG * (step - 1)

            @pl.when(within(chunk))
            def _(step=step, chunk=chunk):
                push(chunk, step, False)

        @pl.when(within(ready - LAG * (n - 1)))
        def _():
            scatter_end(ready - LAG * (n - 1))

        @pl.when(ready == 0)
        def _():
            load_gu.wait()
            load_d.wait()

        @pl.when(within(ready))
        def _():
            compute(ready)
            for step in range(1, n):
                push(ready, step, True)

        late, turns = ready - chunks, LAG * (n - 1)

        @pl.when((late >= 0) & (late < turns))
        def _():
            lax.fori_loop(blocks * late // turns, blocks * (late + 1) // turns, grad_gu, 0)

        return carry

    lax.fori_loop(0, chunks + n - 2 + LAG * (n - 1), stage, 0)
    load_m.wait()
    load_cot.wait()
    gain = gain_ref[0, 1:2, :]
    dgain_ref[...] = jnp.zeros_like(dgain_ref)

    def finish(rows):
        middle = m_ref[rows, :]
        dn = dn2[rows, :]
        inverse = lax.rsqrt(jnp.mean(middle * middle, axis=-1, keepdims=True) + norm_eps)
        scaled = dn * gain
        dgain_ref[0:1, :] += jnp.sum(dn * middle * inverse, axis=0, keepdims=True)
        dm = (
            inverse * scaled
            - middle * inverse**3 * jnp.mean(scaled * middle, axis=-1, keepdims=True)
            + cot_ref[rows, :].astype(F32)
        )
        dm_ref[rows, :] = dm
        ga_ref[rows, :] = dm.astype(BF)

    by_rows(tokens, finish)
    for index in range(blocks):
        dw_out(index).wait()
    for chunk in range(chunks):
        z_out(chunk).wait()
        gather_of(chunk).drain()
        scatter_of(chunk).drain()


def feed(n, chunks, n2, gf_all, wgu, wd, m, gain, cot):
    tokens, width = n2.shape
    group_len = n * tokens
    ff = wd.shape[1]
    vmem = pl.BlockSpec(memory_space=pltpu.VMEM)
    hbm = pl.BlockSpec(memory_space=pl.ANY)
    return pl.pallas_call(
        functools.partial(feed_kernel, n, chunks),
        out_shape=(
            jax.ShapeDtypeStruct((group_len, ff), BF),
            jax.ShapeDtypeStruct((tokens, width), F32),
            jax.ShapeDtypeStruct((tokens, width), BF),
            jax.ShapeDtypeStruct((8, width), F32),
            jax.ShapeDtypeStruct((width, 2 * ff), BF),
        ),
        in_specs=[hbm] * 5 + [vmem, hbm],
        out_specs=(hbm, vmem, vmem, vmem, hbm),
        scratch_shapes=[
            pltpu.VMEM((tokens, width), F32),
            pltpu.VMEM((tokens, width), BF),
            pltpu.VMEM((width, 2 * ff), BF),
            pltpu.VMEM((group_len, width), BF),
            pltpu.VMEM((group_len, width), BF),
            pltpu.VMEM((group_len, ff), BF),
            pltpu.VMEM((group_len, 2 * ff), BF),
            pltpu.VMEM((width, 2 * ff), BF),
            pltpu.VMEM((width, ff), BF),
            pltpu.VMEM((chunks, group_len // chunks, width), F32),
            pltpu.VMEM((tokens, width), F32),
            pltpu.VMEM((chunks, 2, n, tokens // chunks, width), BF),
            pltpu.SemaphoreType.DMA((4,)),
            pltpu.SemaphoreType.DMA((chunks,)),
            pltpu.SemaphoreType.DMA((chunks, n)),
            pltpu.SemaphoreType.DMA((chunks,)),
            pltpu.SemaphoreType.DMA((2 * ff // 256,)),
            pltpu.SemaphoreType.DMA((chunks, 2, n, 1)),
            pltpu.SemaphoreType.DMA((chunks, 2, n, 1)),
            pltpu.SemaphoreType.DMA((chunks, 2, n, 1)),
            pltpu.SemaphoreType.DMA((chunks, 2, n, 1)),
        ],
        compiler_params=pltpu.CompilerParams(
            collective_id=3, has_side_effects=True, vmem_limit_bytes=VMEM_LIMIT
        ),
        cost_estimate=pl.CostEstimate(
            flops=18 * group_len * width * ff, bytes_accessed=250 * tokens * width * 2, transcendentals=0
        ),
        name="feed_both",
    )(n2, gf_all, wgu, wd, m, gain, cot)


def attend_back_kernel(
    n,
    dp,
    kv_local,
    chunks,
    ga_hbm,
    wout_hbm,
    wd_hbm,
    z_hbm,
    prob_hbm,
    gf_hbm,
    dwgu_hbm,
    m_hbm,
    q_hbm,
    k_hbm,
    v_hbm,
    o_hbm,
    cos_hbm,
    low_hbm,
    high_hbm,
    out_hbm,
    stat_ref,
    dqkv_hbm,
    dwd_hbm,
    ga_out,
    grad_gu_hbm,
    out_ref,
    m_ref,
    q_ref,
    k_ref,
    v_ref,
    o_ref,
    cos_ref,
    sin_low_ref,
    sin_high_ref,
    dqkv_ref,
    dwd_ref,
    grad_gu_ref,
    keep,
    held,
    ga_all,
    gf,
    wout,
    wd,
    z_all,
    k_t,
    prob,
    d_out,
    dk,
    dv,
    part,
    sums,
    load_sem,
    gf_sem,
    prob_sem,
    out_sem,
    piece_sem,
    ag_send,
    ag_recv,
    rs_send,
    rs_recv,
    keep_sem,
    dp_send,
    dp_recv,
):
    z = lax.axis_index("tensor")
    me = lax.axis_index("dp")
    dp_bits = dp.bit_length() - 1
    others = [{"dp": across(me, bit)} for bit in range(dp_bits)]
    greet(n, others)
    tokens, width = ga_hbm.shape
    heads = REPEAT * kv_local
    group_len = n * tokens
    piece = tokens // chunks
    scale = HEAD_WIDTH ** (-0.5)
    loads = [
        pltpu.make_async_copy(source, target, load_sem.at[index])
        for index, (source, target) in enumerate(
            [
                (ga_hbm, ga_all.at[rows_at(z, tokens)]),
                (wout_hbm, wout),
                (k_hbm, k_ref),
                (v_hbm, v_ref),
                (q_hbm, q_ref),
                (o_hbm, o_ref),
                (cos_hbm, cos_ref),
                (low_hbm, sin_low_ref),
                (high_hbm, sin_high_ref),
                (z_hbm, z_all),
                (wd_hbm, wd),
                (m_hbm, m_ref),
            ]
        )
    ]
    for load in loads:
        load.start()

    def load_gf(chunk, slot):
        return pltpu.make_async_copy(
            gf_hbm.at[pl.ds(pl.multiple_of(slot * tokens + chunk * piece, piece), piece)],
            gf.at[pl.ds(pl.multiple_of((chunk * n + slot) * piece, piece), piece)],
            gf_sem.at[chunk, slot],
        )

    for chunk in range(chunks):
        for slot in range(n):
            load_gf(chunk, slot).start()

    def load_prob(slot):
        return pltpu.make_async_copy(prob_hbm.at[slot], prob, prob_sem)

    greeted(n, others)
    gather = Gather(n, lambda slot: ga_all.at[rows_at(slot, tokens)], ag_send, ag_recv)
    loads[0].wait()
    gather.begin()
    halving = Halving(
        dp, grad_gu_ref.shape[0], dwgu_hbm, keep, held, keep_sem, dp_send, dp_recv
    )
    halving.begin()
    scatter = Scatter(n, sums, rs_send, rs_recv)
    for load in loads[1:-1]:
        load.wait()
    for group in range(kv_local):
        k_t[group] = k_ref[group].astype(F32).T.astype(BF)
    dk[...] = jnp.zeros_like(dk)
    dv[...] = jnp.zeros_like(dv)
    group_lanes = (REPEAT + 2) * LANES

    def turn_back(values, rows):
        return (
            values * cos_ref[rows, :]
            - pltpu.roll(values, LANES - HEAD_WIDTH // 2, 1) * sin_low_ref[rows, :]
            - pltpu.roll(values, HEAD_WIDTH // 2, 1) * sin_high_ref[rows, :]
        )

    def back(slot):
        rows = rows_at(slot, tokens)
        d_o = nn(ga_all[rows, :], wout[...])
        d_out[...] = d_o.astype(BF)

        def one_head(head, carry):
            group = head // REPEAT
            lanes = rows_at(head, LANES)
            do_h = d_out[:, lanes]
            both = do_h.astype(F32) * o_ref[rows, lanes].astype(F32)
            delta = jnp.sum(both.T, axis=0, keepdims=True)
            dprob = nt(v_ref[group], do_h)
            weights = prob[head]
            ds = (weights.astype(F32) * (dprob - delta)).astype(BF)
            dv[group] += nn(weights, do_h)
            dk[group] += nn(ds, q_ref[head, rows, :])
            dq = nn(k_t[group], ds).T * scale
            first = group * (REPEAT + 2) + head % REPEAT
            dqkv_ref[rows, rows_at(first, LANES)] = turn_back(dq, rows).astype(BF)
            return carry

        lax.fori_loop(0, heads, one_head, 0)

    def feed_rows(target):
        pieces = [
            z_all[
                pl.ds(
                    pl.multiple_of(chunk * n * piece + target * piece, piece), piece
                ),
                :,
            ]
            for chunk in range(chunks)
        ]
        rows = jnp.concatenate(pieces, axis=0) if chunks > 1 else pieces[0]
        for first in range(0, width, 512):
            part[:, first : first + 512] = nt(rows, wd[first : first + 512, :])

    def turn_of(index, carry):
        came, near = (index + 1) // 2, (index + 1) % 2
        slot = z - (1 - 2 * near) * came
        valid = (slot >= 0) & (slot < n)

        @pl.when(valid)
        def _():
            load_prob(slot).start()

        @pl.when(index > 0)
        def _():
            gather.arrive(came, near, came < n - 1)

        step, side = index // 2 + 1, index % 2
        target, sends = scatter.turn(step, side)

        @pl.when(sends & (step < n))
        def _():
            feed_rows(target)
            scatter.push(step, side, part)

        @pl.when(valid)
        def _():
            load_prob(slot).wait()
            back(slot)

        return carry

    for chunk in range(chunks):
        for slot in range(n):
            load_gf(chunk, slot).wait()
    ff = wd_hbm.shape[1]
    down_blocks = ff // 256

    def grad_down(first, last):
        def body(index, carry):
            cols = rows_at(index, 256)
            dwd_ref[:, cols] = tn(gf[...], z_all[:, cols]).astype(BF)
            return carry

        lax.fori_loop(first, last, body, 0)

    turns = 2 * n - 1

    def turn_and_grad(index, carry):
        turn_of(index, 0)
        grad_down(down_blocks * index // turns, down_blocks * (index + 1) // turns)
        for stage in range(dp_bits):

            @pl.when(index == 2 * stage + 1)
            def _(stage=stage):
                halving.advance(stage)

        return carry

    lax.fori_loop(0, turns, turn_and_grad, 0)

    def finish_keys(slot, carry):
        rows = rows_at(slot, tokens)
        for group in range(kv_local):
            first = group * group_lanes + REPEAT * LANES
            dqkv_ref[rows, first : first + LANES] = turn_back(
                dk[group, rows, :] * scale, rows
            ).astype(BF)
            dqkv_ref[rows, first + LANES : first + 2 * LANES] = dv[group, rows, :].astype(BF)
        return carry

    lax.fori_loop(0, n, finish_keys, 0)
    outs = [
        pltpu.make_async_copy(source, target, out_sem.at[index])
        for index, (source, target) in enumerate(
            [(dqkv_ref, dqkv_hbm), (dwd_ref, dwd_hbm), (ga_all, ga_out), (grad_gu_ref, grad_gu_hbm)]
        )
    ]
    for out in outs[:3]:
        out.start()
    for half in range(2):
        grad_gu_ref[:, half, :] = halving.result(half)
    outs[3].start()
    feed_rows(z)
    loads[-1].wait()
    stat_ref[...] = jnp.zeros_like(stat_ref)

    def finish(rows):
        branch = part[rows, :]
        result = m_ref[rows, :] + branch
        out_ref[rows, :] = result
        stat_ref[0:1, :] += jnp.sum(result * result, axis=0, keepdims=True)
        stat_ref[1:2, :] += jnp.sum(branch * branch, axis=0, keepdims=True)

    def piece_out(piece):
        size = tokens // PIECES
        rows = pl.ds(piece * size, size)
        return pltpu.make_async_copy(out_ref.at[rows], out_hbm.at[rows], piece_sem.at[piece])

    def settled(piece, first, rows):
        by_rows(rows, finish, first)
        piece_out(piece).start()

    scatter.settle(part, settled)
    for piece in range(PIECES):
        piece_out(piece).wait()
    for out in outs:
        out.wait()
    gather.drain()
    scatter.drain()
    halving.drain()


def attend_back(n, dp, kv_local, chunks, ga, wout, wd, z_all, prob, gf, dwgu, m, q, k, v, o, tables):
    tokens, width = ga.shape
    group_len = n * tokens
    heads = REPEAT * kv_local
    ff = wd.shape[1]
    owned = width // dp
    lanes = (REPEAT + 2) * kv_local * LANES
    vmem = pl.BlockSpec(memory_space=pltpu.VMEM)
    hbm = pl.BlockSpec(memory_space=pl.ANY)
    return pl.pallas_call(
        functools.partial(attend_back_kernel, n, dp, kv_local, chunks),
        out_shape=(
            jax.ShapeDtypeStruct((tokens, width), F32),
            jax.ShapeDtypeStruct((8, width), F32),
            jax.ShapeDtypeStruct((group_len, lanes), BF),
            jax.ShapeDtypeStruct((width, ff), BF),
            jax.ShapeDtypeStruct((group_len, width), BF),
            jax.ShapeDtypeStruct((owned, 2, ff), F32),
        ),
        in_specs=[hbm] * 15,
        out_specs=(hbm, vmem, hbm, hbm, hbm, hbm),
        scratch_shapes=[
            pltpu.VMEM((tokens, width), F32),
            pltpu.VMEM((tokens, width), F32),
            pltpu.VMEM(q.shape, BF),
            pltpu.VMEM(k.shape, BF),
            pltpu.VMEM(v.shape, BF),
            pltpu.VMEM(o.shape, BF),
            *[pltpu.VMEM((group_len, LANES), F32)] * 3,
            pltpu.VMEM((group_len, lanes), BF),
            pltpu.VMEM((width, ff), BF),
            pltpu.VMEM((owned, 2, ff), F32),
            pltpu.VMEM((2, dp // 2, owned, ff), BF),
            pltpu.VMEM((2, dp - 1, owned, ff), BF),
            pltpu.VMEM((group_len, width), BF),
            pltpu.VMEM((group_len, width), BF),
            pltpu.VMEM(wout.shape, BF),
            pltpu.VMEM(wd.shape, BF),
            pltpu.VMEM((group_len, ff), BF),
            pltpu.VMEM((kv_local, LANES, group_len), BF),
            pltpu.VMEM((heads, group_len, tokens), BF),
            pltpu.VMEM((tokens, heads * LANES), BF),
            pltpu.VMEM((kv_local, group_len, LANES), F32),
            pltpu.VMEM((kv_local, group_len, LANES), F32),
            pltpu.VMEM((tokens, width), F32),
            pltpu.VMEM((2, n, tokens, width), BF),
            pltpu.SemaphoreType.DMA((12,)),
            pltpu.SemaphoreType.DMA((chunks, n)),
            pltpu.SemaphoreType.DMA,
            pltpu.SemaphoreType.DMA((4,)),
            pltpu.SemaphoreType.DMA((PIECES,)),
            pltpu.SemaphoreType.DMA((2, n, PIECES)),
            pltpu.SemaphoreType.DMA((2, n, PIECES)),
            pltpu.SemaphoreType.DMA((2, n, PIECES)),
            pltpu.SemaphoreType.DMA((2, n, PIECES)),
            pltpu.SemaphoreType.DMA((2, dp // 2)),
            pltpu.SemaphoreType.DMA((2, dp)),
            pltpu.SemaphoreType.DMA((2, dp)),
        ],
        compiler_params=pltpu.CompilerParams(
            collective_id=4, has_side_effects=True, vmem_limit_bytes=VMEM_LIMIT
        ),
        cost_estimate=pl.CostEstimate(
            flops=8 * group_len * width * ff, bytes_accessed=200 * tokens * width * 2, transcendentals=0
        ),
        name="attend_backward",
    )(ga, wout, wd, z_all, prob, gf, dwgu, m, q, k, v, o, *tables)


def last_kernel(
    n,
    dp,
    cells,
    out_heads,
    dqkv_hbm,
    wqkv_hbm,
    x_hbm,
    dm_hbm,
    gain_ref,
    dgain_two_ref,
    stat_one_ref,
    stat_two_ref,
    g1_hbm,
    ga_hbm,
    o_hbm,
    dwd_hbm,
    dx_hbm,
    gains_ref,
    rms_ref,
    grad_out_ref,
    grad_qkv_ref,
    grad_down_ref,
    dx_ref,
    dqkv,
    wqkv,
    x,
    dm,
    g1,
    ga,
    o,
    dw,
    part,
    sums,
    down_keep,
    down_held,
    head_keep,
    head_held,
    vector,
    vectors,
    load_sem,
    piece_sem,
    rs_send,
    rs_recv,
    down_keep_sem,
    down_send,
    down_recv,
    head_keep_sem,
    head_send,
    head_recv,
    all_send,
    all_recv,
):
    z = lax.axis_index("tensor")
    me = lax.axis_index("dp")
    tokens, width = x.shape
    dp_bits, z_bits = dp.bit_length() - 1, n.bit_length() - 1
    partners = [{"dp": across(me, bit)} for bit in range(dp_bits)]
    partners += [{"tensor": across(z, bit)} for bit in range(z_bits)]
    others = partners[:dp_bits] + partners[dp_bits + 1 :]
    greet(n, others)
    owned = grad_out_ref.shape[0]
    loads = [
        pltpu.make_async_copy(source, target, load_sem.at[index])
        for index, (source, target) in enumerate(
            [
                (wqkv_hbm, wqkv),
                (dqkv_hbm, dqkv),
                (g1_hbm, g1),
                (ga_hbm, ga),
                (o_hbm, o),
                (x_hbm, x),
                (dm_hbm, dm),
            ]
        )
    ]
    for load in loads:
        load.start()
    greeted(n, others)
    down = Halving(dp, owned, dwd_hbm, down_keep, down_held, down_keep_sem, down_send, down_recv)
    down.begin()
    halving = Halving(dp, owned, dw, head_keep, head_held, head_keep_sem, head_send, head_recv)
    scatter = Scatter(n, sums, rs_send, rs_recv)
    gain = gain_ref[0, 0:1, :]
    vector[...] = jnp.zeros_like(vector)
    vector[1:2, :] = dgain_two_ref[0:1, :]
    vector[2:3, :] = stat_one_ref[0:1, :]
    vector[3:4, :] = stat_two_ref[0:1, :]
    vector[4:5, :] = stat_one_ref[1:2, :]
    vector[5:6, :] = stat_two_ref[1:2, :]
    for load in loads[:3]:
        load.wait()

    def compute(index, carry):
        step, side = index // 2 + 1, index % 2
        target, due = scatter.turn(step, side)

        @pl.when(due)
        def _():
            rows = rows_at(target, tokens)

            def block(number, carry):
                cols = rows_at(number, 256)
                values = nt(dqkv[rows, :], wqkv[cols, :])
                part[rows, cols] = values
                vector[0:1, cols] += jnp.sum(
                    values * g1[rows, cols].astype(F32), axis=0, keepdims=True
                )
                return carry

            lax.fori_loop(0, width // 256, block, 0)

            @pl.when((step < n) & jnp.logical_not(scatter.has_source(side)))
            def _():
                scatter.push(step, side, part, target * tokens)

        return carry

    lax.fori_loop(0, 2 * n - 1, compute, 0)
    vector[0:1, :] = vector[0:1, :] / gain

    def exchange(index):
        return pltpu.make_async_remote_copy(
            src_ref=vector if index == 0 else vectors.at[index - 1],
            dst_ref=vectors.at[index],
            send_sem=all_send.at[index],
            recv_sem=all_recv.at[index],
            device_id=partners[index],
            device_id_type=MESH,
        )

    def meet(index):
        exchange(index).wait_recv()
        held = vector[...] if index == 0 else vectors[index - 1]
        vectors[index] += held
        if index + 1 < len(partners):
            exchange(index + 1).start()

    exchange(0).start()
    down.advance(0)
    out_lanes = o.shape[1]

    def grad_qkv(index, carry):
        place = pl.ds(pl.multiple_of(out_lanes + index * 256, 256), 256)
        dw[:, place] = tn(g1[...], dqkv[:, rows_at(index, 256)]).astype(BF)
        return carry

    def grad_out(index, carry):
        cols = rows_at(index, 256)
        dw[:, cols] = tn(ga[...], o[:, cols]).astype(BF)
        return carry

    def grads():
        for load in loads[3:]:
            load.wait()
        lax.fori_loop(0, dqkv.shape[1] // 256, grad_qkv, 0)
        lax.fori_loop(0, out_lanes // 256, grad_out, 0)
        halving.begin()

    def push_came(step):
        for side in range(2):
            target, sends = scatter.turn(step, side)

            @pl.when(sends & scatter.has_source(side))
            def _(side=side, target=target):
                scatter.push(step, side, part, target * tokens)

    work = [grads]
    for index in range(max(len(partners), dp_bits + 1)):
        if index < len(partners):
            work.append(functools.partial(meet, index))
        if index + 1 < dp_bits:
            work.append(functools.partial(down.advance, index + 1))
        if 1 <= index <= dp_bits:
            work.append(functools.partial(halving.advance, index - 1))
    done = 0
    for step in range(2, n):
        push_came(step)
        until = len(work) * (step - 1) // (n - 2)
        for item in work[done:until]:
            item()
        done = until
    for item in work[done:]:
        item()
    for half in range(2):
        columns = down.columns(half)
        grad_down_ref[:, columns] = down.result(half)
    place = 0
    for half in range(2):
        block = halving.result(half)
        for index in range(block.shape[1] // LANES):
            values = block[:, index * LANES : index * LANES + HEAD_WIDTH]
            if place < out_heads:
                grad_out_ref[:, place * HEAD_WIDTH : (place + 1) * HEAD_WIDTH] = values
            else:
                head = place - out_heads
                grad_qkv_ref[:, head * HEAD_WIDTH : (head + 1) * HEAD_WIDTH] = values
            place += 1
    total = vectors[len(partners) - 1]
    gains_ref[0] = total[0:2, :]
    squares = jnp.sqrt(jnp.sum(total, axis=1, keepdims=True) * (1.0 / cells))
    row = lax.broadcasted_iota(jnp.int32, (8, 4), 0)
    column = lax.broadcasted_iota(jnp.int32, (8, 4), 1)
    rms_ref[...] = jnp.sum(jnp.where(row == column + 2, squares, 0.0), axis=0, keepdims=True)
    own = part.at[rows_at(z, tokens)]

    def finish(rows):
        values = x[rows, :]
        dn = own[rows, :]
        inverse = lax.rsqrt(jnp.mean(values * values, axis=-1, keepdims=True) + norm_eps)
        scaled = dn * gain
        dx_ref[rows, :] = (
            inverse * scaled
            - values * inverse**3 * jnp.mean(scaled * values, axis=-1, keepdims=True)
            + dm[rows, :]
        )

    def piece_out(piece):
        size = tokens // PIECES
        rows = pl.ds(piece * size, size)
        return pltpu.make_async_copy(dx_ref.at[rows], dx_hbm.at[rows], piece_sem.at[piece])

    def settled(piece, first, rows):
        by_rows(rows, finish, first)
        piece_out(piece).start()

    scatter.settle(own, settled)
    for piece in range(PIECES):
        piece_out(piece).wait()
    for index in range(len(partners)):
        exchange(index).wait_send()
    down.drain()
    halving.drain()
    scatter.drain()


def last(n, dqkv, wqkv, x, dm, gain, dgain_two, stat_one, stat_two, g1, ga, o, dwd, out_columns, qkv_columns):
    tokens, width = x.shape
    dp = lax.axis_size("dp")
    owned = width // dp
    stages = (dp.bit_length() - 1) + (n.bit_length() - 1)
    ff = dwd.shape[1]
    columns = o.shape[1] + dqkv.shape[1]
    vmem = pl.BlockSpec(memory_space=pltpu.VMEM)
    hbm = pl.BlockSpec(memory_space=pl.ANY)
    return pl.pallas_call(
        functools.partial(last_kernel, n, dp, tokens * width * dp * n, out_columns // HEAD_WIDTH),
        out_shape=(
            jax.ShapeDtypeStruct((tokens, width), F32),
            jax.ShapeDtypeStruct((1, 2, width), F32),
            jax.ShapeDtypeStruct((1, 4), F32),
            jax.ShapeDtypeStruct((owned, out_columns), F32),
            jax.ShapeDtypeStruct((owned, qkv_columns), F32),
            jax.ShapeDtypeStruct((owned, ff), F32),
        ),
        in_specs=[hbm] * 4 + [vmem] * 4 + [hbm] * 4,
        out_specs=(hbm,) + (vmem,) * 5,
        scratch_shapes=[
            pltpu.VMEM(x.shape, F32),
            pltpu.VMEM(dqkv.shape, BF),
            pltpu.VMEM(wqkv.shape, BF),
            pltpu.VMEM(x.shape, F32),
            pltpu.VMEM(dm.shape, F32),
            pltpu.VMEM(g1.shape, BF),
            pltpu.VMEM(ga.shape, BF),
            pltpu.VMEM(o.shape, BF),
            pltpu.VMEM((width, columns), BF),
            pltpu.VMEM((n * tokens, width), F32),
            pltpu.VMEM((2, n, tokens, width), BF),
            pltpu.VMEM((2, dp // 2, owned, ff // 2), BF),
            pltpu.VMEM((2, dp - 1, owned, ff // 2), BF),
            pltpu.VMEM((2, dp // 2, owned, columns // 2), BF),
            pltpu.VMEM((2, dp - 1, owned, columns // 2), BF),
            pltpu.VMEM((8, width), F32),
            pltpu.VMEM((stages, 8, width), F32),
            pltpu.SemaphoreType.DMA((7,)),
            pltpu.SemaphoreType.DMA((PIECES,)),
            pltpu.SemaphoreType.DMA((2, n, PIECES)),
            pltpu.SemaphoreType.DMA((2, n, PIECES)),
            *[
                pltpu.SemaphoreType.DMA((2, dp // 2)),
                pltpu.SemaphoreType.DMA((2, dp)),
                pltpu.SemaphoreType.DMA((2, dp)),
            ]
            * 2,
            pltpu.SemaphoreType.DMA((stages,)),
            pltpu.SemaphoreType.DMA((stages,)),
        ],
        compiler_params=pltpu.CompilerParams(
            collective_id=5, has_side_effects=True, vmem_limit_bytes=VMEM_LIMIT
        ),
        cost_estimate=pl.CostEstimate(
            flops=2 * dqkv.size * width, bytes_accessed=150 * tokens * width * 2, transcendentals=0
        ),
        name="input_gradient",
    )(dqkv, wqkv, x, dm, gain, dgain_two, stat_one, stat_two, g1, ga, o, dwd)


def deliver_kernel(*refs):
    count = len(refs) // 3
    sources, targets, held = refs[:count], refs[count : 2 * count], refs[2 * count : 3 * count]
    sem = refs[-1]
    ins = [
        pltpu.make_async_copy(source, place, sem.at[0, index])
        for index, (source, place) in enumerate(zip(sources, held, strict=True))
    ]
    outs = [
        pltpu.make_async_copy(place, target, sem.at[1, index])
        for index, (place, target) in enumerate(zip(held, targets, strict=True))
    ]
    for copy in ins:
        copy.start()
    for copy, out in zip(ins, outs, strict=True):
        copy.wait()
        out.start()
    for out in outs:
        out.wait()


def deliver(*arrays):
    hbm = pl.BlockSpec(memory_space=pl.ANY)
    return pl.pallas_call(
        deliver_kernel,
        out_shape=[jax.ShapeDtypeStruct(array.shape, array.dtype) for array in arrays],
        in_specs=[hbm] * len(arrays),
        out_specs=[hbm] * len(arrays),
        scratch_shapes=[
            *[pltpu.VMEM(array.shape, array.dtype) for array in arrays],
            pltpu.SemaphoreType.DMA((2, len(arrays))),
        ],
        compiler_params=pltpu.CompilerParams(vmem_limit_bytes=VMEM_LIMIT),
        name="deliver",
    )(*arrays)


def per_device(inputs, norm_gains, w_qkv, w_gate_up, w_out, w_down, segments, positions, cotangent):
    n, dp = lax.axis_size("tensor"), lax.axis_size("dp")
    tokens, width = inputs.shape
    kv_local = w_out.shape[2] // (REPEAT * HEAD_WIDTH)
    chunks = 8
    half = HEAD_WIDTH // 2
    freq_steps = jnp.arange(half, dtype=F32) * (2.0 / HEAD_WIDTH)
    inverse = jnp.power(rope_base, -freq_steps)
    freq = jnp.concatenate([inverse, inverse, jnp.zeros((LANES - HEAD_WIDTH,), F32)])[None]

    (
        wqkv,
        wout,
        wgu,
        wd,
        g1,
        q,
        k,
        v,
        o,
        cosine,
        low,
        high,
        prob,
        gf_all,
        m,
        n2,
        stat_one,
    ) = forward(
        n,
        dp,
        kv_local,
        inputs,
        norm_gains,
        w_qkv,
        w_gate_up,
        w_out,
        w_down,
        cotangent,
        segments.reshape(n, 1, tokens),
        positions.reshape(n, 1, tokens),
        freq,
    )
    z_all, dm, ga, dgain_two, dwgu = feed(n, chunks, n2, gf_all, wgu, wd, m, norm_gains, cotangent)
    output, stat_two, dqkv, dwd, ga_all, grad_gu = attend_back(
        n,
        dp,
        kv_local,
        chunks,
        ga,
        wout,
        wd,
        z_all,
        prob,
        gf_all,
        dwgu,
        m,
        q,
        k,
        v,
        o,
        (cosine, low, high),
    )
    input_grad, gain_total, rms, grad_out, grad_qkv, grad_down = last(
        n,
        dqkv,
        wqkv,
        inputs,
        dm,
        norm_gains,
        dgain_two,
        stat_one,
        stat_two,
        g1,
        ga_all,
        o,
        dwd,
        w_out.shape[2],
        w_qkv.shape[2],
    )
    output, input_grad, grad_qkv, grad_gu, grad_out, grad_down, gain_total, rms = deliver(
        output, input_grad, grad_qkv, grad_gu, grad_out, grad_down, gain_total, rms
    )
    return (
        output,
        input_grad,
        grad_qkv[None],
        grad_gu[None],
        grad_out[None],
        grad_down[None],
        gain_total,
        rms,
    )


def solution(mesh):
    rows = P(("dp", "tensor"), None)
    weights = P(None, "dp", "tensor")
    pairs = P(None, "dp", None, "tensor")
    return jax.shard_map(
        per_device,
        mesh=mesh,
        in_specs=(rows, P(), weights, pairs, weights, weights, P("dp"), P("dp"), rows),
        out_specs=(rows, rows, weights, pairs, weights, weights, P(), P()),
        check_vma=False,
    )
```

```python
import functools

import jax
import jax.numpy as jnp
from jax import lax
from jax.experimental import pallas as pl
from jax.experimental.pallas import tpu as pltpu
from jax.sharding import PartitionSpec as P

HEADS = 16
KV_HEADS = 8
HEAD_WIDTH = 96
REPEAT = HEADS // KV_HEADS
LANES = 128

norm_eps = 1e-05
rope_base = 100000.0
MESH = pl.DeviceIdType.MESH
BF = jnp.bfloat16
F32 = jnp.float32
VMEM_LIMIT = 60 * 2**20
PIECES = 2
LAG = 2


def nn(a, b):
    return lax.dot_general(a, b, (((1,), (0,)), ((), ())), preferred_element_type=F32)


def nt(a, b):
    return lax.dot_general(a, b, (((1,), (1,)), ((), ())), preferred_element_type=F32)


def tn(a, b):
    return lax.dot_general(a, b, (((0,), (0,)), ((), ())), preferred_element_type=F32)


def rows_at(index, size):
    return pl.ds(pl.multiple_of(index * size, size), size)


def greet(n, others=()):
    z = lax.axis_index("tensor")
    barrier = pltpu.get_barrier_semaphore()

    @pl.when(z > 0)
    def _():
        pl.semaphore_signal(barrier, inc=1, device_id={"tensor": z - 1}, device_id_type=MESH)

    @pl.when(z < n - 1)
    def _():
        pl.semaphore_signal(barrier, inc=1, device_id={"tensor": z + 1}, device_id_type=MESH)

    for other in others:
        pl.semaphore_signal(barrier, inc=1, device_id=other, device_id_type=MESH)


def greeted(n, others=()):
    z = lax.axis_index("tensor")
    barrier = pltpu.get_barrier_semaphore()

    @pl.when((z > 0) & (z < n - 1))
    def _():
        pl.semaphore_wait(barrier, 2 + len(others))

    @pl.when((z == 0) | (z == n - 1))
    def _():
        pl.semaphore_wait(barrier, 1 + len(others))


def bit_of(index, bit):
    return (index // (1 << bit)) % 2


def across(index, bit):
    return index + (1 << bit) * (1 - 2 * bit_of(index, bit))


class Gather:
    def __init__(self, n, at, send_sem, recv_sem):
        self.n, self.at, self.send_sem, self.recv_sem = n, at, send_sem, recv_sem
        self.z = lax.axis_index("tensor")
        self.pieces = send_sem.shape[-1]

    def copy(self, slot, step, side, piece, source=None):
        block = self.at(slot)
        size = block.shape[0] // self.pieces
        rows = pl.ds(piece * size, size)
        return pltpu.make_async_remote_copy(
            src_ref=(block if source is None else source).at[rows],
            dst_ref=block.at[rows],
            send_sem=self.send_sem.at[side, step, piece],
            recv_sem=self.recv_sem.at[side, step, piece],
            device_id={"tensor": self.z + 1 - 2 * side},
            device_id_type=MESH,
        )

    def sends(self, step, side):
        z, n = self.z, self.n
        slot = z - (1 - 2 * side) * (step - 1)
        target = z + 1 - 2 * side
        return slot, (slot >= 0) & (slot < n) & (target >= 0) & (target < n)

    def send(self, step, side, piece, source=None, where=True):
        slot, valid = self.sends(step, side)

        @pl.when(valid if where is True else valid & where)
        def _():
            self.copy(slot, step, side, piece, source).start()

    def begin(self, source=None):
        for piece in range(self.pieces):
            for side in range(2):
                self.send(1, side, piece, source)

    def begin_where(self, passes_on):
        for side in range(2):
            source = self.z - (1 - 2 * side)
            other = (source >= 0) & (source < self.n)
            for piece in range(self.pieces):
                self.send(1, side, piece, where=other if passes_on else jnp.logical_not(other))

    def arrive(self, step, side, forward):
        z, n = self.z, self.n
        slot = z - (1 - 2 * side) * step
        for piece in range(self.pieces):

            @pl.when((slot >= 0) & (slot < n))
            def _(piece=piece):
                self.copy(slot, step, side, piece).wait_recv()

            if forward is not False:
                self.send(step + 1, side, piece, where=forward)

    def drain(self, source=None):
        for step in range(1, self.n):
            for side in range(2):
                slot, valid = self.sends(step, side)
                for piece in range(self.pieces):

                    @pl.when(valid)
                    def _(slot=slot, step=step, side=side, piece=piece):
                        self.copy(
                            slot, step, side, piece, source if step == 1 else None
                        ).wait_send()


class Scatter:
    def __init__(self, n, buffer, send_sem, recv_sem):
        self.n, self.buffer, self.send_sem, self.recv_sem = n, buffer, send_sem, recv_sem
        self.z = lax.axis_index("tensor")
        self.pieces = send_sem.shape[-1]
        self.size = buffer.shape[2] // self.pieces

    def rows(self, piece):
        return pl.ds(piece * self.size, self.size)

    def copy(self, step, side, piece):
        return pltpu.make_async_remote_copy(
            src_ref=self.buffer.at[side, step - 1, self.rows(piece)],
            dst_ref=self.buffer.at[side, step, self.rows(piece)],
            send_sem=self.send_sem.at[side, step, piece],
            recv_sem=self.recv_sem.at[side, step, piece],
            device_id={"tensor": self.z + 1 - 2 * side},
            device_id_type=MESH,
        )

    def turn(self, step, side):
        z, n = self.z, self.n
        return z + (1 - 2 * side) * (n - step), step >= 1 + z + side * (n - 1 - 2 * z)

    def has_source(self, side):
        source = self.z - (1 - 2 * side)
        return (source >= 0) & (source < self.n)

    def push(self, step, side, part, first=0):
        has_source = self.has_source(side)
        for piece in range(self.pieces):
            slot = self.buffer.at[side, step - 1, self.rows(piece)]
            rows = pl.ds(pl.multiple_of(first + piece * self.size, self.size), self.size)

            @pl.when(has_source)
            def _(piece=piece, slot=slot, rows=rows):
                self.copy(step - 1, side, piece).wait_recv()
                slot[...] = (part[rows, :] + slot[...].astype(F32)).astype(BF)

            @pl.when(jnp.logical_not(has_source))
            def _(slot=slot, rows=rows):
                slot[...] = part[rows, :].astype(BF)

            self.copy(step, side, piece).start()

    def settle(self, total_ref, then=None):
        for piece in range(self.pieces):
            for side in range(2):

                @pl.when(self.has_source(side))
                def _(side=side, piece=piece):
                    rows = self.rows(piece)
                    self.copy(self.n - 1, side, piece).wait_recv()
                    total_ref[rows, :] += self.buffer[side, self.n - 1, rows, :].astype(F32)

            if then is not None:
                then(piece, piece * self.size, self.size)

    def drain(self):
        for step in range(1, self.n):
            for side in range(2):
                for piece in range(self.pieces):

                    @pl.when(self.turn(step, side)[1])
                    def _(step=step, side=side, piece=piece):
                        self.copy(step, side, piece).wait_send()


def by_rows(rows, body, first=0, block=32):
    def step(index, carry):
        body(pl.ds(pl.multiple_of(first + index * block, block), block))
        return carry

    lax.fori_loop(0, rows // block, step, 0)


def norm_rows(values, gain):
    inverse = lax.rsqrt(jnp.mean(values * values, axis=-1, keepdims=True) + norm_eps)
    return values * inverse * gain, inverse


class Doubling:
    def __init__(self, size, source, target, keep_sem, send_sem, recv_sem):
        self.source, self.target = source, target
        self.keep_sem, self.send_sem, self.recv_sem = keep_sem, send_sem, recv_sem
        self.rows, columns = source.shape
        self.half = columns // 2
        self.me = lax.axis_index("dp")
        self.bits = size.bit_length() - 1
        rest = list(range(1, self.bits))
        self.orders = (rest + [0], rest[::-1] + [0])

    def index(self, order, stage, number):
        index = self.me
        for place in range(stage):
            if (number >> place) & 1:
                index = across(index, order[place])
        return index

    def copy(self, half, stage, number):
        order = self.orders[half]
        columns = slice(half * self.half, (half + 1) * self.half)
        place = self.target.at[rows_at(self.index(order, stage, number), self.rows), columns]
        return pltpu.make_async_remote_copy(
            src_ref=self.source.at[:, columns] if number == 0 else place,
            dst_ref=place,
            send_sem=self.send_sem.at[half, (1 << stage) + number],
            recv_sem=self.recv_sem.at[half, (1 << stage) + number],
            device_id={"dp": across(self.me, order[stage])},
            device_id_type=MESH,
        )

    def arrival(self, half, stage, number):
        order = self.orders[half]
        columns = slice(half * self.half, (half + 1) * self.half)
        index = across(self.index(order, stage, number), order[stage])
        place = self.target.at[rows_at(index, self.rows), columns]
        return pltpu.make_async_remote_copy(
            src_ref=place,
            dst_ref=place,
            send_sem=self.send_sem.at[half, (1 << stage) + number],
            recv_sem=self.recv_sem.at[half, (1 << stage) + number],
            device_id={"dp": across(self.me, order[stage])},
            device_id_type=MESH,
        )

    def own(self):
        return pltpu.make_async_copy(
            self.source, self.target.at[rows_at(self.me, self.rows)], self.keep_sem
        )

    def start(self, stage):
        for half in range(2):
            for number in range(1 << stage):
                self.copy(half, stage, number).start()

    def begin(self):
        self.own().start()
        self.start(0)

    def advance(self, stage):
        for half in range(2):
            for number in range(1 << stage):
                self.arrival(half, stage, number).wait_recv()
        if stage + 1 < self.bits:
            self.start(stage + 1)

    def drain(self, own=True):
        if own:
            self.own().wait()
        for half in range(2):
            for stage in range(self.bits):
                for number in range(1 << stage):
                    self.copy(half, stage, number).wait_send()


class Halving:
    def __init__(self, size, rows, grad, keep, buffer, keep_sem, send_sem, recv_sem):
        self.rows, self.grad, self.keep, self.buffer = rows, grad, keep, buffer
        self.keep_sem, self.send_sem, self.recv_sem = keep_sem, send_sem, recv_sem
        self.me = lax.axis_index("dp")
        self.bits = size.bit_length() - 1
        rest = list(range(1, self.bits))
        self.orders = ([0] + rest, [0] + rest[::-1])
        self.half = buffer.shape[-1]
        self.size = size

    def count(self, stage):
        return self.size >> (stage + 1)

    def offset(self, stage):
        return self.size - (self.size >> stage)

    def block_rows(self, half, number, mine):
        order = self.orders[half]
        first = bit_of(self.me, 0)
        index = first if mine else 1 - first
        later = order[1:]
        for place, bit in enumerate(later):
            index = index + ((number >> (len(later) - 1 - place)) & 1) * (1 << bit)
        return rows_at(index, self.rows)

    def columns(self, half):
        return slice(half * self.half, (half + 1) * self.half)

    def load(self, half, number):
        return pltpu.make_async_copy(
            self.grad.at[self.block_rows(half, number, True), self.columns(half)],
            self.keep.at[half, number],
            self.keep_sem.at[half, number],
        )

    def first_copy(self, half, number):
        return pltpu.make_async_remote_copy(
            src_ref=self.grad.at[self.block_rows(half, number, False), self.columns(half)],
            dst_ref=self.buffer.at[half, number],
            send_sem=self.send_sem.at[half, number],
            recv_sem=self.recv_sem.at[half, number],
            device_id={"dp": across(self.me, 0)},
            device_id_type=MESH,
        )

    def copy(self, half, stage):
        bit = self.orders[half][stage]
        count = self.count(stage)
        goes = (1 - bit_of(self.me, bit)) * count + self.offset(stage - 1)
        return pltpu.make_async_remote_copy(
            src_ref=self.buffer.at[half, pl.ds(goes, count)],
            dst_ref=self.buffer.at[half, pl.ds(self.offset(stage), count)],
            send_sem=self.send_sem.at[half, self.offset(stage)],
            recv_sem=self.recv_sem.at[half, self.offset(stage)],
            device_id={"dp": across(self.me, bit)},
            device_id_type=MESH,
        )

    def begin(self):
        for half in range(2):
            for number in range(self.count(0)):
                self.first_copy(half, number).start()
                self.load(half, number).start()

    def advance(self, stage):
        for half in range(2):
            if stage == 0:
                for number in range(self.count(0)):
                    self.first_copy(half, number).wait_recv()
                    self.load(half, number).wait()
            else:
                self.copy(half, stage).wait_recv()
            if stage == self.bits - 1:
                continue
            base = bit_of(self.me, self.orders[half][stage]) * self.count(stage)

            def add(number, carry, half=half, base=base):
                place = self.offset(stage) + number
                if stage == 0:
                    kept = self.keep[half, number]
                else:
                    kept = self.buffer[half, self.offset(stage - 1) + base + number]
                self.buffer[half, place] = (
                    self.buffer[half, place].astype(F32) + kept.astype(F32)
                ).astype(BF)
                return carry

            lax.fori_loop(0, self.count(stage), add, 0)
            self.copy(half, stage + 1).start()

    def result(self, half):
        stage = self.bits - 1
        base = bit_of(self.me, self.orders[half][stage])
        return self.buffer[half, self.offset(stage)].astype(F32) + self.buffer[
            half, self.offset(stage - 1) + base
        ].astype(F32)

    def drain(self):
        for half in range(2):
            for number in range(self.count(0)):
                self.first_copy(half, number).wait_send()
            for stage in range(1, self.bits):
                self.copy(half, stage).wait_send()


def forward_kernel(
    n,
    dp,
    kv_local,
    x_ref,
    gains_ref,
    wq_ref,
    wgu_ref,
    wo_ref,
    wd_ref,
    cot_ref,
    seg_ref,
    pos_ref,
    freq_ref,
    wqkv_hbm,
    wout_hbm,
    wgu_hbm,
    wd_hbm,
    g1_hbm,
    q_hbm,
    k_hbm,
    v_hbm,
    o_hbm,
    cos_hbm,
    low_hbm,
    high_hbm,
    prob_hbm,
    gf_all,
    m_hbm,
    n2_hbm,
    stat_ref,
    m_ref,
    n2_ref,
    g1,
    wqkv,
    wout,
    own_qkv,
    own_out,
    own_gu,
    q_ref,
    k_ref,
    v_ref,
    o_ref,
    cos_ref,
    low_ref,
    high_ref,
    v_t,
    key_seg,
    key_pos,
    bias,
    prob,
    part,
    sums,
    load_sem,
    out_sem,
    piece_sem,
    prob_sem,
    own_sem,
    n1_send,
    n1_recv,
    ag_send,
    ag_recv,
    rs_send,
    rs_recv,
    keep_sem,
    dp_send,
    dp_recv,
):
    z = lax.axis_index("tensor")
    me = lax.axis_index("dp")
    tokens, width = x_ref.shape
    heads = REPEAT * kv_local
    ff = wd_ref.shape[2]
    half_head = HEAD_WIDTH // 2
    dp_bits = dp.bit_length() - 1
    gain_one, gain_two = gains_ref[0, 0:1, :], gains_ref[0, 1:2, :]
    others = [{"dp": across(me, bit)} for bit in range(dp_bits)]
    greet(n, others)
    first_row = pl.multiple_of(z * tokens, tokens)

    def normalize(rows):
        place = pl.ds(pl.multiple_of(first_row + rows.start, rows.size), rows.size)
        g1[place, :] = norm_rows(x_ref[rows, :], gain_one)[0].astype(BF)

    by_rows(tokens, normalize)
    greeted(n, others)
    spread = Gather(n, lambda slot: g1.at[rows_at(slot, tokens)], n1_send, n1_recv)
    spread.begin()
    shards = [
        Doubling(dp, source, target, keep_sem.at[k], dp_send.at[k], dp_recv.at[k])
        for k, (source, target) in enumerate(
            [
                (own_qkv, wqkv_hbm),
                (own_out, wout_hbm),
                (own_gu, wgu_hbm),
                (wd_ref.at[0], wd_hbm),
            ]
        )
    ]
    early, late = shards[:2], shards[2:]
    for padded, shard in ((own_qkv, wq_ref), (own_out, wo_ref)):
        padded[...] = jnp.zeros_like(padded)
        for head in range(padded.shape[1] // LANES):
            padded[:, head * LANES : head * LANES + HEAD_WIDTH] = shard[
                0, :, head * HEAD_WIDTH : (head + 1) * HEAD_WIDTH
            ]
    for shard in early:
        shard.begin()
    own_gu[:, :ff] = wgu_ref[0, :, 0, :]
    own_gu[:, ff:] = wgu_ref[0, :, 1, :]

    def tables(slot, carry):
        rows = rows_at(slot, tokens)

        def column(row):
            return jnp.broadcast_to(row.astype(F32), (LANES, tokens)).T

        places = column(pos_ref[slot])
        key_pos[rows, :] = places
        key_seg[rows, :] = column(seg_ref[slot])
        angles = places * freq_ref[...]
        sine = jnp.sin(angles)
        lane = lax.broadcasted_iota(jnp.int32, sine.shape, 1)
        cos_ref[rows, :] = jnp.cos(angles)
        low_ref[rows, :] = jnp.where(lane < half_head, -sine, 0.0)
        high_ref[rows, :] = jnp.where((lane >= half_head) & (lane < HEAD_WIDTH), sine, 0.0)
        return carry

    lax.fori_loop(0, n, tables, 0)
    for shard in early:
        shard.advance(0)
    for side in range(2):
        spread.arrive(1, side, n > 2)
    for stage in range(1, dp_bits):
        for shard in early:
            shard.advance(stage)
        if stage == max(dp_bits - 2, 1):
            for shard in late:
                shard.begin()
    for shard in early:
        shard.own().wait()
    loads = [
        pltpu.make_async_copy(wqkv_hbm, wqkv, load_sem.at[0]),
        pltpu.make_async_copy(wout_hbm, wout, load_sem.at[1]),
    ]
    for load in loads:
        load.start()
    gather = Gather(n, lambda slot: gf_all.at[rows_at(slot, tokens)], ag_send, ag_recv)
    keep = pltpu.make_async_copy(cot_ref, gf_all.at[rows_at(z, tokens)], own_sem)
    keep.start()
    loads[0].wait()
    group_width = (REPEAT + 2) * LANES

    def project(slot):
        rows = rows_at(slot, tokens)
        cosine, low, high = cos_ref[rows, :], low_ref[rows, :], high_ref[rows, :]

        def turn(values):
            return (
                values * cosine
                + pltpu.roll(values, LANES - half_head, 1) * low
                + pltpu.roll(values, half_head, 1) * high
            ).astype(BF)

        for group in range(kv_local):
            joined = nn(g1[rows, :], wqkv[:, group * group_width : (group + 1) * group_width])
            for member in range(REPEAT):
                q_ref[group * REPEAT + member, rows, :] = turn(
                    joined[:, member * LANES : (member + 1) * LANES]
                )
            k_ref[group, rows, :] = turn(joined[:, REPEAT * LANES : (REPEAT + 1) * LANES])
            values = joined[:, (REPEAT + 1) * LANES :]
            v_ref[group, rows, :] = values.astype(BF)

    def project_of(index, carry):
        came, near = (index + 1) // 2, (index + 1) % 2
        slot = z - (1 - 2 * near) * came

        @pl.when(came > 1)
        def _():
            spread.arrive(came, near, came < n - 1)

        @pl.when(index == 2 * (n - 2))
        def _():
            gather.begin(cot_ref)

        for stage in range(min(2, dp_bits)):

            @pl.when(index == 3 + 2 * stage)
            def _(stage=stage):
                for shard in late:
                    shard.advance(stage)

        @pl.when((slot >= 0) & (slot < n))
        def _():
            project(slot)

        return carry

    lax.fori_loop(0, 2 * n - 1, project_of, 0)
    outs = [
        pltpu.make_async_copy(source, target, out_sem.at[k])
        for k, (source, target) in enumerate(
            [
                (q_ref, q_hbm),
                (k_ref, k_hbm),
                (v_ref, v_hbm),
                (cos_ref, cos_hbm),
                (low_ref, low_hbm),
                (high_ref, high_hbm),
                (g1, g1_hbm),
                (o_ref, o_hbm),
            ]
        )
    ]
    for out in outs[:-1]:
        out.start()
    for group in range(kv_local):
        v_t[group] = v_ref[group].astype(F32).T.astype(BF)
    loads[1].wait()
    scatter = Scatter(n, sums, rs_send, rs_recv)
    log2_scale = HEAD_WIDTH ** (-0.5) * 1.4426950408889634

    def attend(target):
        rows = rows_at(target, tokens)
        for first in range(0, tokens, LANES):
            lanes = slice(first, first + LANES)
            seen = (key_seg[...] == 0.0) | (
                key_seg[...] == seg_ref[target, :, lanes].astype(F32)
            )
            seen = seen & (key_pos[...] <= pos_ref[target, :, lanes].astype(F32))
            bias[:, lanes] = jnp.where(seen, 0.0, -1e30)

        def one_head(head, carry):
            group = head // REPEAT
            scores = nt(k_ref[group], q_ref[head, rows, :]) * log2_scale + bias[...]
            top = jnp.max(scores, axis=0, keepdims=True)
            weights = jnp.exp2(scores - top)
            total = jnp.sum(weights, axis=0, keepdims=True)
            prob[head] = (weights * (1.0 / total)).astype(BF)
            mixed = nn(v_t[group], prob[head])
            o_ref[rows, rows_at(head, LANES)] = mixed.T.astype(BF)
            return carry

        lax.fori_loop(0, heads, one_head, 0)
        out = pltpu.make_async_copy(prob, prob_hbm.at[target], prob_sem)
        out.start()
        for first in range(0, width, 512):
            part[:, first : first + 512] = nt(o_ref[rows, :], wout[first : first + 512, :])
        out.wait()

    def turn_of(index, carry):
        step, side = index // 2 + 1, index % 2
        target, valid = scatter.turn(step, side)

        @pl.when(valid)
        def _():
            attend(target)

            @pl.when(step < n)
            def _():
                scatter.push(step, side, part)

        for stage in range(2, dp_bits):

            @pl.when(index == 2 * (stage - 2) + 1)
            def _(stage=stage):
                for shard in late:
                    shard.advance(stage)

        @pl.when(step < n)
        def _():
            gather.arrive(step, side, step < n - 1)

        return carry

    lax.fori_loop(0, 2 * (n - 1) + 1, turn_of, 0)
    outs[-1].start()
    stat_ref[...] = jnp.zeros_like(stat_ref)

    def finish(rows):
        branch = part[rows, :]
        middle = x_ref[rows, :] + branch
        m_ref[rows, :] = middle
        n2_ref[rows, :] = norm_rows(middle, gain_two)[0].astype(BF)
        stat_ref[0:1, :] += jnp.sum(middle * middle, axis=0, keepdims=True)
        stat_ref[1:2, :] += jnp.sum(branch * branch, axis=0, keepdims=True)

    def piece_out(piece):
        size = tokens // PIECES
        rows = pl.ds(piece * size, size)
        return [
            pltpu.make_async_copy(source.at[rows], target.at[rows], piece_sem.at[k, piece])
            for k, (source, target) in enumerate([(n2_ref, n2_hbm), (m_ref, m_hbm)])
        ]

    def settled(piece, first, rows):
        by_rows(rows, finish, first)
        for out in piece_out(piece):
            out.start()

    scatter.settle(part, settled)
    for piece in range(PIECES):
        for out in piece_out(piece):
            out.wait()
    keep.wait()
    for out in outs:
        out.wait()
    spread.drain()
    gather.drain(cot_ref)
    scatter.drain()
    for shard in early:
        shard.drain(own=False)
    for shard in late:
        shard.drain()


def forward(n, dp, kv_local, x, gains, w_qkv, w_gate_up, w_out, w_down, cot, seg, pos, freq):
    tokens, width = x.shape
    group_len = n * tokens
    heads = REPEAT * kv_local
    owned = w_qkv.shape[1]
    ff = w_down.shape[2]
    lanes, out_lanes = (REPEAT + 2) * kv_local * LANES, heads * LANES
    vmem = pl.BlockSpec(memory_space=pltpu.VMEM)
    hbm = pl.BlockSpec(memory_space=pl.ANY)
    kept = [
        ((heads, group_len, LANES), BF),
        ((kv_local, group_len, LANES), BF),
        ((kv_local, group_len, LANES), BF),
        ((group_len, out_lanes), BF),
        ((group_len, LANES), F32),
        ((group_len, LANES), F32),
        ((group_len, LANES), F32),
    ]
    flops = 2 * group_len * (
        width * lanes + width * out_lanes + 2 * heads * group_len * LANES
    )
    return pl.pallas_call(
        functools.partial(forward_kernel, n, dp, kv_local),
        out_shape=(
            jax.ShapeDtypeStruct((width, lanes), BF),
            jax.ShapeDtypeStruct((width, out_lanes), BF),
            jax.ShapeDtypeStruct((width, 2 * ff), BF),
            jax.ShapeDtypeStruct((width, ff), BF),
            jax.ShapeDtypeStruct((group_len, width), BF),
            *[jax.ShapeDtypeStruct(shape, kind) for shape, kind in kept],
            jax.ShapeDtypeStruct((n, heads, group_len, tokens), BF),
            jax.ShapeDtypeStruct((group_len, width), BF),
            jax.ShapeDtypeStruct((tokens, width), F32),
            jax.ShapeDtypeStruct((tokens, width), BF),
            jax.ShapeDtypeStruct((8, width), F32),
        ),
        in_specs=[vmem] * 10,
        out_specs=(hbm,) * 16 + (vmem,),
        scratch_shapes=[
            pltpu.VMEM((tokens, width), F32),
            pltpu.VMEM((tokens, width), BF),
            pltpu.VMEM((group_len, width), BF),
            pltpu.VMEM((width, lanes), BF),
            pltpu.VMEM((width, out_lanes), BF),
            pltpu.VMEM((owned, lanes), BF),
            pltpu.VMEM((owned, out_lanes), BF),
            pltpu.VMEM((owned, 2 * ff), BF),
            *[pltpu.VMEM(shape, kind) for shape, kind in kept],
            pltpu.VMEM((kv_local, LANES, group_len), BF),
            pltpu.VMEM((group_len, LANES), F32),
            pltpu.VMEM((group_len, LANES), F32),
            pltpu.VMEM((group_len, tokens), F32),
            pltpu.VMEM((heads, group_len, tokens), BF),
            pltpu.VMEM((tokens, width), F32),
            pltpu.VMEM((2, n, tokens, width), BF),
            pltpu.SemaphoreType.DMA((2,)),
            pltpu.SemaphoreType.DMA((8,)),
            pltpu.SemaphoreType.DMA((2, PIECES)),
            pltpu.SemaphoreType.DMA,
            pltpu.SemaphoreType.DMA,
            *[pltpu.SemaphoreType.DMA((2, n, PIECES))] * 6,
            pltpu.SemaphoreType.DMA((4,)),
            pltpu.SemaphoreType.DMA((4, 2, dp)),
            pltpu.SemaphoreType.DMA((4, 2, dp)),
        ],
        compiler_params=pltpu.CompilerParams(
            collective_id=1, has_side_effects=True, vmem_limit_bytes=VMEM_LIMIT
        ),
        cost_estimate=pl.CostEstimate(
            flops=flops, bytes_accessed=200 * tokens * width * 2, transcendentals=0
        ),
        name="attend_forward",
    )(x, gains, w_qkv, w_gate_up, w_out, w_down, cot, seg, pos, freq)


def feed_kernel(
    n,
    chunks,
    n2_hbm,
    gf_hbm,
    wgu_hbm,
    wd_hbm,
    m_hbm,
    gain_ref,
    cot_hbm,
    z_hbm,
    dm_ref,
    ga_ref,
    dgain_ref,
    dwgu_hbm,
    m_ref,
    cot_ref,
    dwgu_ref,
    n2_all,
    gf_all,
    z_all,
    dgu,
    wgu,
    wd,
    part,
    dn2,
    sums,
    load_sem,
    n2_sem,
    gf_sem,
    z_sem,
    dw_sem,
    ag_send,
    ag_recv,
    rs_send,
    rs_recv,
):
    z = lax.axis_index("tensor")
    greet(n)
    tokens, width = n2_hbm.shape
    ff = wd_hbm.shape[1]
    piece = tokens // chunks
    rows_chunk = n * piece
    load_gu = pltpu.make_async_copy(wgu_hbm, wgu, load_sem.at[0])
    load_d = pltpu.make_async_copy(wd_hbm, wd, load_sem.at[1])

    def load_gf(chunk, slot):
        return pltpu.make_async_copy(
            gf_hbm.at[pl.ds(pl.multiple_of(slot * tokens + chunk * piece, piece), piece)],
            gf_all.at[pl.ds(pl.multiple_of(chunk * rows_chunk + slot * piece, piece), piece)],
            gf_sem.at[chunk, slot],
        )


    def load_n2(chunk):
        return pltpu.make_async_copy(
            n2_hbm.at[chunk * piece : (chunk + 1) * piece],
            n2_all.at[pl.ds(pl.multiple_of(chunk * rows_chunk + z * piece, piece), piece)],
            n2_sem.at[chunk],
        )

    for chunk in range(chunks):
        load_n2(chunk).start()
    load_gu.start()
    load_d.start()
    for chunk in range(chunks):
        for slot in range(n):
            load_gf(chunk, slot).start()
    load_m = pltpu.make_async_copy(m_hbm, m_ref, load_sem.at[2])
    load_cot = pltpu.make_async_copy(cot_hbm, cot_ref, load_sem.at[3])
    load_m.start()
    load_cot.start()
    greeted(n)
    for chunk in range(chunks):
        load_n2(chunk).wait()

    def gather_of(chunk):
        return Gather(
            n,
            lambda slot: n2_all.at[
                pl.ds(pl.multiple_of(chunk * rows_chunk + slot * piece, piece), piece)
            ],
            ag_send.at[chunk],
            ag_recv.at[chunk],
        )

    def scatter_of(chunk):
        return Scatter(n, sums.at[chunk], rs_send.at[chunk], rs_recv.at[chunk])

    gather_of(0).begin_where(True)
    for chunk in range(chunks):
        gather_of(chunk).begin_where(False)

    def scatter_end(chunk):
        own = dn2.at[rows_at(chunk, piece)]
        own[...] = part[chunk, rows_at(z, piece), :]
        scatter_of(chunk).settle(own)

    block = 256
    hidden_blocks = ff // block
    out_blocks = width // 512

    def hidden_block(chunk, index):
        rows = rows_at(chunk, rows_chunk)
        cols = rows_at(index, block)
        up_cols = pl.ds(pl.multiple_of(ff + index * block, block), block)
        gate = nn(n2_all[rows, :], wgu[:, cols])
        up = nn(n2_all[rows, :], wgu[:, up_cols])
        dz = nn(gf_all[rows, :], wd[:, cols])
        s = 1.0 / (1.0 + jnp.exp(-gate))
        act = gate * s
        z_all[rows, cols] = (act * up).astype(BF)
        dgu[rows, cols] = (dz * up * (s * (1.0 + gate * (1.0 - s)))).astype(BF)
        dgu[rows, up_cols] = (dz * act).astype(BF)

    def out_block(chunk, index):
        rows = rows_at(chunk, rows_chunk)
        cols = rows_at(index, 512)
        part[chunk, :, cols] = nt(dgu[rows, :], wgu[cols, :])

    def z_out(chunk):
        rows = rows_at(chunk, rows_chunk)
        return pltpu.make_async_copy(z_all.at[rows], z_hbm.at[rows], z_sem.at[chunk])

    def compute(chunk):
        for slot in range(n):
            load_gf(chunk, slot).wait()

        def hidden(index, carry):
            hidden_block(chunk, index)
            return carry

        def out(index, carry):
            out_block(chunk, index)
            return carry

        lax.fori_loop(0, hidden_blocks, hidden, 0)
        lax.fori_loop(0, out_blocks, out, 0)
        z_out(chunk).start()

    def grad_gu(index, carry):
        cols = rows_at(index, 256)
        dwgu_ref[:, cols] = tn(n2_all[...], dgu[:, cols]).astype(BF)
        dw_out(index).start()
        return carry

    def dw_out(index):
        cols = rows_at(index, 256)
        return pltpu.make_async_copy(dwgu_ref.at[:, cols], dwgu_hbm.at[:, cols], dw_sem.at[index])

    blocks = 2 * ff // 256

    def within(chunk):
        return (chunk >= 0) & (chunk < chunks)

    def stage(index, carry):
        for step in range(n - 1, 0, -1):
            chunk = index - (step - 1)

            @pl.when(within(chunk))
            def _(step=step, chunk=chunk):
                for side in range(2):
                    gather_of(chunk).arrive(step, side, step < n - 1)

        @pl.when(index + 1 < chunks)
        def _():
            gather_of(index + 1).begin_where(True)

        ready = index - (n - 2)

        def push(chunk, step, starts):
            scatter = scatter_of(chunk)
            for side in range(2):
                target, valid = scatter.turn(step, side)
                other = scatter.has_source(side)

                @pl.when(valid & (jnp.logical_not(other) if starts else other))
                def _(side=side, target=target):
                    scatter.push(step, side, part.at[chunk], target * piece)

        for step in range(n - 1, 1, -1):
            chunk = ready - LAG * (step - 1)

            @pl.when(within(chunk))
            def _(step=step, chunk=chunk):
                push(chunk, step, False)

        @pl.when(within(ready - LAG * (n - 1)))
        def _():
            scatter_end(ready - LAG * (n - 1))

        @pl.when(ready == 0)
        def _():
            load_gu.wait()
            load_d.wait()

        @pl.when(within(ready))
        def _():
            compute(ready)
            for step in range(1, n):
                push(ready, step, True)

        late, turns = ready - chunks, LAG * (n - 1)

        @pl.when((late >= 0) & (late < turns))
        def _():
            lax.fori_loop(blocks * late // turns, blocks * (late + 1) // turns, grad_gu, 0)

        return carry

    lax.fori_loop(0, chunks + n - 2 + LAG * (n - 1), stage, 0)
    load_m.wait()
    load_cot.wait()
    gain = gain_ref[0, 1:2, :]
    dgain_ref[...] = jnp.zeros_like(dgain_ref)

    def finish(rows):
        middle = m_ref[rows, :]
        dn = dn2[rows, :]
        inverse = lax.rsqrt(jnp.mean(middle * middle, axis=-1, keepdims=True) + norm_eps)
        scaled = dn * gain
        dgain_ref[0:1, :] += jnp.sum(dn * middle * inverse, axis=0, keepdims=True)
        dm = (
            inverse * scaled
            - middle * inverse**3 * jnp.mean(scaled * middle, axis=-1, keepdims=True)
            + cot_ref[rows, :].astype(F32)
        )
        dm_ref[rows, :] = dm
        ga_ref[rows, :] = dm.astype(BF)

    by_rows(tokens, finish)
    for index in range(blocks):
        dw_out(index).wait()
    for chunk in range(chunks):
        z_out(chunk).wait()
        gather_of(chunk).drain()
        scatter_of(chunk).drain()


def feed(n, chunks, n2, gf_all, wgu, wd, m, gain, cot):
    tokens, width = n2.shape
    group_len = n * tokens
    ff = wd.shape[1]
    vmem = pl.BlockSpec(memory_space=pltpu.VMEM)
    hbm = pl.BlockSpec(memory_space=pl.ANY)
    return pl.pallas_call(
        functools.partial(feed_kernel, n, chunks),
        out_shape=(
            jax.ShapeDtypeStruct((group_len, ff), BF),
            jax.ShapeDtypeStruct((tokens, width), F32),
            jax.ShapeDtypeStruct((tokens, width), BF),
            jax.ShapeDtypeStruct((8, width), F32),
            jax.ShapeDtypeStruct((width, 2 * ff), BF),
        ),
        in_specs=[hbm] * 5 + [vmem, hbm],
        out_specs=(hbm, vmem, vmem, vmem, hbm),
        scratch_shapes=[
            pltpu.VMEM((tokens, width), F32),
            pltpu.VMEM((tokens, width), BF),
            pltpu.VMEM((width, 2 * ff), BF),
            pltpu.VMEM((group_len, width), BF),
            pltpu.VMEM((group_len, width), BF),
            pltpu.VMEM((group_len, ff), BF),
            pltpu.VMEM((group_len, 2 * ff), BF),
            pltpu.VMEM((width, 2 * ff), BF),
            pltpu.VMEM((width, ff), BF),
            pltpu.VMEM((chunks, group_len // chunks, width), F32),
            pltpu.VMEM((tokens, width), F32),
            pltpu.VMEM((chunks, 2, n, tokens // chunks, width), BF),
            pltpu.SemaphoreType.DMA((4,)),
            pltpu.SemaphoreType.DMA((chunks,)),
            pltpu.SemaphoreType.DMA((chunks, n)),
            pltpu.SemaphoreType.DMA((chunks,)),
            pltpu.SemaphoreType.DMA((2 * ff // 256,)),
            pltpu.SemaphoreType.DMA((chunks, 2, n, 1)),
            pltpu.SemaphoreType.DMA((chunks, 2, n, 1)),
            pltpu.SemaphoreType.DMA((chunks, 2, n, 1)),
            pltpu.SemaphoreType.DMA((chunks, 2, n, 1)),
        ],
        compiler_params=pltpu.CompilerParams(
            collective_id=3, has_side_effects=True, vmem_limit_bytes=VMEM_LIMIT
        ),
        cost_estimate=pl.CostEstimate(
            flops=18 * group_len * width * ff, bytes_accessed=250 * tokens * width * 2, transcendentals=0
        ),
        name="feed_both",
    )(n2, gf_all, wgu, wd, m, gain, cot)


def attend_back_kernel(
    n,
    dp,
    kv_local,
    chunks,
    ga_hbm,
    wout_hbm,
    wd_hbm,
    z_hbm,
    prob_hbm,
    gf_hbm,
    dwgu_hbm,
    m_hbm,
    q_hbm,
    k_hbm,
    v_hbm,
    o_hbm,
    cos_hbm,
    low_hbm,
    high_hbm,
    out_hbm,
    stat_ref,
    dqkv_hbm,
    dwd_hbm,
    ga_out,
    grad_gu_hbm,
    out_ref,
    m_ref,
    q_ref,
    k_ref,
    v_ref,
    o_ref,
    cos_ref,
    sin_low_ref,
    sin_high_ref,
    dqkv_ref,
    dwd_ref,
    grad_gu_ref,
    keep,
    held,
    ga_all,
    gf,
    wout,
    wd,
    z_all,
    k_t,
    prob,
    d_out,
    dk,
    dv,
    part,
    sums,
    load_sem,
    gf_sem,
    prob_sem,
    out_sem,
    piece_sem,
    ag_send,
    ag_recv,
    rs_send,
    rs_recv,
    keep_sem,
    dp_send,
    dp_recv,
):
    z = lax.axis_index("tensor")
    me = lax.axis_index("dp")
    dp_bits = dp.bit_length() - 1
    others = [{"dp": across(me, bit)} for bit in range(dp_bits)]
    greet(n, others)
    tokens, width = ga_hbm.shape
    heads = REPEAT * kv_local
    group_len = n * tokens
    piece = tokens // chunks
    scale = HEAD_WIDTH ** (-0.5)
    loads = [
        pltpu.make_async_copy(source, target, load_sem.at[index])
        for index, (source, target) in enumerate(
            [
                (ga_hbm, ga_all.at[rows_at(z, tokens)]),
                (wout_hbm, wout),
                (k_hbm, k_ref),
                (v_hbm, v_ref),
                (q_hbm, q_ref),
                (o_hbm, o_ref),
                (cos_hbm, cos_ref),
                (low_hbm, sin_low_ref),
                (high_hbm, sin_high_ref),
                (z_hbm, z_all),
                (wd_hbm, wd),
                (m_hbm, m_ref),
            ]
        )
    ]
    for load in loads:
        load.start()

    def load_gf(chunk, slot):
        return pltpu.make_async_copy(
            gf_hbm.at[pl.ds(pl.multiple_of(slot * tokens + chunk * piece, piece), piece)],
            gf.at[pl.ds(pl.multiple_of((chunk * n + slot) * piece, piece), piece)],
            gf_sem.at[chunk, slot],
        )

    for chunk in range(chunks):
        for slot in range(n):
            load_gf(chunk, slot).start()

    def load_prob(slot):
        return pltpu.make_async_copy(prob_hbm.at[slot], prob, prob_sem)

    greeted(n, others)
    gather = Gather(n, lambda slot: ga_all.at[rows_at(slot, tokens)], ag_send, ag_recv)
    loads[0].wait()
    gather.begin()
    halving = Halving(
        dp, grad_gu_ref.shape[0], dwgu_hbm, keep, held, keep_sem, dp_send, dp_recv
    )
    halving.begin()
    scatter = Scatter(n, sums, rs_send, rs_recv)
    for load in loads[1:-1]:
        load.wait()
    for group in range(kv_local):
        k_t[group] = k_ref[group].astype(F32).T.astype(BF)
    dk[...] = jnp.zeros_like(dk)
    dv[...] = jnp.zeros_like(dv)
    group_lanes = (REPEAT + 2) * LANES

    def turn_back(values, rows):
        return (
            values * cos_ref[rows, :]
            - pltpu.roll(values, LANES - HEAD_WIDTH // 2, 1) * sin_low_ref[rows, :]
            - pltpu.roll(values, HEAD_WIDTH // 2, 1) * sin_high_ref[rows, :]
        )

    def back(slot):
        rows = rows_at(slot, tokens)
        d_o = nn(ga_all[rows, :], wout[...])
        d_out[...] = d_o.astype(BF)

        def one_head(head, carry):
            group = head // REPEAT
            lanes = rows_at(head, LANES)
            do_h = d_out[:, lanes]
            both = do_h.astype(F32) * o_ref[rows, lanes].astype(F32)
            delta = jnp.sum(both.T, axis=0, keepdims=True)
            dprob = nt(v_ref[group], do_h)
            weights = prob[head]
            ds = (weights.astype(F32) * (dprob - delta)).astype(BF)
            dv[group] += nn(weights, do_h)
            dk[group] += nn(ds, q_ref[head, rows, :])
            dq = nn(k_t[group], ds).T * scale
            first = group * (REPEAT + 2) + head % REPEAT
            dqkv_ref[rows, rows_at(first, LANES)] = turn_back(dq, rows).astype(BF)
            return carry

        lax.fori_loop(0, heads, one_head, 0)

    def feed_rows(target):
        pieces = [
            z_all[
                pl.ds(
                    pl.multiple_of(chunk * n * piece + target * piece, piece), piece
                ),
                :,
            ]
            for chunk in range(chunks)
        ]
        rows = jnp.concatenate(pieces, axis=0) if chunks > 1 else pieces[0]
        for first in range(0, width, 512):
            part[:, first : first + 512] = nt(rows, wd[first : first + 512, :])

    def turn_of(index, carry):
        came, near = (index + 1) // 2, (index + 1) % 2
        slot = z - (1 - 2 * near) * came
        valid = (slot >= 0) & (slot < n)

        @pl.when(valid)
        def _():
            load_prob(slot).start()

        @pl.when(index > 0)
        def _():
            gather.arrive(came, near, came < n - 1)

        step, side = index // 2 + 1, index % 2
        target, sends = scatter.turn(step, side)

        @pl.when(sends & (step < n))
        def _():
            feed_rows(target)
            scatter.push(step, side, part)

        @pl.when(valid)
        def _():
            load_prob(slot).wait()
            back(slot)

        return carry

    for chunk in range(chunks):
        for slot in range(n):
            load_gf(chunk, slot).wait()
    ff = wd_hbm.shape[1]
    down_blocks = ff // 256

    def grad_down(first, last):
        def body(index, carry):
            cols = rows_at(index, 256)
            dwd_ref[:, cols] = tn(gf[...], z_all[:, cols]).astype(BF)
            return carry

        lax.fori_loop(first, last, body, 0)

    turns = 2 * n - 1

    def turn_and_grad(index, carry):
        turn_of(index, 0)
        grad_down(down_blocks * index // turns, down_blocks * (index + 1) // turns)
        for stage in range(dp_bits):

            @pl.when(index == 2 * stage + 1)
            def _(stage=stage):
                halving.advance(stage)

        return carry

    lax.fori_loop(0, turns, turn_and_grad, 0)

    def finish_keys(slot, carry):
        rows = rows_at(slot, tokens)
        for group in range(kv_local):
            first = group * group_lanes + REPEAT * LANES
            dqkv_ref[rows, first : first + LANES] = turn_back(
                dk[group, rows, :] * scale, rows
            ).astype(BF)
            dqkv_ref[rows, first + LANES : first + 2 * LANES] = dv[group, rows, :].astype(BF)
        return carry

    lax.fori_loop(0, n, finish_keys, 0)
    outs = [
        pltpu.make_async_copy(source, target, out_sem.at[index])
        for index, (source, target) in enumerate(
            [(dqkv_ref, dqkv_hbm), (dwd_ref, dwd_hbm), (ga_all, ga_out), (grad_gu_ref, grad_gu_hbm)]
        )
    ]
    for out in outs[:3]:
        out.start()
    for half in range(2):
        grad_gu_ref[:, half, :] = halving.result(half)
    outs[3].start()
    feed_rows(z)
    loads[-1].wait()
    stat_ref[...] = jnp.zeros_like(stat_ref)

    def finish(rows):
        branch = part[rows, :]
        result = m_ref[rows, :] + branch
        out_ref[rows, :] = result
        stat_ref[0:1, :] += jnp.sum(result * result, axis=0, keepdims=True)
        stat_ref[1:2, :] += jnp.sum(branch * branch, axis=0, keepdims=True)

    def piece_out(piece):
        size = tokens // PIECES
        rows = pl.ds(piece * size, size)
        return pltpu.make_async_copy(out_ref.at[rows], out_hbm.at[rows], piece_sem.at[piece])

    def settled(piece, first, rows):
        by_rows(rows, finish, first)
        piece_out(piece).start()

    scatter.settle(part, settled)
    for piece in range(PIECES):
        piece_out(piece).wait()
    for out in outs:
        out.wait()
    gather.drain()
    scatter.drain()
    halving.drain()


def attend_back(n, dp, kv_local, chunks, ga, wout, wd, z_all, prob, gf, dwgu, m, q, k, v, o, tables):
    tokens, width = ga.shape
    group_len = n * tokens
    heads = REPEAT * kv_local
    ff = wd.shape[1]
    owned = width // dp
    lanes = (REPEAT + 2) * kv_local * LANES
    vmem = pl.BlockSpec(memory_space=pltpu.VMEM)
    hbm = pl.BlockSpec(memory_space=pl.ANY)
    return pl.pallas_call(
        functools.partial(attend_back_kernel, n, dp, kv_local, chunks),
        out_shape=(
            jax.ShapeDtypeStruct((tokens, width), F32),
            jax.ShapeDtypeStruct((8, width), F32),
            jax.ShapeDtypeStruct((group_len, lanes), BF),
            jax.ShapeDtypeStruct((width, ff), BF),
            jax.ShapeDtypeStruct((group_len, width), BF),
            jax.ShapeDtypeStruct((owned, 2, ff), F32),
        ),
        in_specs=[hbm] * 15,
        out_specs=(hbm, vmem, hbm, hbm, hbm, hbm),
        scratch_shapes=[
            pltpu.VMEM((tokens, width), F32),
            pltpu.VMEM((tokens, width), F32),
            pltpu.VMEM(q.shape, BF),
            pltpu.VMEM(k.shape, BF),
            pltpu.VMEM(v.shape, BF),
            pltpu.VMEM(o.shape, BF),
            *[pltpu.VMEM((group_len, LANES), F32)] * 3,
            pltpu.VMEM((group_len, lanes), BF),
            pltpu.VMEM((width, ff), BF),
            pltpu.VMEM((owned, 2, ff), F32),
            pltpu.VMEM((2, dp // 2, owned, ff), BF),
            pltpu.VMEM((2, dp - 1, owned, ff), BF),
            pltpu.VMEM((group_len, width), BF),
            pltpu.VMEM((group_len, width), BF),
            pltpu.VMEM(wout.shape, BF),
            pltpu.VMEM(wd.shape, BF),
            pltpu.VMEM((group_len, ff), BF),
            pltpu.VMEM((kv_local, LANES, group_len), BF),
            pltpu.VMEM((heads, group_len, tokens), BF),
            pltpu.VMEM((tokens, heads * LANES), BF),
            pltpu.VMEM((kv_local, group_len, LANES), F32),
            pltpu.VMEM((kv_local, group_len, LANES), F32),
            pltpu.VMEM((tokens, width), F32),
            pltpu.VMEM((2, n, tokens, width), BF),
            pltpu.SemaphoreType.DMA((12,)),
            pltpu.SemaphoreType.DMA((chunks, n)),
            pltpu.SemaphoreType.DMA,
            pltpu.SemaphoreType.DMA((4,)),
            pltpu.SemaphoreType.DMA((PIECES,)),
            pltpu.SemaphoreType.DMA((2, n, PIECES)),
            pltpu.SemaphoreType.DMA((2, n, PIECES)),
            pltpu.SemaphoreType.DMA((2, n, PIECES)),
            pltpu.SemaphoreType.DMA((2, n, PIECES)),
            pltpu.SemaphoreType.DMA((2, dp // 2)),
            pltpu.SemaphoreType.DMA((2, dp)),
            pltpu.SemaphoreType.DMA((2, dp)),
        ],
        compiler_params=pltpu.CompilerParams(
            collective_id=4, has_side_effects=True, vmem_limit_bytes=VMEM_LIMIT
        ),
        cost_estimate=pl.CostEstimate(
            flops=8 * group_len * width * ff, bytes_accessed=200 * tokens * width * 2, transcendentals=0
        ),
        name="attend_backward",
    )(ga, wout, wd, z_all, prob, gf, dwgu, m, q, k, v, o, *tables)


class Sharing:
    def __init__(self, axis, size, source, slots, send_sem, recv_sem):
        self.axis, self.size, self.source, self.slots = axis, size, source, slots
        self.send_sem, self.recv_sem = send_sem, recv_sem
        self.me = lax.axis_index(axis)

    def copy(self, offset):
        return pltpu.make_async_remote_copy(
            src_ref=self.source,
            dst_ref=self.slots.at[self.me],
            send_sem=self.send_sem.at[offset],
            recv_sem=self.recv_sem.at[offset],
            device_id={self.axis: (self.me + offset) % self.size},
            device_id_type=MESH,
        )

    def arrival(self, offset):
        place = self.slots.at[(self.me + self.size - offset) % self.size]
        return pltpu.make_async_remote_copy(
            src_ref=place,
            dst_ref=place,
            send_sem=self.send_sem.at[offset],
            recv_sem=self.recv_sem.at[offset],
            device_id={self.axis: (self.me + self.size - offset) % self.size},
            device_id_type=MESH,
        )

    def begin(self):
        for offset in range(1, self.size):
            self.copy(offset).start()
        self.slots[self.me] = self.source[...]

    def total(self):
        for offset in range(1, self.size):
            self.arrival(offset).wait_recv()
        total = self.slots[0]
        for index in range(1, self.size):
            total = total + self.slots[index]
        return total

    def drain(self):
        for offset in range(1, self.size):
            self.copy(offset).wait_send()


def last_kernel(
    n,
    dp,
    cells,
    out_heads,
    dqkv_hbm,
    wqkv_hbm,
    x_hbm,
    dm_hbm,
    gain_ref,
    dgain_two_ref,
    stat_one_ref,
    stat_two_ref,
    g1_hbm,
    ga_hbm,
    o_hbm,
    dwd_hbm,
    dx_hbm,
    gains_ref,
    rms_ref,
    grad_out_ref,
    grad_qkv_ref,
    grad_down_ref,
    dx_ref,
    dqkv,
    wqkv,
    x,
    dm,
    g1,
    ga,
    o,
    dw,
    part,
    sums,
    down_keep,
    down_held,
    head_keep,
    head_held,
    vector,
    packed,
    group_sum,
    dp_slots,
    z_slots,
    load_sem,
    piece_sem,
    rs_send,
    rs_recv,
    down_keep_sem,
    down_send,
    down_recv,
    head_keep_sem,
    head_send,
    head_recv,
    dp_slot_send,
    dp_slot_recv,
    z_slot_send,
    z_slot_recv,
):
    z = lax.axis_index("tensor")
    me = lax.axis_index("dp")
    tokens, width = x.shape
    dp_bits = dp.bit_length() - 1
    others = [{"dp": (me + offset) % dp} for offset in range(1, dp)]
    others += [{"tensor": (z + offset) % n} for offset in range(1, n)]
    barrier = pltpu.get_barrier_semaphore()
    for other in others:
        pl.semaphore_signal(barrier, inc=1, device_id=other, device_id_type=MESH)
    owned = grad_out_ref.shape[0]
    loads = [
        pltpu.make_async_copy(source, target, load_sem.at[index])
        for index, (source, target) in enumerate(
            [
                (wqkv_hbm, wqkv),
                (dqkv_hbm, dqkv),
                (g1_hbm, g1),
                (ga_hbm, ga),
                (o_hbm, o),
                (x_hbm, x),
                (dm_hbm, dm),
            ]
        )
    ]
    for load in loads:
        load.start()
    pl.semaphore_wait(barrier, len(others))
    down = Halving(dp, owned, dwd_hbm, down_keep, down_held, down_keep_sem, down_send, down_recv)
    down.begin()
    halving = Halving(dp, owned, dw, head_keep, head_held, head_keep_sem, head_send, head_recv)
    scatter = Scatter(n, sums, rs_send, rs_recv)
    gain = gain_ref[0, 0:1, :]
    vector[...] = jnp.zeros_like(vector)
    vector[1:2, :] = dgain_two_ref[0:1, :]
    vector[2:3, :] = stat_one_ref[0:1, :]
    vector[3:4, :] = stat_two_ref[0:1, :]
    vector[4:5, :] = stat_one_ref[1:2, :]
    vector[5:6, :] = stat_two_ref[1:2, :]
    for load in loads[:3]:
        load.wait()
    out_lanes = o.shape[1]

    def grad_qkv(index, carry):
        place = pl.ds(pl.multiple_of(out_lanes + index * 256, 256), 256)
        dw[:, place] = tn(g1[...], dqkv[:, rows_at(index, 256)]).astype(BF)
        return carry

    def grad_out(index, carry):
        cols = rows_at(index, 256)
        dw[:, cols] = tn(ga[...], o[:, cols]).astype(BF)
        return carry

    def compute(index, carry):
        step, side = index // 2 + 1, index % 2
        target, due = scatter.turn(step, side)

        @pl.when(due)
        def _():
            rows = rows_at(target, tokens)

            def block(number, carry):
                cols = rows_at(number, 256)
                values = nt(dqkv[rows, :], wqkv[cols, :])
                part[rows, cols] = values
                vector[0:1, cols] += jnp.sum(
                    values * g1[rows, cols].astype(F32), axis=0, keepdims=True
                )
                return carry

            lax.fori_loop(0, width // 256, block, 0)

            @pl.when((step < n - 1) & jnp.logical_not(scatter.has_source(side)))
            def _():
                scatter.push(step, side, part, target * tokens)

        return carry

    def compute_and_grads(index, carry):
        compute(index, 0)

        @pl.when(index == 1)
        def _():
            for load in loads[3:]:
                load.wait()
            lax.fori_loop(0, dqkv.shape[1] // 256, grad_qkv, 0)
            lax.fori_loop(0, out_lanes // 256, grad_out, 0)
            halving.begin()

        return carry

    lax.fori_loop(0, 2 * n - 1, compute_and_grads, 0)
    vector[0:1, :] = vector[0:1, :] / gain

    blocks = width // LANES
    packed[...] = jnp.zeros_like(packed)
    for row in range(6):
        parts = [
            vector[row : row + 1, index * LANES : (index + 1) * LANES] for index in range(blocks)
        ]
        if row < 2:
            for index, values in enumerate(parts):
                packed[row * blocks + index : row * blocks + index + 1, :] = values
        else:
            place = 2 * blocks + row - 2
            packed[place : place + 1, :] = functools.reduce(jnp.add, parts)
    near = Sharing("dp", dp, packed, dp_slots, dp_slot_send, dp_slot_recv)
    far = Sharing("tensor", n, group_sum, z_slots, z_slot_send, z_slot_recv)
    near.begin()
    down.advance(0)
    halving.advance(0)

    def push_came(step):
        for side in range(2):
            target, sends = scatter.turn(step, side)

            @pl.when(sends & scatter.has_source(side))
            def _(side=side, target=target):
                scatter.push(step, side, part, target * tokens)

    def push_last_start():
        for side in range(2):
            target, sends = scatter.turn(n - 1, side)

            @pl.when(sends & jnp.logical_not(scatter.has_source(side)))
            def _(side=side, target=target):
                scatter.push(n - 1, side, part, target * tokens)

    done = 1
    for step in range(2, n):
        push_came(step)
        if step == 2:
            group_sum[...] = near.total()
            far.begin()
            push_last_start()
        until = 1 + (dp_bits - 1) * (step - 1) // (n - 1)
        for stage in range(done, until):
            down.advance(stage)
            halving.advance(stage)
        done = until
    for stage in range(done, dp_bits):
        down.advance(stage)
        halving.advance(stage)
    for half in range(2):
        columns = down.columns(half)
        grad_down_ref[:, columns] = down.result(half)
    place = 0
    for half in range(2):
        block = halving.result(half)
        for index in range(block.shape[1] // LANES):
            values = block[:, index * LANES : index * LANES + HEAD_WIDTH]
            if place < out_heads:
                grad_out_ref[:, place * HEAD_WIDTH : (place + 1) * HEAD_WIDTH] = values
            else:
                head = place - out_heads
                grad_qkv_ref[:, head * HEAD_WIDTH : (head + 1) * HEAD_WIDTH] = values
            place += 1
    total = far.total()
    for which in range(2):
        for index in range(blocks):
            gains_ref[0, which : which + 1, index * LANES : (index + 1) * LANES] = total[
                which * blocks + index : which * blocks + index + 1, :
            ]
    squares = jnp.sqrt(jnp.sum(total, axis=1, keepdims=True) * (1.0 / cells))
    row = lax.broadcasted_iota(jnp.int32, (total.shape[0], 4), 0)
    column = lax.broadcasted_iota(jnp.int32, (total.shape[0], 4), 1)
    rms_ref[...] = jnp.sum(jnp.where(row == column + 2 * blocks, squares, 0.0), axis=0, keepdims=True)
    own = part.at[rows_at(z, tokens)]

    def finish(rows):
        values = x[rows, :]
        dn = own[rows, :]
        inverse = lax.rsqrt(jnp.mean(values * values, axis=-1, keepdims=True) + norm_eps)
        scaled = dn * gain
        dx_ref[rows, :] = (
            inverse * scaled
            - values * inverse**3 * jnp.mean(scaled * values, axis=-1, keepdims=True)
            + dm[rows, :]
        )

    def piece_out(piece):
        size = tokens // PIECES
        rows = pl.ds(piece * size, size)
        return pltpu.make_async_copy(dx_ref.at[rows], dx_hbm.at[rows], piece_sem.at[piece])

    def settled(piece, first, rows):
        by_rows(rows, finish, first)
        piece_out(piece).start()

    scatter.settle(own, settled)
    for piece in range(PIECES):
        piece_out(piece).wait()
    near.drain()
    far.drain()
    down.drain()
    halving.drain()
    scatter.drain()


def last(n, dqkv, wqkv, x, dm, gain, dgain_two, stat_one, stat_two, g1, ga, o, dwd, out_columns, qkv_columns):
    tokens, width = x.shape
    dp = lax.axis_size("dp")
    owned = width // dp
    ff = dwd.shape[1]
    columns = o.shape[1] + dqkv.shape[1]
    small = -(-(2 * width // LANES + 4) // 8) * 8
    vmem = pl.BlockSpec(memory_space=pltpu.VMEM)
    hbm = pl.BlockSpec(memory_space=pl.ANY)
    return pl.pallas_call(
        functools.partial(last_kernel, n, dp, tokens * width * dp * n, out_columns // HEAD_WIDTH),
        out_shape=(
            jax.ShapeDtypeStruct((tokens, width), F32),
            jax.ShapeDtypeStruct((1, 2, width), F32),
            jax.ShapeDtypeStruct((1, 4), F32),
            jax.ShapeDtypeStruct((owned, out_columns), F32),
            jax.ShapeDtypeStruct((owned, qkv_columns), F32),
            jax.ShapeDtypeStruct((owned, ff), F32),
        ),
        in_specs=[hbm] * 4 + [vmem] * 4 + [hbm] * 4,
        out_specs=(hbm,) + (vmem,) * 5,
        scratch_shapes=[
            pltpu.VMEM(x.shape, F32),
            pltpu.VMEM(dqkv.shape, BF),
            pltpu.VMEM(wqkv.shape, BF),
            pltpu.VMEM(x.shape, F32),
            pltpu.VMEM(dm.shape, F32),
            pltpu.VMEM(g1.shape, BF),
            pltpu.VMEM(ga.shape, BF),
            pltpu.VMEM(o.shape, BF),
            pltpu.VMEM((width, columns), BF),
            pltpu.VMEM((n * tokens, width), F32),
            pltpu.VMEM((2, n, tokens, width), BF),
            pltpu.VMEM((2, dp // 2, owned, ff // 2), BF),
            pltpu.VMEM((2, dp - 1, owned, ff // 2), BF),
            pltpu.VMEM((2, dp // 2, owned, columns // 2), BF),
            pltpu.VMEM((2, dp - 1, owned, columns // 2), BF),
            pltpu.VMEM((8, width), F32),
            pltpu.VMEM((small, LANES), F32),
            pltpu.VMEM((small, LANES), F32),
            pltpu.VMEM((dp, small, LANES), F32),
            pltpu.VMEM((n, small, LANES), F32),
            pltpu.SemaphoreType.DMA((7,)),
            pltpu.SemaphoreType.DMA((PIECES,)),
            pltpu.SemaphoreType.DMA((2, n, PIECES)),
            pltpu.SemaphoreType.DMA((2, n, PIECES)),
            *[
                pltpu.SemaphoreType.DMA((2, dp // 2)),
                pltpu.SemaphoreType.DMA((2, dp)),
                pltpu.SemaphoreType.DMA((2, dp)),
            ]
            * 2,
            pltpu.SemaphoreType.DMA((dp,)),
            pltpu.SemaphoreType.DMA((dp,)),
            pltpu.SemaphoreType.DMA((n,)),
            pltpu.SemaphoreType.DMA((n,)),
        ],
        compiler_params=pltpu.CompilerParams(
            collective_id=5, has_side_effects=True, vmem_limit_bytes=VMEM_LIMIT
        ),
        cost_estimate=pl.CostEstimate(
            flops=2 * dqkv.size * width, bytes_accessed=150 * tokens * width * 2, transcendentals=0
        ),
        name="input_gradient",
    )(dqkv, wqkv, x, dm, gain, dgain_two, stat_one, stat_two, g1, ga, o, dwd)


def deliver_kernel(*refs):
    count = len(refs) // 3
    sources, targets, held = refs[:count], refs[count : 2 * count], refs[2 * count : 3 * count]
    sem = refs[-1]
    ins = [
        pltpu.make_async_copy(source, place, sem.at[0, index])
        for index, (source, place) in enumerate(zip(sources, held, strict=True))
    ]
    outs = [
        pltpu.make_async_copy(place, target, sem.at[1, index])
        for index, (place, target) in enumerate(zip(held, targets, strict=True))
    ]
    for copy in ins:
        copy.start()
    for copy, out in zip(ins, outs, strict=True):
        copy.wait()
        out.start()
    for out in outs:
        out.wait()


def deliver(*arrays):
    hbm = pl.BlockSpec(memory_space=pl.ANY)
    return pl.pallas_call(
        deliver_kernel,
        out_shape=[jax.ShapeDtypeStruct(array.shape, array.dtype) for array in arrays],
        in_specs=[hbm] * len(arrays),
        out_specs=[hbm] * len(arrays),
        scratch_shapes=[
            *[pltpu.VMEM(array.shape, array.dtype) for array in arrays],
            pltpu.SemaphoreType.DMA((2, len(arrays))),
        ],
        compiler_params=pltpu.CompilerParams(vmem_limit_bytes=VMEM_LIMIT),
        name="deliver",
    )(*arrays)


def per_device(inputs, norm_gains, w_qkv, w_gate_up, w_out, w_down, segments, positions, cotangent):
    n, dp = lax.axis_size("tensor"), lax.axis_size("dp")
    tokens, width = inputs.shape
    kv_local = w_out.shape[2] // (REPEAT * HEAD_WIDTH)
    chunks = 8
    half = HEAD_WIDTH // 2
    freq_steps = jnp.arange(half, dtype=F32) * (2.0 / HEAD_WIDTH)
    inverse = jnp.power(rope_base, -freq_steps)
    freq = jnp.concatenate([inverse, inverse, jnp.zeros((LANES - HEAD_WIDTH,), F32)])[None]

    (
        wqkv,
        wout,
        wgu,
        wd,
        g1,
        q,
        k,
        v,
        o,
        cosine,
        low,
        high,
        prob,
        gf_all,
        m,
        n2,
        stat_one,
    ) = forward(
        n,
        dp,
        kv_local,
        inputs,
        norm_gains,
        w_qkv,
        w_gate_up,
        w_out,
        w_down,
        cotangent,
        segments.reshape(n, 1, tokens),
        positions.reshape(n, 1, tokens),
        freq,
    )
    z_all, dm, ga, dgain_two, dwgu = feed(n, chunks, n2, gf_all, wgu, wd, m, norm_gains, cotangent)
    output, stat_two, dqkv, dwd, ga_all, grad_gu = attend_back(
        n,
        dp,
        kv_local,
        chunks,
        ga,
        wout,
        wd,
        z_all,
        prob,
        gf_all,
        dwgu,
        m,
        q,
        k,
        v,
        o,
        (cosine, low, high),
    )
    input_grad, gain_total, rms, grad_out, grad_qkv, grad_down = last(
        n,
        dqkv,
        wqkv,
        inputs,
        dm,
        norm_gains,
        dgain_two,
        stat_one,
        stat_two,
        g1,
        ga_all,
        o,
        dwd,
        w_out.shape[2],
        w_qkv.shape[2],
    )
    output, input_grad, grad_qkv, grad_gu, grad_out, grad_down, gain_total, rms = deliver(
        output, input_grad, grad_qkv, grad_gu, grad_out, grad_down, gain_total, rms
    )
    return (
        output,
        input_grad,
        grad_qkv[None],
        grad_gu[None],
        grad_out[None],
        grad_down[None],
        gain_total,
        rms,
    )


def solution(mesh):
    rows = P(("dp", "tensor"), None)
    weights = P(None, "dp", "tensor")
    pairs = P(None, "dp", None, "tensor")
    return jax.shard_map(
        per_device,
        mesh=mesh,
        in_specs=(rows, P(), weights, pairs, weights, weights, P("dp"), P("dp"), rows),
        out_specs=(rows, rows, weights, pairs, weights, weights, P(), P()),
        check_vma=False,
    )
```

```python
import functools

import jax
import jax.numpy as jnp
from jax import lax
from jax.experimental import pallas as pl
from jax.experimental.pallas import tpu as pltpu
from jax.sharding import PartitionSpec as P

HEADS = 16
KV_HEADS = 8
HEAD_WIDTH = 96
REPEAT = HEADS // KV_HEADS
LANES = 128

norm_eps = 1e-05
rope_base = 100000.0
MESH = pl.DeviceIdType.MESH
BF = jnp.bfloat16
F32 = jnp.float32
VMEM_LIMIT = 60 * 2**20
PIECES = 2
LAG = 2


def nn(a, b):
    return lax.dot_general(a, b, (((1,), (0,)), ((), ())), preferred_element_type=F32)


def nt(a, b):
    return lax.dot_general(a, b, (((1,), (1,)), ((), ())), preferred_element_type=F32)


def tn(a, b):
    return lax.dot_general(a, b, (((0,), (0,)), ((), ())), preferred_element_type=F32)


def rows_at(index, size):
    return pl.ds(pl.multiple_of(index * size, size), size)


def greet(n, others=()):
    z = lax.axis_index("tensor")
    barrier = pltpu.get_barrier_semaphore()

    @pl.when(z > 0)
    def _():
        pl.semaphore_signal(barrier, inc=1, device_id={"tensor": z - 1}, device_id_type=MESH)

    @pl.when(z < n - 1)
    def _():
        pl.semaphore_signal(barrier, inc=1, device_id={"tensor": z + 1}, device_id_type=MESH)

    for other in others:
        pl.semaphore_signal(barrier, inc=1, device_id=other, device_id_type=MESH)


def greeted(n, others=()):
    z = lax.axis_index("tensor")
    barrier = pltpu.get_barrier_semaphore()

    @pl.when((z > 0) & (z < n - 1))
    def _():
        pl.semaphore_wait(barrier, 2 + len(others))

    @pl.when((z == 0) | (z == n - 1))
    def _():
        pl.semaphore_wait(barrier, 1 + len(others))


def bit_of(index, bit):
    return (index // (1 << bit)) % 2


def across(index, bit):
    return index + (1 << bit) * (1 - 2 * bit_of(index, bit))


class Gather:
    def __init__(self, n, at, send_sem, recv_sem):
        self.n, self.at, self.send_sem, self.recv_sem = n, at, send_sem, recv_sem
        self.z = lax.axis_index("tensor")
        self.pieces = send_sem.shape[-1]

    def copy(self, slot, step, side, piece, source=None):
        block = self.at(slot)
        size = block.shape[0] // self.pieces
        rows = pl.ds(piece * size, size)
        return pltpu.make_async_remote_copy(
            src_ref=(block if source is None else source).at[rows],
            dst_ref=block.at[rows],
            send_sem=self.send_sem.at[side, step, piece],
            recv_sem=self.recv_sem.at[side, step, piece],
            device_id={"tensor": self.z + 1 - 2 * side},
            device_id_type=MESH,
        )

    def sends(self, step, side):
        z, n = self.z, self.n
        slot = z - (1 - 2 * side) * (step - 1)
        target = z + 1 - 2 * side
        return slot, (slot >= 0) & (slot < n) & (target >= 0) & (target < n)

    def send(self, step, side, piece, source=None, where=True):
        slot, valid = self.sends(step, side)

        @pl.when(valid if where is True else valid & where)
        def _():
            self.copy(slot, step, side, piece, source).start()

    def begin(self, source=None):
        for piece in range(self.pieces):
            for side in range(2):
                self.send(1, side, piece, source)

    def begin_where(self, passes_on):
        for side in range(2):
            source = self.z - (1 - 2 * side)
            other = (source >= 0) & (source < self.n)
            for piece in range(self.pieces):
                self.send(1, side, piece, where=other if passes_on else jnp.logical_not(other))

    def arrive(self, step, side, forward):
        z, n = self.z, self.n
        slot = z - (1 - 2 * side) * step
        for piece in range(self.pieces):

            @pl.when((slot >= 0) & (slot < n))
            def _(piece=piece):
                self.copy(slot, step, side, piece).wait_recv()

            if forward is not False:
                self.send(step + 1, side, piece, where=forward)

    def drain(self, source=None):
        for step in range(1, self.n):
            for side in range(2):
                slot, valid = self.sends(step, side)
                for piece in range(self.pieces):

                    @pl.when(valid)
                    def _(slot=slot, step=step, side=side, piece=piece):
                        self.copy(
                            slot, step, side, piece, source if step == 1 else None
                        ).wait_send()


class Scatter:
    def __init__(self, n, buffer, send_sem, recv_sem):
        self.n, self.buffer, self.send_sem, self.recv_sem = n, buffer, send_sem, recv_sem
        self.z = lax.axis_index("tensor")
        self.pieces = send_sem.shape[-1]
        self.size = buffer.shape[2] // self.pieces

    def rows(self, piece):
        return pl.ds(piece * self.size, self.size)

    def copy(self, step, side, piece):
        return pltpu.make_async_remote_copy(
            src_ref=self.buffer.at[side, step - 1, self.rows(piece)],
            dst_ref=self.buffer.at[side, step, self.rows(piece)],
            send_sem=self.send_sem.at[side, step, piece],
            recv_sem=self.recv_sem.at[side, step, piece],
            device_id={"tensor": self.z + 1 - 2 * side},
            device_id_type=MESH,
        )

    def turn(self, step, side):
        z, n = self.z, self.n
        return z + (1 - 2 * side) * (n - step), step >= 1 + z + side * (n - 1 - 2 * z)

    def has_source(self, side):
        source = self.z - (1 - 2 * side)
        return (source >= 0) & (source < self.n)

    def push(self, step, side, part, first=0):
        has_source = self.has_source(side)
        for piece in range(self.pieces):
            slot = self.buffer.at[side, step - 1, self.rows(piece)]
            rows = pl.ds(pl.multiple_of(first + piece * self.size, self.size), self.size)

            @pl.when(has_source)
            def _(piece=piece, slot=slot, rows=rows):
                self.copy(step - 1, side, piece).wait_recv()
                slot[...] = (part[rows, :] + slot[...].astype(F32)).astype(BF)

            @pl.when(jnp.logical_not(has_source))
            def _(slot=slot, rows=rows):
                slot[...] = part[rows, :].astype(BF)

            self.copy(step, side, piece).start()

    def settle(self, total_ref, then=None):
        for piece in range(self.pieces):
            for side in range(2):

                @pl.when(self.has_source(side))
                def _(side=side, piece=piece):
                    rows = self.rows(piece)
                    self.copy(self.n - 1, side, piece).wait_recv()
                    total_ref[rows, :] += self.buffer[side, self.n - 1, rows, :].astype(F32)

            if then is not None:
                then(piece, piece * self.size, self.size)

    def drain(self):
        for step in range(1, self.n):
            for side in range(2):
                for piece in range(self.pieces):

                    @pl.when(self.turn(step, side)[1])
                    def _(step=step, side=side, piece=piece):
                        self.copy(step, side, piece).wait_send()


def by_rows(rows, body, first=0, block=32):
    def step(index, carry):
        body(pl.ds(pl.multiple_of(first + index * block, block), block))
        return carry

    lax.fori_loop(0, rows // block, step, 0)


def norm_rows(values, gain):
    inverse = lax.rsqrt(jnp.mean(values * values, axis=-1, keepdims=True) + norm_eps)
    return values * inverse * gain, inverse


class Doubling:
    def __init__(self, size, source, target, keep_sem, send_sem, recv_sem):
        self.source, self.target = source, target
        self.keep_sem, self.send_sem, self.recv_sem = keep_sem, send_sem, recv_sem
        self.rows, columns = source.shape
        self.half = columns // 2
        self.me = lax.axis_index("dp")
        self.bits = size.bit_length() - 1
        rest = list(range(1, self.bits))
        self.orders = (rest + [0], rest[::-1] + [0])

    def index(self, order, stage, number):
        index = self.me
        for place in range(stage):
            if (number >> place) & 1:
                index = across(index, order[place])
        return index

    def copy(self, half, stage, number):
        order = self.orders[half]
        columns = slice(half * self.half, (half + 1) * self.half)
        place = self.target.at[rows_at(self.index(order, stage, number), self.rows), columns]
        return pltpu.make_async_remote_copy(
            src_ref=self.source.at[:, columns] if number == 0 else place,
            dst_ref=place,
            send_sem=self.send_sem.at[half, (1 << stage) + number],
            recv_sem=self.recv_sem.at[half, (1 << stage) + number],
            device_id={"dp": across(self.me, order[stage])},
            device_id_type=MESH,
        )

    def arrival(self, half, stage, number):
        order = self.orders[half]
        columns = slice(half * self.half, (half + 1) * self.half)
        index = across(self.index(order, stage, number), order[stage])
        place = self.target.at[rows_at(index, self.rows), columns]
        return pltpu.make_async_remote_copy(
            src_ref=place,
            dst_ref=place,
            send_sem=self.send_sem.at[half, (1 << stage) + number],
            recv_sem=self.recv_sem.at[half, (1 << stage) + number],
            device_id={"dp": across(self.me, order[stage])},
            device_id_type=MESH,
        )

    def own(self):
        return pltpu.make_async_copy(
            self.source, self.target.at[rows_at(self.me, self.rows)], self.keep_sem
        )

    def start(self, stage):
        for half in range(2):
            for number in range(1 << stage):
                self.copy(half, stage, number).start()

    def begin(self):
        self.own().start()
        self.start(0)

    def advance(self, stage):
        for half in range(2):
            for number in range(1 << stage):
                self.arrival(half, stage, number).wait_recv()
        if stage + 1 < self.bits:
            self.start(stage + 1)

    def drain(self, own=True):
        if own:
            self.own().wait()
        for half in range(2):
            for stage in range(self.bits):
                for number in range(1 << stage):
                    self.copy(half, stage, number).wait_send()


class Halving:
    def __init__(self, size, rows, grad, keep, buffer, keep_sem, send_sem, recv_sem):
        self.rows, self.grad, self.keep, self.buffer = rows, grad, keep, buffer
        self.keep_sem, self.send_sem, self.recv_sem = keep_sem, send_sem, recv_sem
        self.me = lax.axis_index("dp")
        self.bits = size.bit_length() - 1
        rest = list(range(1, self.bits))
        self.orders = ([0] + rest, [0] + rest[::-1])
        self.half = buffer.shape[-1]
        self.size = size

    def count(self, stage):
        return self.size >> (stage + 1)

    def offset(self, stage):
        return self.size - (self.size >> stage)

    def block_rows(self, half, number, mine):
        order = self.orders[half]
        first = bit_of(self.me, 0)
        index = first if mine else 1 - first
        later = order[1:]
        for place, bit in enumerate(later):
            index = index + ((number >> (len(later) - 1 - place)) & 1) * (1 << bit)
        return rows_at(index, self.rows)

    def columns(self, half):
        return slice(half * self.half, (half + 1) * self.half)

    def load(self, half, number):
        return pltpu.make_async_copy(
            self.grad.at[self.block_rows(half, number, True), self.columns(half)],
            self.keep.at[half, number],
            self.keep_sem.at[half, number],
        )

    def first_copy(self, half, number):
        return pltpu.make_async_remote_copy(
            src_ref=self.grad.at[self.block_rows(half, number, False), self.columns(half)],
            dst_ref=self.buffer.at[half, number],
            send_sem=self.send_sem.at[half, number],
            recv_sem=self.recv_sem.at[half, number],
            device_id={"dp": across(self.me, 0)},
            device_id_type=MESH,
        )

    def copy(self, half, stage):
        bit = self.orders[half][stage]
        count = self.count(stage)
        goes = (1 - bit_of(self.me, bit)) * count + self.offset(stage - 1)
        return pltpu.make_async_remote_copy(
            src_ref=self.buffer.at[half, pl.ds(goes, count)],
            dst_ref=self.buffer.at[half, pl.ds(self.offset(stage), count)],
            send_sem=self.send_sem.at[half, self.offset(stage)],
            recv_sem=self.recv_sem.at[half, self.offset(stage)],
            device_id={"dp": across(self.me, bit)},
            device_id_type=MESH,
        )

    def begin(self):
        for half in range(2):
            for number in range(self.count(0)):
                self.first_copy(half, number).start()
                self.load(half, number).start()

    def advance(self, stage):
        for half in range(2):
            if stage == 0:
                for number in range(self.count(0)):
                    self.first_copy(half, number).wait_recv()
                    self.load(half, number).wait()
            else:
                self.copy(half, stage).wait_recv()
            if stage == self.bits - 1:
                continue
            base = bit_of(self.me, self.orders[half][stage]) * self.count(stage)

            def add(number, carry, half=half, base=base):
                place = self.offset(stage) + number
                if stage == 0:
                    kept = self.keep[half, number]
                else:
                    kept = self.buffer[half, self.offset(stage - 1) + base + number]
                self.buffer[half, place] = (
                    self.buffer[half, place].astype(F32) + kept.astype(F32)
                ).astype(BF)
                return carry

            lax.fori_loop(0, self.count(stage), add, 0)
            self.copy(half, stage + 1).start()

    def result(self, half):
        stage = self.bits - 1
        base = bit_of(self.me, self.orders[half][stage])
        return self.buffer[half, self.offset(stage)].astype(F32) + self.buffer[
            half, self.offset(stage - 1) + base
        ].astype(F32)

    def drain(self):
        for half in range(2):
            for number in range(self.count(0)):
                self.first_copy(half, number).wait_send()
            for stage in range(1, self.bits):
                self.copy(half, stage).wait_send()


def forward_kernel(
    n,
    dp,
    kv_local,
    x_ref,
    gains_ref,
    wq_ref,
    wgu_ref,
    wo_ref,
    wd_ref,
    cot_ref,
    seg_ref,
    pos_ref,
    freq_ref,
    wqkv_hbm,
    wout_hbm,
    wgu_hbm,
    wd_hbm,
    g1_hbm,
    q_hbm,
    k_hbm,
    v_hbm,
    o_hbm,
    cos_hbm,
    low_hbm,
    high_hbm,
    prob_hbm,
    gf_all,
    m_hbm,
    n2_hbm,
    stat_ref,
    m_ref,
    n2_ref,
    g1,
    wqkv,
    wout,
    own_qkv,
    own_out,
    own_gu,
    q_ref,
    k_ref,
    v_ref,
    o_ref,
    cos_ref,
    low_ref,
    high_ref,
    v_t,
    key_seg,
    key_pos,
    bias,
    prob,
    part,
    sums,
    load_sem,
    out_sem,
    piece_sem,
    prob_sem,
    own_sem,
    n1_send,
    n1_recv,
    ag_send,
    ag_recv,
    rs_send,
    rs_recv,
    keep_sem,
    dp_send,
    dp_recv,
):
    z = lax.axis_index("tensor")
    me = lax.axis_index("dp")
    tokens, width = x_ref.shape
    heads = REPEAT * kv_local
    ff = wd_ref.shape[2]
    half_head = HEAD_WIDTH // 2
    dp_bits = dp.bit_length() - 1
    gain_one, gain_two = gains_ref[0, 0:1, :], gains_ref[0, 1:2, :]
    others = [{"dp": across(me, bit)} for bit in range(dp_bits)]
    greet(n, others)
    first_row = pl.multiple_of(z * tokens, tokens)

    def normalize(rows):
        place = pl.ds(pl.multiple_of(first_row + rows.start, rows.size), rows.size)
        g1[place, :] = norm_rows(x_ref[rows, :], gain_one)[0].astype(BF)

    by_rows(tokens, normalize)
    greeted(n, others)
    spread = Gather(n, lambda slot: g1.at[rows_at(slot, tokens)], n1_send, n1_recv)
    spread.begin()
    shards = [
        Doubling(dp, source, target, keep_sem.at[k], dp_send.at[k], dp_recv.at[k])
        for k, (source, target) in enumerate(
            [
                (own_qkv, wqkv_hbm),
                (own_out, wout_hbm),
                (own_gu, wgu_hbm),
                (wd_ref.at[0], wd_hbm),
            ]
        )
    ]
    early, late = shards[:2], shards[2:]
    for padded, shard in ((own_qkv, wq_ref), (own_out, wo_ref)):
        padded[...] = jnp.zeros_like(padded)
        for head in range(padded.shape[1] // LANES):
            padded[:, head * LANES : head * LANES + HEAD_WIDTH] = shard[
                0, :, head * HEAD_WIDTH : (head + 1) * HEAD_WIDTH
            ]
    for shard in early:
        shard.begin()
    own_gu[:, :ff] = wgu_ref[0, :, 0, :]
    own_gu[:, ff:] = wgu_ref[0, :, 1, :]

    def tables(slot, carry):
        rows = rows_at(slot, tokens)

        def column(row):
            return jnp.broadcast_to(row.astype(F32), (LANES, tokens)).T

        places = column(pos_ref[slot])
        key_pos[rows, :] = places
        key_seg[rows, :] = column(seg_ref[slot])
        angles = places * freq_ref[...]
        sine = jnp.sin(angles)
        lane = lax.broadcasted_iota(jnp.int32, sine.shape, 1)
        cos_ref[rows, :] = jnp.cos(angles)
        low_ref[rows, :] = jnp.where(lane < half_head, -sine, 0.0)
        high_ref[rows, :] = jnp.where((lane >= half_head) & (lane < HEAD_WIDTH), sine, 0.0)
        return carry

    lax.fori_loop(0, n, tables, 0)
    for shard in early:
        shard.advance(0)
    for side in range(2):
        spread.arrive(1, side, n > 2)
    for stage in range(1, dp_bits):
        for shard in early:
            shard.advance(stage)
        if stage == max(dp_bits - 2, 1):
            for shard in late:
                shard.begin()
    for shard in early:
        shard.own().wait()
    loads = [
        pltpu.make_async_copy(wqkv_hbm, wqkv, load_sem.at[0]),
        pltpu.make_async_copy(wout_hbm, wout, load_sem.at[1]),
    ]
    for load in loads:
        load.start()
    gather = Gather(n, lambda slot: gf_all.at[rows_at(slot, tokens)], ag_send, ag_recv)
    keep = pltpu.make_async_copy(cot_ref, gf_all.at[rows_at(z, tokens)], own_sem)
    keep.start()
    loads[0].wait()
    group_width = (REPEAT + 2) * LANES

    def project(slot):
        rows = rows_at(slot, tokens)
        cosine, low, high = cos_ref[rows, :], low_ref[rows, :], high_ref[rows, :]

        def turn(values):
            return (
                values * cosine
                + pltpu.roll(values, LANES - half_head, 1) * low
                + pltpu.roll(values, half_head, 1) * high
            ).astype(BF)

        for group in range(kv_local):
            joined = nn(g1[rows, :], wqkv[:, group * group_width : (group + 1) * group_width])
            for member in range(REPEAT):
                q_ref[group * REPEAT + member, rows, :] = turn(
                    joined[:, member * LANES : (member + 1) * LANES]
                )
            k_ref[group, rows, :] = turn(joined[:, REPEAT * LANES : (REPEAT + 1) * LANES])
            values = joined[:, (REPEAT + 1) * LANES :]
            v_ref[group, rows, :] = values.astype(BF)

    def project_of(index, carry):
        came, near = (index + 1) // 2, (index + 1) % 2
        slot = z - (1 - 2 * near) * came

        @pl.when(came > 1)
        def _():
            spread.arrive(came, near, came < n - 1)

        @pl.when(index == 2 * (n - 2))
        def _():
            gather.begin(cot_ref)

        for stage in range(min(2, dp_bits)):

            @pl.when(index == 3 + 2 * stage)
            def _(stage=stage):
                for shard in late:
                    shard.advance(stage)

        @pl.when((slot >= 0) & (slot < n))
        def _():
            project(slot)

        return carry

    lax.fori_loop(0, 2 * n - 1, project_of, 0)
    outs = [
        pltpu.make_async_copy(source, target, out_sem.at[k])
        for k, (source, target) in enumerate(
            [
                (q_ref, q_hbm),
                (k_ref, k_hbm),
                (v_ref, v_hbm),
                (cos_ref, cos_hbm),
                (low_ref, low_hbm),
                (high_ref, high_hbm),
                (g1, g1_hbm),
                (o_ref, o_hbm),
            ]
        )
    ]
    for out in outs[:-1]:
        out.start()
    for group in range(kv_local):
        v_t[group] = v_ref[group].astype(F32).T.astype(BF)
    loads[1].wait()
    scatter = Scatter(n, sums, rs_send, rs_recv)
    log2_scale = HEAD_WIDTH ** (-0.5) * 1.4426950408889634

    def attend(target):
        rows = rows_at(target, tokens)
        for first in range(0, tokens, LANES):
            lanes = slice(first, first + LANES)
            seen = (key_seg[...] == 0.0) | (
                key_seg[...] == seg_ref[target, :, lanes].astype(F32)
            )
            seen = seen & (key_pos[...] <= pos_ref[target, :, lanes].astype(F32))
            bias[:, lanes] = jnp.where(seen, 0.0, -1e30)

        def one_head(head, carry):
            group = head // REPEAT
            scores = nt(k_ref[group], q_ref[head, rows, :]) * log2_scale + bias[...]
            top = jnp.max(scores, axis=0, keepdims=True)
            weights = jnp.exp2(scores - top)
            total = jnp.sum(weights, axis=0, keepdims=True)
            prob[head] = (weights * (1.0 / total)).astype(BF)
            mixed = nn(v_t[group], prob[head])
            o_ref[rows, rows_at(head, LANES)] = mixed.T.astype(BF)
            return carry

        lax.fori_loop(0, heads, one_head, 0)
        out = pltpu.make_async_copy(prob, prob_hbm.at[target], prob_sem)
        out.start()
        for first in range(0, width, 512):
            part[:, first : first + 512] = nt(o_ref[rows, :], wout[first : first + 512, :])
        out.wait()

    def turn_of(index, carry):
        step, side = index // 2 + 1, index % 2
        target, valid = scatter.turn(step, side)

        @pl.when(valid)
        def _():
            attend(target)

            @pl.when(step < n)
            def _():
                scatter.push(step, side, part)

        for stage in range(2, dp_bits):

            @pl.when(index == 2 * (stage - 2) + 1)
            def _(stage=stage):
                for shard in late:
                    shard.advance(stage)

        @pl.when(step < n)
        def _():
            gather.arrive(step, side, step < n - 1)

        return carry

    lax.fori_loop(0, 2 * (n - 1) + 1, turn_of, 0)
    outs[-1].start()
    stat_ref[...] = jnp.zeros_like(stat_ref)

    def finish(rows):
        branch = part[rows, :]
        middle = x_ref[rows, :] + branch
        m_ref[rows, :] = middle
        n2_ref[rows, :] = norm_rows(middle, gain_two)[0].astype(BF)
        stat_ref[0:1, :] += jnp.sum(middle * middle, axis=0, keepdims=True)
        stat_ref[1:2, :] += jnp.sum(branch * branch, axis=0, keepdims=True)

    def piece_out(piece):
        size = tokens // PIECES
        rows = pl.ds(piece * size, size)
        return [
            pltpu.make_async_copy(source.at[rows], target.at[rows], piece_sem.at[k, piece])
            for k, (source, target) in enumerate([(n2_ref, n2_hbm), (m_ref, m_hbm)])
        ]

    def settled(piece, first, rows):
        by_rows(rows, finish, first)
        for out in piece_out(piece):
            out.start()

    scatter.settle(part, settled)
    for piece in range(PIECES):
        for out in piece_out(piece):
            out.wait()
    keep.wait()
    for out in outs:
        out.wait()
    spread.drain()
    gather.drain(cot_ref)
    scatter.drain()
    for shard in early:
        shard.drain(own=False)
    for shard in late:
        shard.drain()


def forward(n, dp, kv_local, x, gains, w_qkv, w_gate_up, w_out, w_down, cot, seg, pos, freq):
    tokens, width = x.shape
    group_len = n * tokens
    heads = REPEAT * kv_local
    owned = w_qkv.shape[1]
    ff = w_down.shape[2]
    lanes, out_lanes = (REPEAT + 2) * kv_local * LANES, heads * LANES
    vmem = pl.BlockSpec(memory_space=pltpu.VMEM)
    hbm = pl.BlockSpec(memory_space=pl.ANY)
    kept = [
        ((heads, group_len, LANES), BF),
        ((kv_local, group_len, LANES), BF),
        ((kv_local, group_len, LANES), BF),
        ((group_len, out_lanes), BF),
        ((group_len, LANES), F32),
        ((group_len, LANES), F32),
        ((group_len, LANES), F32),
    ]
    flops = 2 * group_len * (
        width * lanes + width * out_lanes + 2 * heads * group_len * LANES
    )
    return pl.pallas_call(
        functools.partial(forward_kernel, n, dp, kv_local),
        out_shape=(
            jax.ShapeDtypeStruct((width, lanes), BF),
            jax.ShapeDtypeStruct((width, out_lanes), BF),
            jax.ShapeDtypeStruct((width, 2 * ff), BF),
            jax.ShapeDtypeStruct((width, ff), BF),
            jax.ShapeDtypeStruct((group_len, width), BF),
            *[jax.ShapeDtypeStruct(shape, kind) for shape, kind in kept],
            jax.ShapeDtypeStruct((n, heads, group_len, tokens), BF),
            jax.ShapeDtypeStruct((group_len, width), BF),
            jax.ShapeDtypeStruct((tokens, width), F32),
            jax.ShapeDtypeStruct((tokens, width), BF),
            jax.ShapeDtypeStruct((8, width), F32),
        ),
        in_specs=[vmem] * 10,
        out_specs=(hbm,) * 16 + (vmem,),
        scratch_shapes=[
            pltpu.VMEM((tokens, width), F32),
            pltpu.VMEM((tokens, width), BF),
            pltpu.VMEM((group_len, width), BF),
            pltpu.VMEM((width, lanes), BF),
            pltpu.VMEM((width, out_lanes), BF),
            pltpu.VMEM((owned, lanes), BF),
            pltpu.VMEM((owned, out_lanes), BF),
            pltpu.VMEM((owned, 2 * ff), BF),
            *[pltpu.VMEM(shape, kind) for shape, kind in kept],
            pltpu.VMEM((kv_local, LANES, group_len), BF),
            pltpu.VMEM((group_len, LANES), F32),
            pltpu.VMEM((group_len, LANES), F32),
            pltpu.VMEM((group_len, tokens), F32),
            pltpu.VMEM((heads, group_len, tokens), BF),
            pltpu.VMEM((tokens, width), F32),
            pltpu.VMEM((2, n, tokens, width), BF),
            pltpu.SemaphoreType.DMA((2,)),
            pltpu.SemaphoreType.DMA((8,)),
            pltpu.SemaphoreType.DMA((2, PIECES)),
            pltpu.SemaphoreType.DMA,
            pltpu.SemaphoreType.DMA,
            *[pltpu.SemaphoreType.DMA((2, n, PIECES))] * 6,
            pltpu.SemaphoreType.DMA((4,)),
            pltpu.SemaphoreType.DMA((4, 2, dp)),
            pltpu.SemaphoreType.DMA((4, 2, dp)),
        ],
        compiler_params=pltpu.CompilerParams(
            collective_id=1, has_side_effects=True, vmem_limit_bytes=VMEM_LIMIT
        ),
        cost_estimate=pl.CostEstimate(
            flops=flops, bytes_accessed=200 * tokens * width * 2, transcendentals=0
        ),
        name="attend_forward",
    )(x, gains, w_qkv, w_gate_up, w_out, w_down, cot, seg, pos, freq)


def feed_kernel(
    n,
    chunks,
    n2_hbm,
    gf_hbm,
    wgu_hbm,
    wd_hbm,
    m_hbm,
    gain_ref,
    cot_hbm,
    z_hbm,
    dm_ref,
    ga_ref,
    dgain_ref,
    dwgu_hbm,
    m_ref,
    cot_ref,
    dwgu_ref,
    n2_all,
    gf_all,
    z_all,
    dgu,
    wgu,
    wd,
    part,
    dn2,
    sums,
    load_sem,
    n2_sem,
    gf_sem,
    z_sem,
    dw_sem,
    ag_send,
    ag_recv,
    rs_send,
    rs_recv,
):
    z = lax.axis_index("tensor")
    greet(n)
    tokens, width = n2_hbm.shape
    ff = wd_hbm.shape[1]
    piece = tokens // chunks
    rows_chunk = n * piece
    load_gu = pltpu.make_async_copy(wgu_hbm, wgu, load_sem.at[0])
    load_d = pltpu.make_async_copy(wd_hbm, wd, load_sem.at[1])

    def load_gf(chunk, slot):
        return pltpu.make_async_copy(
            gf_hbm.at[pl.ds(pl.multiple_of(slot * tokens + chunk * piece, piece), piece)],
            gf_all.at[pl.ds(pl.multiple_of(chunk * rows_chunk + slot * piece, piece), piece)],
            gf_sem.at[chunk, slot],
        )


    def load_n2(chunk):
        return pltpu.make_async_copy(
            n2_hbm.at[chunk * piece : (chunk + 1) * piece],
            n2_all.at[pl.ds(pl.multiple_of(chunk * rows_chunk + z * piece, piece), piece)],
            n2_sem.at[chunk],
        )

    for chunk in range(chunks):
        load_n2(chunk).start()
    load_gu.start()
    load_d.start()
    for chunk in range(chunks):
        for slot in range(n):
            load_gf(chunk, slot).start()
    load_m = pltpu.make_async_copy(m_hbm, m_ref, load_sem.at[2])
    load_cot = pltpu.make_async_copy(cot_hbm, cot_ref, load_sem.at[3])
    load_m.start()
    load_cot.start()
    greeted(n)
    for chunk in range(chunks):
        load_n2(chunk).wait()

    def gather_of(chunk):
        return Gather(
            n,
            lambda slot: n2_all.at[
                pl.ds(pl.multiple_of(chunk * rows_chunk + slot * piece, piece), piece)
            ],
            ag_send.at[chunk],
            ag_recv.at[chunk],
        )

    def scatter_of(chunk):
        return Scatter(n, sums.at[chunk], rs_send.at[chunk], rs_recv.at[chunk])

    gather_of(0).begin_where(True)
    if chunks > 1:
        gather_of(1).begin_where(True)
    for chunk in range(chunks):
        gather_of(chunk).begin_where(False)

    def scatter_end(chunk):
        own = dn2.at[rows_at(chunk, piece)]
        own[...] = part[chunk, rows_at(z, piece), :]
        scatter_of(chunk).settle(own)

    block = 256
    hidden_blocks = ff // block
    out_blocks = width // 512

    def hidden_block(chunk, index):
        rows = rows_at(chunk, rows_chunk)
        cols = rows_at(index, block)
        up_cols = pl.ds(pl.multiple_of(ff + index * block, block), block)
        gate = nn(n2_all[rows, :], wgu[:, cols])
        up = nn(n2_all[rows, :], wgu[:, up_cols])
        dz = nn(gf_all[rows, :], wd[:, cols])
        s = 1.0 / (1.0 + jnp.exp(-gate))
        act = gate * s
        z_all[rows, cols] = (act * up).astype(BF)
        dgu[rows, cols] = (dz * up * (s * (1.0 + gate * (1.0 - s)))).astype(BF)
        dgu[rows, up_cols] = (dz * act).astype(BF)

    def out_block(chunk, index):
        rows = rows_at(chunk, rows_chunk)
        cols = rows_at(index, 512)
        part[chunk, :, cols] = nt(dgu[rows, :], wgu[cols, :])

    def z_out(chunk):
        rows = rows_at(chunk, rows_chunk)
        return pltpu.make_async_copy(z_all.at[rows], z_hbm.at[rows], z_sem.at[chunk])

    def compute(chunk):
        for slot in range(n):
            load_gf(chunk, slot).wait()

        def hidden(index, carry):
            hidden_block(chunk, index)
            return carry

        def out(index, carry):
            out_block(chunk, index)
            return carry

        lax.fori_loop(0, hidden_blocks, hidden, 0)
        lax.fori_loop(0, out_blocks, out, 0)
        z_out(chunk).start()

    def grad_gu(index, carry):
        cols = rows_at(index, 256)
        dwgu_ref[:, cols] = tn(n2_all[...], dgu[:, cols]).astype(BF)
        dw_out(index).start()
        return carry

    def dw_out(index):
        cols = rows_at(index, 256)
        return pltpu.make_async_copy(dwgu_ref.at[:, cols], dwgu_hbm.at[:, cols], dw_sem.at[index])

    blocks = 2 * ff // 256

    def within(chunk):
        return (chunk >= 0) & (chunk < chunks)

    def stage(index, carry):
        for step in range(n - 1, 0, -1):
            chunk = index - (step - 1)

            @pl.when(within(chunk))
            def _(step=step, chunk=chunk):
                for side in range(2):
                    gather_of(chunk).arrive(step, side, step < n - 1)

        @pl.when(index + 2 < chunks)
        def _():
            gather_of(index + 2).begin_where(True)

        ready = index - (n - 2)

        def push(chunk, step, starts):
            scatter = scatter_of(chunk)
            for side in range(2):
                target, valid = scatter.turn(step, side)
                other = scatter.has_source(side)

                @pl.when(valid & (jnp.logical_not(other) if starts else other))
                def _(side=side, target=target):
                    scatter.push(step, side, part.at[chunk], target * piece)

        @pl.when(ready == 0)
        def _():
            load_gu.wait()
            load_d.wait()

        @pl.when(within(ready))
        def _():
            compute(ready)
            for step in range(1, n):
                push(ready, step, True)

        for step in range(n - 1, 1, -1):
            chunk = ready - LAG * (step - 1)

            @pl.when(within(chunk))
            def _(step=step, chunk=chunk):
                push(chunk, step, False)

        @pl.when(within(ready - LAG * (n - 1)))
        def _():
            scatter_end(ready - LAG * (n - 1))

        late, turns = ready - chunks, LAG * (n - 1)

        @pl.when((late >= 0) & (late < turns))
        def _():
            lax.fori_loop(blocks * late // turns, blocks * (late + 1) // turns, grad_gu, 0)

        return carry

    lax.fori_loop(0, chunks + n - 2 + LAG * (n - 1), stage, 0)
    load_m.wait()
    load_cot.wait()
    gain = gain_ref[0, 1:2, :]
    dgain_ref[...] = jnp.zeros_like(dgain_ref)

    def finish(rows):
        middle = m_ref[rows, :]
        dn = dn2[rows, :]
        inverse = lax.rsqrt(jnp.mean(middle * middle, axis=-1, keepdims=True) + norm_eps)
        scaled = dn * gain
        dgain_ref[0:1, :] += jnp.sum(dn * middle * inverse, axis=0, keepdims=True)
        dm = (
            inverse * scaled
            - middle * inverse**3 * jnp.mean(scaled * middle, axis=-1, keepdims=True)
            + cot_ref[rows, :].astype(F32)
        )
        dm_ref[rows, :] = dm
        ga_ref[rows, :] = dm.astype(BF)

    by_rows(tokens, finish)
    for index in range(blocks):
        dw_out(index).wait()
    for chunk in range(chunks):
        z_out(chunk).wait()
        gather_of(chunk).drain()
        scatter_of(chunk).drain()


def feed(n, chunks, n2, gf_all, wgu, wd, m, gain, cot):
    tokens, width = n2.shape
    group_len = n * tokens
    ff = wd.shape[1]
    vmem = pl.BlockSpec(memory_space=pltpu.VMEM)
    hbm = pl.BlockSpec(memory_space=pl.ANY)
    return pl.pallas_call(
        functools.partial(feed_kernel, n, chunks),
        out_shape=(
            jax.ShapeDtypeStruct((group_len, ff), BF),
            jax.ShapeDtypeStruct((tokens, width), F32),
            jax.ShapeDtypeStruct((tokens, width), BF),
            jax.ShapeDtypeStruct((8, width), F32),
            jax.ShapeDtypeStruct((width, 2 * ff), BF),
        ),
        in_specs=[hbm] * 5 + [vmem, hbm],
        out_specs=(hbm, vmem, vmem, vmem, hbm),
        scratch_shapes=[
            pltpu.VMEM((tokens, width), F32),
            pltpu.VMEM((tokens, width), BF),
            pltpu.VMEM((width, 2 * ff), BF),
            pltpu.VMEM((group_len, width), BF),
            pltpu.VMEM((group_len, width), BF),
            pltpu.VMEM((group_len, ff), BF),
            pltpu.VMEM((group_len, 2 * ff), BF),
            pltpu.VMEM((width, 2 * ff), BF),
            pltpu.VMEM((width, ff), BF),
            pltpu.VMEM((chunks, group_len // chunks, width), F32),
            pltpu.VMEM((tokens, width), F32),
            pltpu.VMEM((chunks, 2, n, tokens // chunks, width), BF),
            pltpu.SemaphoreType.DMA((4,)),
            pltpu.SemaphoreType.DMA((chunks,)),
            pltpu.SemaphoreType.DMA((chunks, n)),
            pltpu.SemaphoreType.DMA((chunks,)),
            pltpu.SemaphoreType.DMA((2 * ff // 256,)),
            pltpu.SemaphoreType.DMA((chunks, 2, n, 1)),
            pltpu.SemaphoreType.DMA((chunks, 2, n, 1)),
            pltpu.SemaphoreType.DMA((chunks, 2, n, 1)),
            pltpu.SemaphoreType.DMA((chunks, 2, n, 1)),
        ],
        compiler_params=pltpu.CompilerParams(
            collective_id=3, has_side_effects=True, vmem_limit_bytes=VMEM_LIMIT
        ),
        cost_estimate=pl.CostEstimate(
            flops=18 * group_len * width * ff, bytes_accessed=250 * tokens * width * 2, transcendentals=0
        ),
        name="feed_both",
    )(n2, gf_all, wgu, wd, m, gain, cot)


def attend_back_kernel(
    n,
    dp,
    kv_local,
    chunks,
    ga_hbm,
    wout_hbm,
    wd_hbm,
    z_hbm,
    prob_hbm,
    gf_hbm,
    dwgu_hbm,
    m_hbm,
    q_hbm,
    k_hbm,
    v_hbm,
    o_hbm,
    cos_hbm,
    low_hbm,
    high_hbm,
    out_hbm,
    stat_ref,
    dqkv_hbm,
    dwd_hbm,
    ga_out,
    grad_gu_hbm,
    out_ref,
    m_ref,
    q_ref,
    k_ref,
    v_ref,
    o_ref,
    cos_ref,
    sin_low_ref,
    sin_high_ref,
    dqkv_ref,
    dwd_ref,
    grad_gu_ref,
    keep,
    held,
    ga_all,
    gf,
    wout,
    wd,
    z_all,
    k_t,
    prob,
    d_out,
    dk,
    dv,
    part,
    sums,
    load_sem,
    gf_sem,
    prob_sem,
    out_sem,
    piece_sem,
    ag_send,
    ag_recv,
    rs_send,
    rs_recv,
    keep_sem,
    dp_send,
    dp_recv,
):
    z = lax.axis_index("tensor")
    me = lax.axis_index("dp")
    dp_bits = dp.bit_length() - 1
    others = [{"dp": across(me, bit)} for bit in range(dp_bits)]
    greet(n, others)
    tokens, width = ga_hbm.shape
    heads = REPEAT * kv_local
    group_len = n * tokens
    piece = tokens // chunks
    scale = HEAD_WIDTH ** (-0.5)
    loads = [
        pltpu.make_async_copy(source, target, load_sem.at[index])
        for index, (source, target) in enumerate(
            [
                (ga_hbm, ga_all.at[rows_at(z, tokens)]),
                (wout_hbm, wout),
                (k_hbm, k_ref),
                (v_hbm, v_ref),
                (q_hbm, q_ref),
                (o_hbm, o_ref),
                (cos_hbm, cos_ref),
                (low_hbm, sin_low_ref),
                (high_hbm, sin_high_ref),
                (z_hbm, z_all),
                (wd_hbm, wd),
                (m_hbm, m_ref),
            ]
        )
    ]
    for load in loads:
        load.start()

    def load_gf(chunk, slot):
        return pltpu.make_async_copy(
            gf_hbm.at[pl.ds(pl.multiple_of(slot * tokens + chunk * piece, piece), piece)],
            gf.at[pl.ds(pl.multiple_of((chunk * n + slot) * piece, piece), piece)],
            gf_sem.at[chunk, slot],
        )

    for chunk in range(chunks):
        for slot in range(n):
            load_gf(chunk, slot).start()

    def load_prob(slot):
        return pltpu.make_async_copy(prob_hbm.at[slot], prob, prob_sem)

    greeted(n, others)
    gather = Gather(n, lambda slot: ga_all.at[rows_at(slot, tokens)], ag_send, ag_recv)
    loads[0].wait()
    gather.begin()
    halving = Halving(
        dp, grad_gu_ref.shape[0], dwgu_hbm, keep, held, keep_sem, dp_send, dp_recv
    )
    halving.begin()
    scatter = Scatter(n, sums, rs_send, rs_recv)
    for load in loads[1:-1]:
        load.wait()
    for group in range(kv_local):
        k_t[group] = k_ref[group].astype(F32).T.astype(BF)
    dk[...] = jnp.zeros_like(dk)
    dv[...] = jnp.zeros_like(dv)
    group_lanes = (REPEAT + 2) * LANES

    def turn_back(values, rows):
        return (
            values * cos_ref[rows, :]
            - pltpu.roll(values, LANES - HEAD_WIDTH // 2, 1) * sin_low_ref[rows, :]
            - pltpu.roll(values, HEAD_WIDTH // 2, 1) * sin_high_ref[rows, :]
        )

    def back(slot):
        rows = rows_at(slot, tokens)
        d_o = nn(ga_all[rows, :], wout[...])
        d_out[...] = d_o.astype(BF)

        def one_head(head, carry):
            group = head // REPEAT
            lanes = rows_at(head, LANES)
            do_h = d_out[:, lanes]
            both = do_h.astype(F32) * o_ref[rows, lanes].astype(F32)
            delta = jnp.sum(both.T, axis=0, keepdims=True)
            dprob = nt(v_ref[group], do_h)
            weights = prob[head]
            ds = (weights.astype(F32) * (dprob - delta)).astype(BF)
            dv[group] += nn(weights, do_h)
            dk[group] += nn(ds, q_ref[head, rows, :])
            dq = nn(k_t[group], ds).T * scale
            first = group * (REPEAT + 2) + head % REPEAT
            dqkv_ref[rows, rows_at(first, LANES)] = turn_back(dq, rows).astype(BF)
            return carry

        lax.fori_loop(0, heads, one_head, 0)

    def feed_rows(target):
        pieces = [
            z_all[
                pl.ds(
                    pl.multiple_of(chunk * n * piece + target * piece, piece), piece
                ),
                :,
            ]
            for chunk in range(chunks)
        ]
        rows = jnp.concatenate(pieces, axis=0) if chunks > 1 else pieces[0]
        for first in range(0, width, 512):
            part[:, first : first + 512] = nt(rows, wd[first : first + 512, :])

    def turn_of(index, carry):
        came, near = (index + 1) // 2, (index + 1) % 2
        slot = z - (1 - 2 * near) * came
        valid = (slot >= 0) & (slot < n)

        @pl.when(valid)
        def _():
            load_prob(slot).start()

        @pl.when(index > 0)
        def _():
            gather.arrive(came, near, came < n - 1)

        step, side = index // 2 + 1, index % 2
        target, sends = scatter.turn(step, side)

        @pl.when(sends & (step < n))
        def _():
            feed_rows(target)
            scatter.push(step, side, part)

        @pl.when(valid)
        def _():
            load_prob(slot).wait()
            back(slot)

        return carry

    for chunk in range(chunks):
        for slot in range(n):
            load_gf(chunk, slot).wait()
    ff = wd_hbm.shape[1]
    down_blocks = ff // 256

    def grad_down(first, last):
        def body(index, carry):
            cols = rows_at(index, 256)
            dwd_ref[:, cols] = tn(gf[...], z_all[:, cols]).astype(BF)
            return carry

        lax.fori_loop(first, last, body, 0)

    turns = 2 * n - 1

    def turn_and_grad(index, carry):
        turn_of(index, 0)
        grad_down(down_blocks * index // turns, down_blocks * (index + 1) // turns)
        for stage in range(dp_bits):

            @pl.when(index == 2 * stage + 1)
            def _(stage=stage):
                halving.advance(stage)

        return carry

    lax.fori_loop(0, turns, turn_and_grad, 0)

    def finish_keys(slot, carry):
        rows = rows_at(slot, tokens)
        for group in range(kv_local):
            first = group * group_lanes + REPEAT * LANES
            dqkv_ref[rows, first : first + LANES] = turn_back(
                dk[group, rows, :] * scale, rows
            ).astype(BF)
            dqkv_ref[rows, first + LANES : first + 2 * LANES] = dv[group, rows, :].astype(BF)
        return carry

    lax.fori_loop(0, n, finish_keys, 0)
    outs = [
        pltpu.make_async_copy(source, target, out_sem.at[index])
        for index, (source, target) in enumerate(
            [(dqkv_ref, dqkv_hbm), (dwd_ref, dwd_hbm), (ga_all, ga_out), (grad_gu_ref, grad_gu_hbm)]
        )
    ]
    for out in outs[:3]:
        out.start()
    for half in range(2):
        grad_gu_ref[:, half, :] = halving.result(half)
    outs[3].start()
    feed_rows(z)
    loads[-1].wait()
    stat_ref[...] = jnp.zeros_like(stat_ref)

    def finish(rows):
        branch = part[rows, :]
        result = m_ref[rows, :] + branch
        out_ref[rows, :] = result
        stat_ref[0:1, :] += jnp.sum(result * result, axis=0, keepdims=True)
        stat_ref[1:2, :] += jnp.sum(branch * branch, axis=0, keepdims=True)

    def piece_out(piece):
        size = tokens // PIECES
        rows = pl.ds(piece * size, size)
        return pltpu.make_async_copy(out_ref.at[rows], out_hbm.at[rows], piece_sem.at[piece])

    def settled(piece, first, rows):
        by_rows(rows, finish, first)
        piece_out(piece).start()

    scatter.settle(part, settled)
    for piece in range(PIECES):
        piece_out(piece).wait()
    for out in outs:
        out.wait()
    gather.drain()
    scatter.drain()
    halving.drain()


def attend_back(n, dp, kv_local, chunks, ga, wout, wd, z_all, prob, gf, dwgu, m, q, k, v, o, tables):
    tokens, width = ga.shape
    group_len = n * tokens
    heads = REPEAT * kv_local
    ff = wd.shape[1]
    owned = width // dp
    lanes = (REPEAT + 2) * kv_local * LANES
    vmem = pl.BlockSpec(memory_space=pltpu.VMEM)
    hbm = pl.BlockSpec(memory_space=pl.ANY)
    return pl.pallas_call(
        functools.partial(attend_back_kernel, n, dp, kv_local, chunks),
        out_shape=(
            jax.ShapeDtypeStruct((tokens, width), F32),
            jax.ShapeDtypeStruct((8, width), F32),
            jax.ShapeDtypeStruct((group_len, lanes), BF),
            jax.ShapeDtypeStruct((width, ff), BF),
            jax.ShapeDtypeStruct((group_len, width), BF),
            jax.ShapeDtypeStruct((owned, 2, ff), F32),
        ),
        in_specs=[hbm] * 15,
        out_specs=(hbm, vmem, hbm, hbm, hbm, hbm),
        scratch_shapes=[
            pltpu.VMEM((tokens, width), F32),
            pltpu.VMEM((tokens, width), F32),
            pltpu.VMEM(q.shape, BF),
            pltpu.VMEM(k.shape, BF),
            pltpu.VMEM(v.shape, BF),
            pltpu.VMEM(o.shape, BF),
            *[pltpu.VMEM((group_len, LANES), F32)] * 3,
            pltpu.VMEM((group_len, lanes), BF),
            pltpu.VMEM((width, ff), BF),
            pltpu.VMEM((owned, 2, ff), F32),
            pltpu.VMEM((2, dp // 2, owned, ff), BF),
            pltpu.VMEM((2, dp - 1, owned, ff), BF),
            pltpu.VMEM((group_len, width), BF),
            pltpu.VMEM((group_len, width), BF),
            pltpu.VMEM(wout.shape, BF),
            pltpu.VMEM(wd.shape, BF),
            pltpu.VMEM((group_len, ff), BF),
            pltpu.VMEM((kv_local, LANES, group_len), BF),
            pltpu.VMEM((heads, group_len, tokens), BF),
            pltpu.VMEM((tokens, heads * LANES), BF),
            pltpu.VMEM((kv_local, group_len, LANES), F32),
            pltpu.VMEM((kv_local, group_len, LANES), F32),
            pltpu.VMEM((tokens, width), F32),
            pltpu.VMEM((2, n, tokens, width), BF),
            pltpu.SemaphoreType.DMA((12,)),
            pltpu.SemaphoreType.DMA((chunks, n)),
            pltpu.SemaphoreType.DMA,
            pltpu.SemaphoreType.DMA((4,)),
            pltpu.SemaphoreType.DMA((PIECES,)),
            pltpu.SemaphoreType.DMA((2, n, PIECES)),
            pltpu.SemaphoreType.DMA((2, n, PIECES)),
            pltpu.SemaphoreType.DMA((2, n, PIECES)),
            pltpu.SemaphoreType.DMA((2, n, PIECES)),
            pltpu.SemaphoreType.DMA((2, dp // 2)),
            pltpu.SemaphoreType.DMA((2, dp)),
            pltpu.SemaphoreType.DMA((2, dp)),
        ],
        compiler_params=pltpu.CompilerParams(
            collective_id=4, has_side_effects=True, vmem_limit_bytes=VMEM_LIMIT
        ),
        cost_estimate=pl.CostEstimate(
            flops=8 * group_len * width * ff, bytes_accessed=200 * tokens * width * 2, transcendentals=0
        ),
        name="attend_backward",
    )(ga, wout, wd, z_all, prob, gf, dwgu, m, q, k, v, o, *tables)


class Sharing:
    def __init__(self, axis, size, source, slots, send_sem, recv_sem):
        self.axis, self.size, self.source, self.slots = axis, size, source, slots
        self.send_sem, self.recv_sem = send_sem, recv_sem
        self.me = lax.axis_index(axis)

    def copy(self, offset):
        return pltpu.make_async_remote_copy(
            src_ref=self.source,
            dst_ref=self.slots.at[self.me],
            send_sem=self.send_sem.at[offset],
            recv_sem=self.recv_sem.at[offset],
            device_id={self.axis: (self.me + offset) % self.size},
            device_id_type=MESH,
        )

    def arrival(self, offset):
        place = self.slots.at[(self.me + self.size - offset) % self.size]
        return pltpu.make_async_remote_copy(
            src_ref=place,
            dst_ref=place,
            send_sem=self.send_sem.at[offset],
            recv_sem=self.recv_sem.at[offset],
            device_id={self.axis: (self.me + self.size - offset) % self.size},
            device_id_type=MESH,
        )

    def begin(self):
        for offset in range(1, self.size):
            self.copy(offset).start()
        self.slots[self.me] = self.source[...]

    def total(self):
        for offset in range(1, self.size):
            self.arrival(offset).wait_recv()
        total = self.slots[0]
        for index in range(1, self.size):
            total = total + self.slots[index]
        return total

    def drain(self):
        for offset in range(1, self.size):
            self.copy(offset).wait_send()


def last_kernel(
    n,
    dp,
    cells,
    out_heads,
    dqkv_hbm,
    wqkv_hbm,
    x_hbm,
    dm_hbm,
    gain_ref,
    dgain_two_ref,
    stat_one_ref,
    stat_two_ref,
    g1_hbm,
    ga_hbm,
    o_hbm,
    dwd_hbm,
    dx_hbm,
    gains_ref,
    rms_ref,
    grad_out_ref,
    grad_qkv_ref,
    grad_down_ref,
    dx_ref,
    dqkv,
    wqkv,
    x,
    dm,
    g1,
    ga,
    o,
    dw,
    part,
    sums,
    down_keep,
    down_held,
    head_keep,
    head_held,
    vector,
    packed,
    group_sum,
    dp_slots,
    z_slots,
    load_sem,
    piece_sem,
    rs_send,
    rs_recv,
    down_keep_sem,
    down_send,
    down_recv,
    head_keep_sem,
    head_send,
    head_recv,
    dp_slot_send,
    dp_slot_recv,
    z_slot_send,
    z_slot_recv,
):
    z = lax.axis_index("tensor")
    me = lax.axis_index("dp")
    tokens, width = x.shape
    dp_bits = dp.bit_length() - 1
    others = [{"dp": (me + offset) % dp} for offset in range(1, dp)]
    others += [{"tensor": (z + offset) % n} for offset in range(1, n)]
    barrier = pltpu.get_barrier_semaphore()
    for other in others:
        pl.semaphore_signal(barrier, inc=1, device_id=other, device_id_type=MESH)
    owned = grad_out_ref.shape[0]
    loads = [
        pltpu.make_async_copy(source, target, load_sem.at[index])
        for index, (source, target) in enumerate(
            [
                (wqkv_hbm, wqkv),
                (dqkv_hbm, dqkv),
                (g1_hbm, g1),
                (ga_hbm, ga),
                (o_hbm, o),
                (x_hbm, x),
                (dm_hbm, dm),
            ]
        )
    ]
    for load in loads:
        load.start()
    pl.semaphore_wait(barrier, len(others))
    down = Halving(dp, owned, dwd_hbm, down_keep, down_held, down_keep_sem, down_send, down_recv)
    down.begin()
    halving = Halving(dp, owned, dw, head_keep, head_held, head_keep_sem, head_send, head_recv)
    scatter = Scatter(n, sums, rs_send, rs_recv)
    gain = gain_ref[0, 0:1, :]
    vector[...] = jnp.zeros_like(vector)
    vector[1:2, :] = dgain_two_ref[0:1, :]
    vector[2:3, :] = stat_one_ref[0:1, :]
    vector[3:4, :] = stat_two_ref[0:1, :]
    vector[4:5, :] = stat_one_ref[1:2, :]
    vector[5:6, :] = stat_two_ref[1:2, :]
    for load in loads[:3]:
        load.wait()
    out_lanes = o.shape[1]

    def grad_qkv(index, carry):
        place = pl.ds(pl.multiple_of(out_lanes + index * 256, 256), 256)
        dw[:, place] = tn(g1[...], dqkv[:, rows_at(index, 256)]).astype(BF)
        return carry

    def grad_out(index, carry):
        cols = rows_at(index, 256)
        dw[:, cols] = tn(ga[...], o[:, cols]).astype(BF)
        return carry

    def compute(index, carry):
        step, side = index // 2 + 1, index % 2
        target, due = scatter.turn(step, side)

        @pl.when(due)
        def _():
            rows = rows_at(target, tokens)

            def block(number, carry):
                cols = rows_at(number, 256)
                values = nt(dqkv[rows, :], wqkv[cols, :])
                part[rows, cols] = values
                vector[0:1, cols] += jnp.sum(
                    values * g1[rows, cols].astype(F32), axis=0, keepdims=True
                )
                return carry

            lax.fori_loop(0, width // 256, block, 0)

            @pl.when((step < n - 1) & jnp.logical_not(scatter.has_source(side)))
            def _():
                scatter.push(step, side, part, target * tokens)

        return carry

    def compute_and_grads(index, carry):
        compute(index, 0)

        @pl.when(index == 1)
        def _():
            for load in loads[3:]:
                load.wait()
            lax.fori_loop(0, dqkv.shape[1] // 256, grad_qkv, 0)
            lax.fori_loop(0, out_lanes // 256, grad_out, 0)
            halving.begin()

        return carry

    lax.fori_loop(0, 2 * n - 1, compute_and_grads, 0)
    vector[0:1, :] = vector[0:1, :] / gain

    blocks = width // LANES
    packed[...] = jnp.zeros_like(packed)
    for row in range(6):
        parts = [
            vector[row : row + 1, index * LANES : (index + 1) * LANES] for index in range(blocks)
        ]
        if row < 2:
            for index, values in enumerate(parts):
                packed[row * blocks + index : row * blocks + index + 1, :] = values
        else:
            place = 2 * blocks + row - 2
            packed[place : place + 1, :] = functools.reduce(jnp.add, parts)
    near = Sharing("dp", dp, packed, dp_slots, dp_slot_send, dp_slot_recv)
    far = Sharing("tensor", n, group_sum, z_slots, z_slot_send, z_slot_recv)
    near.begin()
    down.advance(0)
    halving.advance(0)

    def push_came(step):
        for side in range(2):
            target, sends = scatter.turn(step, side)

            @pl.when(sends & scatter.has_source(side))
            def _(side=side, target=target):
                scatter.push(step, side, part, target * tokens)

    def push_last_start():
        for side in range(2):
            target, sends = scatter.turn(n - 1, side)

            @pl.when(sends & jnp.logical_not(scatter.has_source(side)))
            def _(side=side, target=target):
                scatter.push(n - 1, side, part, target * tokens)

    done = 1
    for step in range(2, n):
        push_came(step)
        if step == 2:
            group_sum[...] = near.total()
            far.begin()
            push_last_start()
        until = 1 + (dp_bits - 1) * (step - 1) // (n - 1)
        for stage in range(done, until):
            down.advance(stage)
            halving.advance(stage)
        done = until
    for stage in range(done, dp_bits):
        down.advance(stage)
        halving.advance(stage)
    for half in range(2):
        columns = down.columns(half)
        grad_down_ref[:, columns] = down.result(half)
    place = 0
    for half in range(2):
        block = halving.result(half)
        for index in range(block.shape[1] // LANES):
            values = block[:, index * LANES : index * LANES + HEAD_WIDTH]
            if place < out_heads:
                grad_out_ref[:, place * HEAD_WIDTH : (place + 1) * HEAD_WIDTH] = values
            else:
                head = place - out_heads
                grad_qkv_ref[:, head * HEAD_WIDTH : (head + 1) * HEAD_WIDTH] = values
            place += 1
    total = far.total()
    for which in range(2):
        for index in range(blocks):
            gains_ref[0, which : which + 1, index * LANES : (index + 1) * LANES] = total[
                which * blocks + index : which * blocks + index + 1, :
            ]
    squares = jnp.sqrt(jnp.sum(total, axis=1, keepdims=True) * (1.0 / cells))
    row = lax.broadcasted_iota(jnp.int32, (total.shape[0], 4), 0)
    column = lax.broadcasted_iota(jnp.int32, (total.shape[0], 4), 1)
    rms_ref[...] = jnp.sum(jnp.where(row == column + 2 * blocks, squares, 0.0), axis=0, keepdims=True)
    own = part.at[rows_at(z, tokens)]

    def finish(rows):
        values = x[rows, :]
        dn = own[rows, :]
        inverse = lax.rsqrt(jnp.mean(values * values, axis=-1, keepdims=True) + norm_eps)
        scaled = dn * gain
        dx_ref[rows, :] = (
            inverse * scaled
            - values * inverse**3 * jnp.mean(scaled * values, axis=-1, keepdims=True)
            + dm[rows, :]
        )

    def piece_out(piece):
        size = tokens // PIECES
        rows = pl.ds(piece * size, size)
        return pltpu.make_async_copy(dx_ref.at[rows], dx_hbm.at[rows], piece_sem.at[piece])

    def settled(piece, first, rows):
        by_rows(rows, finish, first)
        piece_out(piece).start()

    scatter.settle(own, settled)
    for piece in range(PIECES):
        piece_out(piece).wait()
    near.drain()
    far.drain()
    down.drain()
    halving.drain()
    scatter.drain()


def last(n, dqkv, wqkv, x, dm, gain, dgain_two, stat_one, stat_two, g1, ga, o, dwd, out_columns, qkv_columns):
    tokens, width = x.shape
    dp = lax.axis_size("dp")
    owned = width // dp
    ff = dwd.shape[1]
    columns = o.shape[1] + dqkv.shape[1]
    small = -(-(2 * width // LANES + 4) // 8) * 8
    vmem = pl.BlockSpec(memory_space=pltpu.VMEM)
    hbm = pl.BlockSpec(memory_space=pl.ANY)
    return pl.pallas_call(
        functools.partial(last_kernel, n, dp, tokens * width * dp * n, out_columns // HEAD_WIDTH),
        out_shape=(
            jax.ShapeDtypeStruct((tokens, width), F32),
            jax.ShapeDtypeStruct((1, 2, width), F32),
            jax.ShapeDtypeStruct((1, 4), F32),
            jax.ShapeDtypeStruct((owned, out_columns), F32),
            jax.ShapeDtypeStruct((owned, qkv_columns), F32),
            jax.ShapeDtypeStruct((owned, ff), F32),
        ),
        in_specs=[hbm] * 4 + [vmem] * 4 + [hbm] * 4,
        out_specs=(hbm,) + (vmem,) * 5,
        scratch_shapes=[
            pltpu.VMEM(x.shape, F32),
            pltpu.VMEM(dqkv.shape, BF),
            pltpu.VMEM(wqkv.shape, BF),
            pltpu.VMEM(x.shape, F32),
            pltpu.VMEM(dm.shape, F32),
            pltpu.VMEM(g1.shape, BF),
            pltpu.VMEM(ga.shape, BF),
            pltpu.VMEM(o.shape, BF),
            pltpu.VMEM((width, columns), BF),
            pltpu.VMEM((n * tokens, width), F32),
            pltpu.VMEM((2, n, tokens, width), BF),
            pltpu.VMEM((2, dp // 2, owned, ff // 2), BF),
            pltpu.VMEM((2, dp - 1, owned, ff // 2), BF),
            pltpu.VMEM((2, dp // 2, owned, columns // 2), BF),
            pltpu.VMEM((2, dp - 1, owned, columns // 2), BF),
            pltpu.VMEM((8, width), F32),
            pltpu.VMEM((small, LANES), F32),
            pltpu.VMEM((small, LANES), F32),
            pltpu.VMEM((dp, small, LANES), F32),
            pltpu.VMEM((n, small, LANES), F32),
            pltpu.SemaphoreType.DMA((7,)),
            pltpu.SemaphoreType.DMA((PIECES,)),
            pltpu.SemaphoreType.DMA((2, n, PIECES)),
            pltpu.SemaphoreType.DMA((2, n, PIECES)),
            *[
                pltpu.SemaphoreType.DMA((2, dp // 2)),
                pltpu.SemaphoreType.DMA((2, dp)),
                pltpu.SemaphoreType.DMA((2, dp)),
            ]
            * 2,
            pltpu.SemaphoreType.DMA((dp,)),
            pltpu.SemaphoreType.DMA((dp,)),
            pltpu.SemaphoreType.DMA((n,)),
            pltpu.SemaphoreType.DMA((n,)),
        ],
        compiler_params=pltpu.CompilerParams(
            collective_id=5, has_side_effects=True, vmem_limit_bytes=VMEM_LIMIT
        ),
        cost_estimate=pl.CostEstimate(
            flops=2 * dqkv.size * width, bytes_accessed=150 * tokens * width * 2, transcendentals=0
        ),
        name="input_gradient",
    )(dqkv, wqkv, x, dm, gain, dgain_two, stat_one, stat_two, g1, ga, o, dwd)


def deliver_kernel(*refs):
    count = len(refs) // 3
    sources, targets, held = refs[:count], refs[count : 2 * count], refs[2 * count : 3 * count]
    sem = refs[-1]
    ins = [
        pltpu.make_async_copy(source, place, sem.at[0, index])
        for index, (source, place) in enumerate(zip(sources, held, strict=True))
    ]
    outs = [
        pltpu.make_async_copy(place, target, sem.at[1, index])
        for index, (place, target) in enumerate(zip(held, targets, strict=True))
    ]
    for copy in ins:
        copy.start()
    for copy, out in zip(ins, outs, strict=True):
        copy.wait()
        out.start()
    for out in outs:
        out.wait()


def deliver(*arrays):
    hbm = pl.BlockSpec(memory_space=pl.ANY)
    return pl.pallas_call(
        deliver_kernel,
        out_shape=[jax.ShapeDtypeStruct(array.shape, array.dtype) for array in arrays],
        in_specs=[hbm] * len(arrays),
        out_specs=[hbm] * len(arrays),
        scratch_shapes=[
            *[pltpu.VMEM(array.shape, array.dtype) for array in arrays],
            pltpu.SemaphoreType.DMA((2, len(arrays))),
        ],
        compiler_params=pltpu.CompilerParams(vmem_limit_bytes=VMEM_LIMIT),
        name="deliver",
    )(*arrays)


def per_device(inputs, norm_gains, w_qkv, w_gate_up, w_out, w_down, segments, positions, cotangent):
    n, dp = lax.axis_size("tensor"), lax.axis_size("dp")
    tokens, width = inputs.shape
    kv_local = w_out.shape[2] // (REPEAT * HEAD_WIDTH)
    chunks = 8
    half = HEAD_WIDTH // 2
    freq_steps = jnp.arange(half, dtype=F32) * (2.0 / HEAD_WIDTH)
    inverse = jnp.power(rope_base, -freq_steps)
    freq = jnp.concatenate([inverse, inverse, jnp.zeros((LANES - HEAD_WIDTH,), F32)])[None]

    (
        wqkv,
        wout,
        wgu,
        wd,
        g1,
        q,
        k,
        v,
        o,
        cosine,
        low,
        high,
        prob,
        gf_all,
        m,
        n2,
        stat_one,
    ) = forward(
        n,
        dp,
        kv_local,
        inputs,
        norm_gains,
        w_qkv,
        w_gate_up,
        w_out,
        w_down,
        cotangent,
        segments.reshape(n, 1, tokens),
        positions.reshape(n, 1, tokens),
        freq,
    )
    z_all, dm, ga, dgain_two, dwgu = feed(n, chunks, n2, gf_all, wgu, wd, m, norm_gains, cotangent)
    output, stat_two, dqkv, dwd, ga_all, grad_gu = attend_back(
        n,
        dp,
        kv_local,
        chunks,
        ga,
        wout,
        wd,
        z_all,
        prob,
        gf_all,
        dwgu,
        m,
        q,
        k,
        v,
        o,
        (cosine, low, high),
    )
    input_grad, gain_total, rms, grad_out, grad_qkv, grad_down = last(
        n,
        dqkv,
        wqkv,
        inputs,
        dm,
        norm_gains,
        dgain_two,
        stat_one,
        stat_two,
        g1,
        ga_all,
        o,
        dwd,
        w_out.shape[2],
        w_qkv.shape[2],
    )
    output, input_grad, grad_qkv, grad_gu, grad_out, grad_down, gain_total, rms = deliver(
        output, input_grad, grad_qkv, grad_gu, grad_out, grad_down, gain_total, rms
    )
    return (
        output,
        input_grad,
        grad_qkv[None],
        grad_gu[None],
        grad_out[None],
        grad_down[None],
        gain_total,
        rms,
    )


def solution(mesh):
    rows = P(("dp", "tensor"), None)
    weights = P(None, "dp", "tensor")
    pairs = P(None, "dp", None, "tensor")
    return jax.shard_map(
        per_device,
        mesh=mesh,
        in_specs=(rows, P(), weights, pairs, weights, weights, P("dp"), P("dp"), rows),
        out_specs=(rows, rows, weights, pairs, weights, weights, P(), P()),
        check_vma=False,
    )
```

```python
import functools

import jax
import jax.numpy as jnp
from jax import lax
from jax.experimental import pallas as pl
from jax.experimental.pallas import tpu as pltpu
from jax.sharding import PartitionSpec as P

HEADS = 16
KV_HEADS = 8
HEAD_WIDTH = 96
REPEAT = HEADS // KV_HEADS
LANES = 128

norm_eps = 1e-05
rope_base = 100000.0
MESH = pl.DeviceIdType.MESH
BF = jnp.bfloat16
F32 = jnp.float32
VMEM_LIMIT = 60 * 2**20
PIECES = 2
LAG = 2


def nn(a, b):
    return lax.dot_general(a, b, (((1,), (0,)), ((), ())), preferred_element_type=F32)


def nt(a, b):
    return lax.dot_general(a, b, (((1,), (1,)), ((), ())), preferred_element_type=F32)


def tn(a, b):
    return lax.dot_general(a, b, (((0,), (0,)), ((), ())), preferred_element_type=F32)


def rows_at(index, size):
    return pl.ds(pl.multiple_of(index * size, size), size)


def greet(n, others=()):
    z = lax.axis_index("tensor")
    barrier = pltpu.get_barrier_semaphore()

    @pl.when(z > 0)
    def _():
        pl.semaphore_signal(barrier, inc=1, device_id={"tensor": z - 1}, device_id_type=MESH)

    @pl.when(z < n - 1)
    def _():
        pl.semaphore_signal(barrier, inc=1, device_id={"tensor": z + 1}, device_id_type=MESH)

    for other in others:
        pl.semaphore_signal(barrier, inc=1, device_id=other, device_id_type=MESH)


def greeted(n, others=()):
    z = lax.axis_index("tensor")
    barrier = pltpu.get_barrier_semaphore()

    @pl.when((z > 0) & (z < n - 1))
    def _():
        pl.semaphore_wait(barrier, 2 + len(others))

    @pl.when((z == 0) | (z == n - 1))
    def _():
        pl.semaphore_wait(barrier, 1 + len(others))


def bit_of(index, bit):
    return (index // (1 << bit)) % 2


def across(index, bit):
    return index + (1 << bit) * (1 - 2 * bit_of(index, bit))


class Gather:
    def __init__(self, n, at, send_sem, recv_sem):
        self.n, self.at, self.send_sem, self.recv_sem = n, at, send_sem, recv_sem
        self.z = lax.axis_index("tensor")
        self.pieces = send_sem.shape[-1]

    def copy(self, slot, step, side, piece, source=None):
        block = self.at(slot)
        size = block.shape[0] // self.pieces
        rows = pl.ds(piece * size, size)
        return pltpu.make_async_remote_copy(
            src_ref=(block if source is None else source).at[rows],
            dst_ref=block.at[rows],
            send_sem=self.send_sem.at[side, step, piece],
            recv_sem=self.recv_sem.at[side, step, piece],
            device_id={"tensor": self.z + 1 - 2 * side},
            device_id_type=MESH,
        )

    def sends(self, step, side):
        z, n = self.z, self.n
        slot = z - (1 - 2 * side) * (step - 1)
        target = z + 1 - 2 * side
        return slot, (slot >= 0) & (slot < n) & (target >= 0) & (target < n)

    def send(self, step, side, piece, source=None, where=True):
        slot, valid = self.sends(step, side)

        @pl.when(valid if where is True else valid & where)
        def _():
            self.copy(slot, step, side, piece, source).start()

    def begin(self, source=None):
        for piece in range(self.pieces):
            for side in range(2):
                self.send(1, side, piece, source)

    def begin_where(self, passes_on):
        for side in range(2):
            source = self.z - (1 - 2 * side)
            other = (source >= 0) & (source < self.n)
            for piece in range(self.pieces):
                self.send(1, side, piece, where=other if passes_on else jnp.logical_not(other))

    def arrive(self, step, side, forward):
        z, n = self.z, self.n
        slot = z - (1 - 2 * side) * step
        for piece in range(self.pieces):

            @pl.when((slot >= 0) & (slot < n))
            def _(piece=piece):
                self.copy(slot, step, side, piece).wait_recv()

            if forward is not False:
                self.send(step + 1, side, piece, where=forward)

    def drain(self, source=None):
        for step in range(1, self.n):
            for side in range(2):
                slot, valid = self.sends(step, side)
                for piece in range(self.pieces):

                    @pl.when(valid)
                    def _(slot=slot, step=step, side=side, piece=piece):
                        self.copy(
                            slot, step, side, piece, source if step == 1 else None
                        ).wait_send()


class Scatter:
    def __init__(self, n, buffer, send_sem, recv_sem):
        self.n, self.buffer, self.send_sem, self.recv_sem = n, buffer, send_sem, recv_sem
        self.z = lax.axis_index("tensor")
        self.pieces = send_sem.shape[-1]
        self.size = buffer.shape[2] // self.pieces

    def rows(self, piece):
        return pl.ds(piece * self.size, self.size)

    def copy(self, step, side, piece):
        return pltpu.make_async_remote_copy(
            src_ref=self.buffer.at[side, step - 1, self.rows(piece)],
            dst_ref=self.buffer.at[side, step, self.rows(piece)],
            send_sem=self.send_sem.at[side, step, piece],
            recv_sem=self.recv_sem.at[side, step, piece],
            device_id={"tensor": self.z + 1 - 2 * side},
            device_id_type=MESH,
        )

    def turn(self, step, side):
        z, n = self.z, self.n
        return z + (1 - 2 * side) * (n - step), step >= 1 + z + side * (n - 1 - 2 * z)

    def has_source(self, side):
        source = self.z - (1 - 2 * side)
        return (source >= 0) & (source < self.n)

    def push(self, step, side, part, first=0):
        has_source = self.has_source(side)
        for piece in range(self.pieces):
            slot = self.buffer.at[side, step - 1, self.rows(piece)]
            rows = pl.ds(pl.multiple_of(first + piece * self.size, self.size), self.size)

            @pl.when(has_source)
            def _(piece=piece, slot=slot, rows=rows):
                self.copy(step - 1, side, piece).wait_recv()
                slot[...] = (part[rows, :] + slot[...].astype(F32)).astype(BF)

            @pl.when(jnp.logical_not(has_source))
            def _(slot=slot, rows=rows):
                slot[...] = part[rows, :].astype(BF)

            self.copy(step, side, piece).start()

    def settle(self, total_ref, then=None):
        for piece in range(self.pieces):
            for side in range(2):

                @pl.when(self.has_source(side))
                def _(side=side, piece=piece):
                    rows = self.rows(piece)
                    self.copy(self.n - 1, side, piece).wait_recv()
                    total_ref[rows, :] += self.buffer[side, self.n - 1, rows, :].astype(F32)

            if then is not None:
                then(piece, piece * self.size, self.size)

    def drain(self):
        for step in range(1, self.n):
            for side in range(2):
                for piece in range(self.pieces):

                    @pl.when(self.turn(step, side)[1])
                    def _(step=step, side=side, piece=piece):
                        self.copy(step, side, piece).wait_send()


def by_rows(rows, body, first=0, block=32):
    def step(index, carry):
        body(pl.ds(pl.multiple_of(first + index * block, block), block))
        return carry

    lax.fori_loop(0, rows // block, step, 0)


def norm_rows(values, gain):
    inverse = lax.rsqrt(jnp.mean(values * values, axis=-1, keepdims=True) + norm_eps)
    return values * inverse * gain, inverse


class Doubling:
    def __init__(self, size, source, target, keep_sem, send_sem, recv_sem):
        self.source, self.target = source, target
        self.keep_sem, self.send_sem, self.recv_sem = keep_sem, send_sem, recv_sem
        self.rows, columns = source.shape
        self.half = columns // 2
        self.me = lax.axis_index("dp")
        self.bits = size.bit_length() - 1
        rest = list(range(1, self.bits))
        self.orders = (rest + [0], rest[::-1] + [0])

    def index(self, order, stage, number):
        index = self.me
        for place in range(stage):
            if (number >> place) & 1:
                index = across(index, order[place])
        return index

    def copy(self, half, stage, number):
        order = self.orders[half]
        columns = slice(half * self.half, (half + 1) * self.half)
        place = self.target.at[rows_at(self.index(order, stage, number), self.rows), columns]
        return pltpu.make_async_remote_copy(
            src_ref=self.source.at[:, columns] if number == 0 else place,
            dst_ref=place,
            send_sem=self.send_sem.at[half, (1 << stage) + number],
            recv_sem=self.recv_sem.at[half, (1 << stage) + number],
            device_id={"dp": across(self.me, order[stage])},
            device_id_type=MESH,
        )

    def arrival(self, half, stage, number):
        order = self.orders[half]
        columns = slice(half * self.half, (half + 1) * self.half)
        index = across(self.index(order, stage, number), order[stage])
        place = self.target.at[rows_at(index, self.rows), columns]
        return pltpu.make_async_remote_copy(
            src_ref=place,
            dst_ref=place,
            send_sem=self.send_sem.at[half, (1 << stage) + number],
            recv_sem=self.recv_sem.at[half, (1 << stage) + number],
            device_id={"dp": across(self.me, order[stage])},
            device_id_type=MESH,
        )

    def own(self):
        return pltpu.make_async_copy(
            self.source, self.target.at[rows_at(self.me, self.rows)], self.keep_sem
        )

    def start(self, stage):
        for half in range(2):
            for number in range(1 << stage):
                self.copy(half, stage, number).start()

    def begin(self):
        self.own().start()
        self.start(0)

    def advance(self, stage):
        for half in range(2):
            for number in range(1 << stage):
                self.arrival(half, stage, number).wait_recv()
        if stage + 1 < self.bits:
            self.start(stage + 1)

    def drain(self, own=True):
        if own:
            self.own().wait()
        for half in range(2):
            for stage in range(self.bits):
                for number in range(1 << stage):
                    self.copy(half, stage, number).wait_send()


class Halving:
    def __init__(self, size, rows, grad, keep, buffer, keep_sem, send_sem, recv_sem):
        self.rows, self.grad, self.keep, self.buffer = rows, grad, keep, buffer
        self.keep_sem, self.send_sem, self.recv_sem = keep_sem, send_sem, recv_sem
        self.me = lax.axis_index("dp")
        self.bits = size.bit_length() - 1
        rest = list(range(1, self.bits))
        self.orders = ([0] + rest, [0] + rest[::-1])
        self.half = buffer.shape[-1]
        self.size = size

    def count(self, stage):
        return self.size >> (stage + 1)

    def offset(self, stage):
        return self.size - (self.size >> stage)

    def block_rows(self, half, number, mine):
        order = self.orders[half]
        first = bit_of(self.me, 0)
        index = first if mine else 1 - first
        later = order[1:]
        for place, bit in enumerate(later):
            index = index + ((number >> (len(later) - 1 - place)) & 1) * (1 << bit)
        return rows_at(index, self.rows)

    def columns(self, half):
        return slice(half * self.half, (half + 1) * self.half)

    def load(self, half, number):
        return pltpu.make_async_copy(
            self.grad.at[self.block_rows(half, number, True), self.columns(half)],
            self.keep.at[half, number],
            self.keep_sem.at[half, number],
        )

    def first_copy(self, half, number):
        return pltpu.make_async_remote_copy(
            src_ref=self.grad.at[self.block_rows(half, number, False), self.columns(half)],
            dst_ref=self.buffer.at[half, number],
            send_sem=self.send_sem.at[half, number],
            recv_sem=self.recv_sem.at[half, number],
            device_id={"dp": across(self.me, 0)},
            device_id_type=MESH,
        )

    def copy(self, half, stage):
        bit = self.orders[half][stage]
        count = self.count(stage)
        goes = (1 - bit_of(self.me, bit)) * count + self.offset(stage - 1)
        return pltpu.make_async_remote_copy(
            src_ref=self.buffer.at[half, pl.ds(goes, count)],
            dst_ref=self.buffer.at[half, pl.ds(self.offset(stage), count)],
            send_sem=self.send_sem.at[half, self.offset(stage)],
            recv_sem=self.recv_sem.at[half, self.offset(stage)],
            device_id={"dp": across(self.me, bit)},
            device_id_type=MESH,
        )

    def begin(self):
        for half in range(2):
            for number in range(self.count(0)):
                self.first_copy(half, number).start()
                self.load(half, number).start()

    def advance(self, stage):
        for half in range(2):
            if stage == 0:
                for number in range(self.count(0)):
                    self.first_copy(half, number).wait_recv()
                    self.load(half, number).wait()
            else:
                self.copy(half, stage).wait_recv()
            if stage == self.bits - 1:
                continue
            base = bit_of(self.me, self.orders[half][stage]) * self.count(stage)

            def add(number, carry, half=half, base=base):
                place = self.offset(stage) + number
                if stage == 0:
                    kept = self.keep[half, number]
                else:
                    kept = self.buffer[half, self.offset(stage - 1) + base + number]
                self.buffer[half, place] = (
                    self.buffer[half, place].astype(F32) + kept.astype(F32)
                ).astype(BF)
                return carry

            lax.fori_loop(0, self.count(stage), add, 0)
            self.copy(half, stage + 1).start()

    def result(self, half):
        stage = self.bits - 1
        base = bit_of(self.me, self.orders[half][stage])
        return self.buffer[half, self.offset(stage)].astype(F32) + self.buffer[
            half, self.offset(stage - 1) + base
        ].astype(F32)

    def drain(self):
        for half in range(2):
            for number in range(self.count(0)):
                self.first_copy(half, number).wait_send()
            for stage in range(1, self.bits):
                self.copy(half, stage).wait_send()


def forward_kernel(
    n,
    dp,
    kv_local,
    x_ref,
    gains_ref,
    wq_ref,
    wgu_ref,
    wo_ref,
    wd_ref,
    cot_ref,
    seg_ref,
    pos_ref,
    freq_ref,
    wqkv_hbm,
    wout_hbm,
    wgu_hbm,
    wd_hbm,
    g1_hbm,
    q_hbm,
    k_hbm,
    v_hbm,
    o_hbm,
    cos_hbm,
    low_hbm,
    high_hbm,
    prob_hbm,
    gf_all,
    m_hbm,
    n2_hbm,
    stat_ref,
    m_ref,
    n2_ref,
    g1,
    wqkv,
    wout,
    own_qkv,
    own_out,
    own_gu,
    q_ref,
    k_ref,
    v_ref,
    o_ref,
    cos_ref,
    low_ref,
    high_ref,
    v_t,
    key_seg,
    key_pos,
    bias,
    prob,
    part,
    sums,
    load_sem,
    out_sem,
    piece_sem,
    prob_sem,
    own_sem,
    n1_send,
    n1_recv,
    ag_send,
    ag_recv,
    rs_send,
    rs_recv,
    keep_sem,
    dp_send,
    dp_recv,
):
    z = lax.axis_index("tensor")
    me = lax.axis_index("dp")
    tokens, width = x_ref.shape
    heads = REPEAT * kv_local
    ff = wd_ref.shape[2]
    half_head = HEAD_WIDTH // 2
    dp_bits = dp.bit_length() - 1
    gain_one, gain_two = gains_ref[0, 0:1, :], gains_ref[0, 1:2, :]
    others = [{"dp": across(me, bit)} for bit in range(dp_bits)]
    greet(n, others)
    first_row = pl.multiple_of(z * tokens, tokens)

    def normalize(rows):
        place = pl.ds(pl.multiple_of(first_row + rows.start, rows.size), rows.size)
        g1[place, :] = norm_rows(x_ref[rows, :], gain_one)[0].astype(BF)

    by_rows(tokens, normalize)
    greeted(n, others)
    spread = Gather(n, lambda slot: g1.at[rows_at(slot, tokens)], n1_send, n1_recv)
    spread.begin()
    shards = [
        Doubling(dp, source, target, keep_sem.at[k], dp_send.at[k], dp_recv.at[k])
        for k, (source, target) in enumerate(
            [
                (own_qkv, wqkv_hbm),
                (own_out, wout_hbm),
                (own_gu, wgu_hbm),
                (wd_ref.at[0], wd_hbm),
            ]
        )
    ]
    early, late = shards[:2], shards[2:]
    for padded, shard in ((own_qkv, wq_ref), (own_out, wo_ref)):
        padded[...] = jnp.zeros_like(padded)
        for head in range(padded.shape[1] // LANES):
            padded[:, head * LANES : head * LANES + HEAD_WIDTH] = shard[
                0, :, head * HEAD_WIDTH : (head + 1) * HEAD_WIDTH
            ]
    for shard in early:
        shard.begin()
    own_gu[:, :ff] = wgu_ref[0, :, 0, :]
    own_gu[:, ff:] = wgu_ref[0, :, 1, :]

    def tables(slot, carry):
        rows = rows_at(slot, tokens)

        def column(row):
            return jnp.broadcast_to(row.astype(F32), (LANES, tokens)).T

        places = column(pos_ref[slot])
        key_pos[rows, :] = places
        key_seg[rows, :] = column(seg_ref[slot])
        angles = places * freq_ref[...]
        sine = jnp.sin(angles)
        lane = lax.broadcasted_iota(jnp.int32, sine.shape, 1)
        cos_ref[rows, :] = jnp.cos(angles)
        low_ref[rows, :] = jnp.where(lane < half_head, -sine, 0.0)
        high_ref[rows, :] = jnp.where((lane >= half_head) & (lane < HEAD_WIDTH), sine, 0.0)
        return carry

    lax.fori_loop(0, n, tables, 0)
    for shard in early:
        shard.advance(0)
    for side in range(2):
        spread.arrive(1, side, n > 2)
    for stage in range(1, dp_bits):
        for shard in early:
            shard.advance(stage)
        if stage == max(dp_bits - 2, 1):
            for shard in late:
                shard.begin()
    for shard in early:
        shard.own().wait()
    loads = [
        pltpu.make_async_copy(wqkv_hbm, wqkv, load_sem.at[0]),
        pltpu.make_async_copy(wout_hbm, wout, load_sem.at[1]),
    ]
    for load in loads:
        load.start()
    gather = Gather(n, lambda slot: gf_all.at[rows_at(slot, tokens)], ag_send, ag_recv)
    keep = pltpu.make_async_copy(cot_ref, gf_all.at[rows_at(z, tokens)], own_sem)
    keep.start()
    loads[0].wait()
    group_width = (REPEAT + 2) * LANES

    def project(slot):
        rows = rows_at(slot, tokens)
        cosine, low, high = cos_ref[rows, :], low_ref[rows, :], high_ref[rows, :]

        def turn(values):
            return (
                values * cosine
                + pltpu.roll(values, LANES - half_head, 1) * low
                + pltpu.roll(values, half_head, 1) * high
            ).astype(BF)

        for group in range(kv_local):
            joined = nn(g1[rows, :], wqkv[:, group * group_width : (group + 1) * group_width])
            for member in range(REPEAT):
                q_ref[group * REPEAT + member, rows, :] = turn(
                    joined[:, member * LANES : (member + 1) * LANES]
                )
            k_ref[group, rows, :] = turn(joined[:, REPEAT * LANES : (REPEAT + 1) * LANES])
            values = joined[:, (REPEAT + 1) * LANES :]
            v_ref[group, rows, :] = values.astype(BF)

    def project_of(index, carry):
        came, near = (index + 1) // 2, (index + 1) % 2
        slot = z - (1 - 2 * near) * came

        @pl.when(came > 1)
        def _():
            spread.arrive(came, near, came < n - 1)

        @pl.when(index == 2 * (n - 2))
        def _():
            gather.begin(cot_ref)

        for stage in range(min(2, dp_bits)):

            @pl.when(index == 3 + 2 * stage)
            def _(stage=stage):
                for shard in late:
                    shard.advance(stage)

        @pl.when((slot >= 0) & (slot < n))
        def _():
            project(slot)

        return carry

    lax.fori_loop(0, 2 * n - 1, project_of, 0)
    outs = [
        pltpu.make_async_copy(source, target, out_sem.at[k])
        for k, (source, target) in enumerate(
            [
                (q_ref, q_hbm),
                (k_ref, k_hbm),
                (v_ref, v_hbm),
                (cos_ref, cos_hbm),
                (low_ref, low_hbm),
                (high_ref, high_hbm),
                (g1, g1_hbm),
                (o_ref, o_hbm),
            ]
        )
    ]
    for out in outs[:-1]:
        out.start()
    for group in range(kv_local):
        v_t[group] = v_ref[group].astype(F32).T.astype(BF)
    loads[1].wait()
    scatter = Scatter(n, sums, rs_send, rs_recv)
    log2_scale = HEAD_WIDTH ** (-0.5) * 1.4426950408889634

    def attend(target):
        rows = rows_at(target, tokens)
        for first in range(0, tokens, LANES):
            lanes = slice(first, first + LANES)
            seen = (key_seg[...] == 0.0) | (
                key_seg[...] == seg_ref[target, :, lanes].astype(F32)
            )
            seen = seen & (key_pos[...] <= pos_ref[target, :, lanes].astype(F32))
            bias[:, lanes] = jnp.where(seen, 0.0, -1e30)

        def one_head(head, carry):
            group = head // REPEAT
            scores = nt(k_ref[group], q_ref[head, rows, :]) * log2_scale + bias[...]
            top = jnp.max(scores, axis=0, keepdims=True)
            weights = jnp.exp2(scores - top)
            total = jnp.sum(weights, axis=0, keepdims=True)
            prob[head] = (weights * (1.0 / total)).astype(BF)
            mixed = nn(v_t[group], prob[head])
            o_ref[rows, rows_at(head, LANES)] = mixed.T.astype(BF)
            return carry

        lax.fori_loop(0, heads, one_head, 0)
        out = pltpu.make_async_copy(prob, prob_hbm.at[target], prob_sem)
        out.start()
        for first in range(0, width, 512):
            part[:, first : first + 512] = nt(o_ref[rows, :], wout[first : first + 512, :])
        out.wait()

    def turn_of(index, carry):
        step, side = index // 2 + 1, index % 2
        target, valid = scatter.turn(step, side)

        @pl.when(valid)
        def _():
            attend(target)

            @pl.when(step < n)
            def _():
                scatter.push(step, side, part)

        for stage in range(2, dp_bits):

            @pl.when(index == 2 * (stage - 2) + 1)
            def _(stage=stage):
                for shard in late:
                    shard.advance(stage)

        @pl.when(step < n)
        def _():
            gather.arrive(step, side, step < n - 1)

        return carry

    lax.fori_loop(0, 2 * (n - 1) + 1, turn_of, 0)
    outs[-1].start()
    stat_ref[...] = jnp.zeros_like(stat_ref)

    def finish(rows):
        branch = part[rows, :]
        middle = x_ref[rows, :] + branch
        m_ref[rows, :] = middle
        n2_ref[rows, :] = norm_rows(middle, gain_two)[0].astype(BF)
        stat_ref[0:1, :] += jnp.sum(middle * middle, axis=0, keepdims=True)
        stat_ref[1:2, :] += jnp.sum(branch * branch, axis=0, keepdims=True)

    def piece_out(piece):
        size = tokens // PIECES
        rows = pl.ds(piece * size, size)
        return [
            pltpu.make_async_copy(source.at[rows], target.at[rows], piece_sem.at[k, piece])
            for k, (source, target) in enumerate([(n2_ref, n2_hbm), (m_ref, m_hbm)])
        ]

    def settled(piece, first, rows):
        by_rows(rows, finish, first)
        for out in piece_out(piece):
            out.start()

    scatter.settle(part, settled)
    for piece in range(PIECES):
        for out in piece_out(piece):
            out.wait()
    keep.wait()
    for out in outs:
        out.wait()
    spread.drain()
    gather.drain(cot_ref)
    scatter.drain()
    for shard in early:
        shard.drain(own=False)
    for shard in late:
        shard.drain()


def forward(n, dp, kv_local, x, gains, w_qkv, w_gate_up, w_out, w_down, cot, seg, pos, freq):
    tokens, width = x.shape
    group_len = n * tokens
    heads = REPEAT * kv_local
    owned = w_qkv.shape[1]
    ff = w_down.shape[2]
    lanes, out_lanes = (REPEAT + 2) * kv_local * LANES, heads * LANES
    vmem = pl.BlockSpec(memory_space=pltpu.VMEM)
    hbm = pl.BlockSpec(memory_space=pl.ANY)
    kept = [
        ((heads, group_len, LANES), BF),
        ((kv_local, group_len, LANES), BF),
        ((kv_local, group_len, LANES), BF),
        ((group_len, out_lanes), BF),
        ((group_len, LANES), F32),
        ((group_len, LANES), F32),
        ((group_len, LANES), F32),
    ]
    flops = 2 * group_len * (
        width * lanes + width * out_lanes + 2 * heads * group_len * LANES
    )
    return pl.pallas_call(
        functools.partial(forward_kernel, n, dp, kv_local),
        out_shape=(
            jax.ShapeDtypeStruct((width, lanes), BF),
            jax.ShapeDtypeStruct((width, out_lanes), BF),
            jax.ShapeDtypeStruct((width, 2 * ff), BF),
            jax.ShapeDtypeStruct((width, ff), BF),
            jax.ShapeDtypeStruct((group_len, width), BF),
            *[jax.ShapeDtypeStruct(shape, kind) for shape, kind in kept],
            jax.ShapeDtypeStruct((n, heads, group_len, tokens), BF),
            jax.ShapeDtypeStruct((group_len, width), BF),
            jax.ShapeDtypeStruct((tokens, width), F32),
            jax.ShapeDtypeStruct((tokens, width), BF),
            jax.ShapeDtypeStruct((8, width), F32),
        ),
        in_specs=[vmem] * 10,
        out_specs=(hbm,) * 16 + (vmem,),
        scratch_shapes=[
            pltpu.VMEM((tokens, width), F32),
            pltpu.VMEM((tokens, width), BF),
            pltpu.VMEM((group_len, width), BF),
            pltpu.VMEM((width, lanes), BF),
            pltpu.VMEM((width, out_lanes), BF),
            pltpu.VMEM((owned, lanes), BF),
            pltpu.VMEM((owned, out_lanes), BF),
            pltpu.VMEM((owned, 2 * ff), BF),
            *[pltpu.VMEM(shape, kind) for shape, kind in kept],
            pltpu.VMEM((kv_local, LANES, group_len), BF),
            pltpu.VMEM((group_len, LANES), F32),
            pltpu.VMEM((group_len, LANES), F32),
            pltpu.VMEM((group_len, tokens), F32),
            pltpu.VMEM((heads, group_len, tokens), BF),
            pltpu.VMEM((tokens, width), F32),
            pltpu.VMEM((2, n, tokens, width), BF),
            pltpu.SemaphoreType.DMA((2,)),
            pltpu.SemaphoreType.DMA((8,)),
            pltpu.SemaphoreType.DMA((2, PIECES)),
            pltpu.SemaphoreType.DMA,
            pltpu.SemaphoreType.DMA,
            *[pltpu.SemaphoreType.DMA((2, n, PIECES))] * 6,
            pltpu.SemaphoreType.DMA((4,)),
            pltpu.SemaphoreType.DMA((4, 2, dp)),
            pltpu.SemaphoreType.DMA((4, 2, dp)),
        ],
        compiler_params=pltpu.CompilerParams(
            collective_id=1, has_side_effects=True, vmem_limit_bytes=VMEM_LIMIT
        ),
        cost_estimate=pl.CostEstimate(
            flops=flops, bytes_accessed=200 * tokens * width * 2, transcendentals=0
        ),
        name="attend_forward",
    )(x, gains, w_qkv, w_gate_up, w_out, w_down, cot, seg, pos, freq)


def feed_kernel(
    n,
    chunks,
    n2_hbm,
    gf_hbm,
    wgu_hbm,
    wd_hbm,
    m_hbm,
    gain_ref,
    cot_hbm,
    z_hbm,
    dm_ref,
    ga_ref,
    dgain_ref,
    dwgu_hbm,
    m_ref,
    cot_ref,
    dwgu_ref,
    n2_all,
    gf_all,
    z_all,
    dgu,
    wgu,
    wd,
    part,
    dn2,
    sums,
    load_sem,
    n2_sem,
    gf_sem,
    z_sem,
    dw_sem,
    ag_send,
    ag_recv,
    rs_send,
    rs_recv,
):
    z = lax.axis_index("tensor")
    greet(n)
    tokens, width = n2_hbm.shape
    ff = wd_hbm.shape[1]
    piece = tokens // chunks
    rows_chunk = n * piece
    load_gu = pltpu.make_async_copy(wgu_hbm, wgu, load_sem.at[0])
    load_d = pltpu.make_async_copy(wd_hbm, wd, load_sem.at[1])

    def load_gf(chunk, slot):
        return pltpu.make_async_copy(
            gf_hbm.at[pl.ds(pl.multiple_of(slot * tokens + chunk * piece, piece), piece)],
            gf_all.at[pl.ds(pl.multiple_of(chunk * rows_chunk + slot * piece, piece), piece)],
            gf_sem.at[chunk, slot],
        )


    def load_n2(chunk):
        return pltpu.make_async_copy(
            n2_hbm.at[chunk * piece : (chunk + 1) * piece],
            n2_all.at[pl.ds(pl.multiple_of(chunk * rows_chunk + z * piece, piece), piece)],
            n2_sem.at[chunk],
        )

    for chunk in range(chunks):
        load_n2(chunk).start()
    load_gu.start()
    load_d.start()
    for chunk in range(chunks):
        for slot in range(n):
            load_gf(chunk, slot).start()
    load_m = pltpu.make_async_copy(m_hbm, m_ref, load_sem.at[2])
    load_cot = pltpu.make_async_copy(cot_hbm, cot_ref, load_sem.at[3])
    load_m.start()
    load_cot.start()
    greeted(n)
    for chunk in range(chunks):
        load_n2(chunk).wait()

    def gather_of(chunk):
        return Gather(
            n,
            lambda slot: n2_all.at[
                pl.ds(pl.multiple_of(chunk * rows_chunk + slot * piece, piece), piece)
            ],
            ag_send.at[chunk],
            ag_recv.at[chunk],
        )

    def scatter_of(chunk):
        return Scatter(n, sums.at[chunk], rs_send.at[chunk], rs_recv.at[chunk])

    gather_of(0).begin_where(True)
    if chunks > 1:
        gather_of(1).begin_where(True)
    for chunk in range(chunks):
        gather_of(chunk).begin_where(False)

    def scatter_end(chunk):
        own = dn2.at[rows_at(chunk, piece)]
        own[...] = part[chunk, rows_at(z, piece), :]
        scatter_of(chunk).settle(own)

    block = 256
    hidden_blocks = ff // block
    out_blocks = width // 512

    def hidden_block(chunk, index):
        rows = rows_at(chunk, rows_chunk)
        cols = rows_at(index, block)
        up_cols = pl.ds(pl.multiple_of(ff + index * block, block), block)
        gate = nn(n2_all[rows, :], wgu[:, cols])
        up = nn(n2_all[rows, :], wgu[:, up_cols])
        dz = nn(gf_all[rows, :], wd[:, cols])
        s = 1.0 / (1.0 + jnp.exp(-gate))
        act = gate * s
        z_all[rows, cols] = (act * up).astype(BF)
        dgu[rows, cols] = (dz * up * (s * (1.0 + gate * (1.0 - s)))).astype(BF)
        dgu[rows, up_cols] = (dz * act).astype(BF)

    def out_block(chunk, index):
        rows = rows_at(chunk, rows_chunk)
        cols = rows_at(index, 512)
        part[chunk, :, cols] = nt(dgu[rows, :], wgu[cols, :])

    def z_out(chunk):
        rows = rows_at(chunk, rows_chunk)
        return pltpu.make_async_copy(z_all.at[rows], z_hbm.at[rows], z_sem.at[chunk])

    def compute(chunk):
        for slot in range(n):
            load_gf(chunk, slot).wait()

        def hidden(index, carry):
            hidden_block(chunk, index)
            return carry

        def out(index, carry):
            out_block(chunk, index)
            return carry

        lax.fori_loop(0, hidden_blocks, hidden, 0)
        lax.fori_loop(0, out_blocks, out, 0)
        z_out(chunk).start()

    def grad_gu(index, carry):
        cols = rows_at(index, 256)
        dwgu_ref[:, cols] = tn(n2_all[...], dgu[:, cols]).astype(BF)
        dw_out(index).start()
        return carry

    def dw_out(index):
        cols = rows_at(index, 256)
        return pltpu.make_async_copy(dwgu_ref.at[:, cols], dwgu_hbm.at[:, cols], dw_sem.at[index])

    blocks = 2 * ff // 256

    def within(chunk):
        return (chunk >= 0) & (chunk < chunks)

    def stage(index, carry):
        for step in range(n - 1, 0, -1):
            chunk = index - (step - 1)

            @pl.when(within(chunk))
            def _(step=step, chunk=chunk):
                for side in range(2):
                    gather_of(chunk).arrive(step, side, step < n - 1)

        @pl.when(index + 2 < chunks)
        def _():
            gather_of(index + 2).begin_where(True)

        ready = index - (n - 2)

        def push(chunk, step, starts):
            scatter = scatter_of(chunk)
            for side in range(2):
                target, valid = scatter.turn(step, side)
                other = scatter.has_source(side)

                @pl.when(valid & (jnp.logical_not(other) if starts else other))
                def _(side=side, target=target):
                    scatter.push(step, side, part.at[chunk], target * piece)

        for step in range(n - 1, 1, -1):
            chunk = ready - LAG * (step - 1)

            @pl.when(within(chunk))
            def _(step=step, chunk=chunk):
                push(chunk, step, False)

        @pl.when(within(ready - LAG * (n - 1)))
        def _():
            scatter_end(ready - LAG * (n - 1))

        @pl.when(ready == 0)
        def _():
            load_gu.wait()
            load_d.wait()

        @pl.when(within(ready))
        def _():
            compute(ready)
            for step in range(1, n):
                push(ready, step, True)

        late, turns = ready - chunks, LAG * (n - 1)

        @pl.when((late >= 0) & (late < turns))
        def _():
            lax.fori_loop(blocks * late // turns, blocks * (late + 1) // turns, grad_gu, 0)

        return carry

    lax.fori_loop(0, chunks + n - 2 + LAG * (n - 1), stage, 0)
    load_m.wait()
    load_cot.wait()
    gain = gain_ref[0, 1:2, :]
    dgain_ref[...] = jnp.zeros_like(dgain_ref)

    def finish(rows):
        middle = m_ref[rows, :]
        dn = dn2[rows, :]
        inverse = lax.rsqrt(jnp.mean(middle * middle, axis=-1, keepdims=True) + norm_eps)
        scaled = dn * gain
        dgain_ref[0:1, :] += jnp.sum(dn * middle * inverse, axis=0, keepdims=True)
        dm = (
            inverse * scaled
            - middle * inverse**3 * jnp.mean(scaled * middle, axis=-1, keepdims=True)
            + cot_ref[rows, :].astype(F32)
        )
        dm_ref[rows, :] = dm
        ga_ref[rows, :] = dm.astype(BF)

    by_rows(tokens, finish)
    for index in range(blocks):
        dw_out(index).wait()
    for chunk in range(chunks):
        z_out(chunk).wait()
        gather_of(chunk).drain()
        scatter_of(chunk).drain()


def feed(n, chunks, n2, gf_all, wgu, wd, m, gain, cot):
    tokens, width = n2.shape
    group_len = n * tokens
    ff = wd.shape[1]
    vmem = pl.BlockSpec(memory_space=pltpu.VMEM)
    hbm = pl.BlockSpec(memory_space=pl.ANY)
    return pl.pallas_call(
        functools.partial(feed_kernel, n, chunks),
        out_shape=(
            jax.ShapeDtypeStruct((group_len, ff), BF),
            jax.ShapeDtypeStruct((tokens, width), F32),
            jax.ShapeDtypeStruct((tokens, width), BF),
            jax.ShapeDtypeStruct((8, width), F32),
            jax.ShapeDtypeStruct((width, 2 * ff), BF),
        ),
        in_specs=[hbm] * 5 + [vmem, hbm],
        out_specs=(hbm, vmem, vmem, vmem, hbm),
        scratch_shapes=[
            pltpu.VMEM((tokens, width), F32),
            pltpu.VMEM((tokens, width), BF),
            pltpu.VMEM((width, 2 * ff), BF),
            pltpu.VMEM((group_len, width), BF),
            pltpu.VMEM((group_len, width), BF),
            pltpu.VMEM((group_len, ff), BF),
            pltpu.VMEM((group_len, 2 * ff), BF),
            pltpu.VMEM((width, 2 * ff), BF),
            pltpu.VMEM((width, ff), BF),
            pltpu.VMEM((chunks, group_len // chunks, width), F32),
            pltpu.VMEM((tokens, width), F32),
            pltpu.VMEM((chunks, 2, n, tokens // chunks, width), BF),
            pltpu.SemaphoreType.DMA((4,)),
            pltpu.SemaphoreType.DMA((chunks,)),
            pltpu.SemaphoreType.DMA((chunks, n)),
            pltpu.SemaphoreType.DMA((chunks,)),
            pltpu.SemaphoreType.DMA((2 * ff // 256,)),
            pltpu.SemaphoreType.DMA((chunks, 2, n, 1)),
            pltpu.SemaphoreType.DMA((chunks, 2, n, 1)),
            pltpu.SemaphoreType.DMA((chunks, 2, n, 1)),
            pltpu.SemaphoreType.DMA((chunks, 2, n, 1)),
        ],
        compiler_params=pltpu.CompilerParams(
            collective_id=3, has_side_effects=True, vmem_limit_bytes=VMEM_LIMIT
        ),
        cost_estimate=pl.CostEstimate(
            flops=18 * group_len * width * ff, bytes_accessed=250 * tokens * width * 2, transcendentals=0
        ),
        name="feed_both",
    )(n2, gf_all, wgu, wd, m, gain, cot)


def attend_back_kernel(
    n,
    dp,
    kv_local,
    chunks,
    ga_hbm,
    wout_hbm,
    wd_hbm,
    z_hbm,
    prob_hbm,
    gf_hbm,
    dwgu_hbm,
    m_hbm,
    q_hbm,
    k_hbm,
    v_hbm,
    o_hbm,
    cos_hbm,
    low_hbm,
    high_hbm,
    out_hbm,
    stat_ref,
    dqkv_hbm,
    dwd_hbm,
    ga_out,
    grad_gu_hbm,
    out_ref,
    m_ref,
    q_ref,
    k_ref,
    v_ref,
    o_ref,
    cos_ref,
    sin_low_ref,
    sin_high_ref,
    dqkv_ref,
    dwd_ref,
    grad_gu_ref,
    keep,
    held,
    ga_all,
    gf,
    wout,
    wd,
    z_all,
    k_t,
    prob,
    d_out,
    dk,
    dv,
    part,
    sums,
    load_sem,
    gf_sem,
    prob_sem,
    out_sem,
    piece_sem,
    ag_send,
    ag_recv,
    rs_send,
    rs_recv,
    keep_sem,
    dp_send,
    dp_recv,
):
    z = lax.axis_index("tensor")
    me = lax.axis_index("dp")
    dp_bits = dp.bit_length() - 1
    others = [{"dp": across(me, bit)} for bit in range(dp_bits)]
    greet(n, others)
    tokens, width = ga_hbm.shape
    heads = REPEAT * kv_local
    group_len = n * tokens
    piece = tokens // chunks
    scale = HEAD_WIDTH ** (-0.5)
    loads = [
        pltpu.make_async_copy(source, target, load_sem.at[index])
        for index, (source, target) in enumerate(
            [
                (ga_hbm, ga_all.at[rows_at(z, tokens)]),
                (wout_hbm, wout),
                (k_hbm, k_ref),
                (v_hbm, v_ref),
                (q_hbm, q_ref),
                (o_hbm, o_ref),
                (cos_hbm, cos_ref),
                (low_hbm, sin_low_ref),
                (high_hbm, sin_high_ref),
                (z_hbm, z_all),
                (wd_hbm, wd),
                (m_hbm, m_ref),
            ]
        )
    ]
    for load in loads:
        load.start()

    def load_gf(chunk, slot):
        return pltpu.make_async_copy(
            gf_hbm.at[pl.ds(pl.multiple_of(slot * tokens + chunk * piece, piece), piece)],
            gf.at[pl.ds(pl.multiple_of((chunk * n + slot) * piece, piece), piece)],
            gf_sem.at[chunk, slot],
        )

    for chunk in range(chunks):
        for slot in range(n):
            load_gf(chunk, slot).start()

    def load_prob(slot):
        return pltpu.make_async_copy(prob_hbm.at[slot], prob, prob_sem)

    greeted(n, others)
    gather = Gather(n, lambda slot: ga_all.at[rows_at(slot, tokens)], ag_send, ag_recv)
    loads[0].wait()
    gather.begin()
    halving = Halving(
        dp, grad_gu_ref.shape[0], dwgu_hbm, keep, held, keep_sem, dp_send, dp_recv
    )
    halving.begin()
    scatter = Scatter(n, sums, rs_send, rs_recv)
    for load in loads[1:-1]:
        load.wait()
    for group in range(kv_local):
        k_t[group] = k_ref[group].astype(F32).T.astype(BF)
    dk[...] = jnp.zeros_like(dk)
    dv[...] = jnp.zeros_like(dv)
    group_lanes = (REPEAT + 2) * LANES

    def turn_back(values, rows):
        return (
            values * cos_ref[rows, :]
            - pltpu.roll(values, LANES - HEAD_WIDTH // 2, 1) * sin_low_ref[rows, :]
            - pltpu.roll(values, HEAD_WIDTH // 2, 1) * sin_high_ref[rows, :]
        )

    def back(slot):
        rows = rows_at(slot, tokens)
        d_o = nn(ga_all[rows, :], wout[...])
        d_out[...] = d_o.astype(BF)

        def one_head(head, carry):
            group = head // REPEAT
            lanes = rows_at(head, LANES)
            do_h = d_out[:, lanes]
            both = do_h.astype(F32) * o_ref[rows, lanes].astype(F32)
            delta = jnp.sum(both.T, axis=0, keepdims=True)
            dprob = nt(v_ref[group], do_h)
            weights = prob[head]
            ds = (weights.astype(F32) * (dprob - delta)).astype(BF)
            dv[group] += nn(weights, do_h)
            dk[group] += nn(ds, q_ref[head, rows, :])
            dq = nn(k_t[group], ds).T * scale
            first = group * (REPEAT + 2) + head % REPEAT
            dqkv_ref[rows, rows_at(first, LANES)] = turn_back(dq, rows).astype(BF)
            return carry

        lax.fori_loop(0, heads, one_head, 0)

    def feed_rows(target):
        pieces = [
            z_all[
                pl.ds(
                    pl.multiple_of(chunk * n * piece + target * piece, piece), piece
                ),
                :,
            ]
            for chunk in range(chunks)
        ]
        rows = jnp.concatenate(pieces, axis=0) if chunks > 1 else pieces[0]
        for first in range(0, width, 512):
            part[:, first : first + 512] = nt(rows, wd[first : first + 512, :])

    def turn_of(index, carry):
        came, near = (index + 1) // 2, (index + 1) % 2
        slot = z - (1 - 2 * near) * came
        valid = (slot >= 0) & (slot < n)

        @pl.when(valid)
        def _():
            load_prob(slot).start()

        @pl.when(index > 0)
        def _():
            gather.arrive(came, near, came < n - 1)

        step, side = index // 2 + 1, index % 2
        target, sends = scatter.turn(step, side)

        @pl.when(sends & (step < n))
        def _():
            feed_rows(target)
            scatter.push(step, side, part)

        @pl.when(valid)
        def _():
            load_prob(slot).wait()
            back(slot)

        return carry

    for chunk in range(chunks):
        for slot in range(n):
            load_gf(chunk, slot).wait()
    ff = wd_hbm.shape[1]
    down_blocks = ff // 256

    def grad_down(first, last):
        def body(index, carry):
            cols = rows_at(index, 256)
            dwd_ref[:, cols] = tn(gf[...], z_all[:, cols]).astype(BF)
            return carry

        lax.fori_loop(first, last, body, 0)

    turns = 2 * n - 1

    def turn_and_grad(index, carry):
        turn_of(index, 0)
        grad_down(down_blocks * index // turns, down_blocks * (index + 1) // turns)
        for stage in range(dp_bits):

            @pl.when(index == 2 * stage + 1)
            def _(stage=stage):
                halving.advance(stage)

        return carry

    lax.fori_loop(0, turns, turn_and_grad, 0)

    def finish_keys(slot, carry):
        rows = rows_at(slot, tokens)
        for group in range(kv_local):
            first = group * group_lanes + REPEAT * LANES
            dqkv_ref[rows, first : first + LANES] = turn_back(
                dk[group, rows, :] * scale, rows
            ).astype(BF)
            dqkv_ref[rows, first + LANES : first + 2 * LANES] = dv[group, rows, :].astype(BF)
        return carry

    lax.fori_loop(0, n, finish_keys, 0)
    outs = [
        pltpu.make_async_copy(source, target, out_sem.at[index])
        for index, (source, target) in enumerate(
            [(dqkv_ref, dqkv_hbm), (dwd_ref, dwd_hbm), (ga_all, ga_out), (grad_gu_ref, grad_gu_hbm)]
        )
    ]
    for out in outs[:3]:
        out.start()
    for half in range(2):
        grad_gu_ref[:, half, :] = halving.result(half)
    outs[3].start()
    feed_rows(z)
    loads[-1].wait()
    stat_ref[...] = jnp.zeros_like(stat_ref)

    def finish(rows):
        branch = part[rows, :]
        result = m_ref[rows, :] + branch
        out_ref[rows, :] = result
        stat_ref[0:1, :] += jnp.sum(result * result, axis=0, keepdims=True)
        stat_ref[1:2, :] += jnp.sum(branch * branch, axis=0, keepdims=True)

    def piece_out(piece):
        size = tokens // PIECES
        rows = pl.ds(piece * size, size)
        return pltpu.make_async_copy(out_ref.at[rows], out_hbm.at[rows], piece_sem.at[piece])

    def settled(piece, first, rows):
        by_rows(rows, finish, first)
        piece_out(piece).start()

    scatter.settle(part, settled)
    for piece in range(PIECES):
        piece_out(piece).wait()
    for out in outs:
        out.wait()
    gather.drain()
    scatter.drain()
    halving.drain()


def attend_back(n, dp, kv_local, chunks, ga, wout, wd, z_all, prob, gf, dwgu, m, q, k, v, o, tables):
    tokens, width = ga.shape
    group_len = n * tokens
    heads = REPEAT * kv_local
    ff = wd.shape[1]
    owned = width // dp
    lanes = (REPEAT + 2) * kv_local * LANES
    vmem = pl.BlockSpec(memory_space=pltpu.VMEM)
    hbm = pl.BlockSpec(memory_space=pl.ANY)
    return pl.pallas_call(
        functools.partial(attend_back_kernel, n, dp, kv_local, chunks),
        out_shape=(
            jax.ShapeDtypeStruct((tokens, width), F32),
            jax.ShapeDtypeStruct((8, width), F32),
            jax.ShapeDtypeStruct((group_len, lanes), BF),
            jax.ShapeDtypeStruct((width, ff), BF),
            jax.ShapeDtypeStruct((group_len, width), BF),
            jax.ShapeDtypeStruct((owned, 2, ff), F32),
        ),
        in_specs=[hbm] * 15,
        out_specs=(hbm, vmem, hbm, hbm, hbm, hbm),
        scratch_shapes=[
            pltpu.VMEM((tokens, width), F32),
            pltpu.VMEM((tokens, width), F32),
            pltpu.VMEM(q.shape, BF),
            pltpu.VMEM(k.shape, BF),
            pltpu.VMEM(v.shape, BF),
            pltpu.VMEM(o.shape, BF),
            *[pltpu.VMEM((group_len, LANES), F32)] * 3,
            pltpu.VMEM((group_len, lanes), BF),
            pltpu.VMEM((width, ff), BF),
            pltpu.VMEM((owned, 2, ff), F32),
            pltpu.VMEM((2, dp // 2, owned, ff), BF),
            pltpu.VMEM((2, dp - 1, owned, ff), BF),
            pltpu.VMEM((group_len, width), BF),
            pltpu.VMEM((group_len, width), BF),
            pltpu.VMEM(wout.shape, BF),
            pltpu.VMEM(wd.shape, BF),
            pltpu.VMEM((group_len, ff), BF),
            pltpu.VMEM((kv_local, LANES, group_len), BF),
            pltpu.VMEM((heads, group_len, tokens), BF),
            pltpu.VMEM((tokens, heads * LANES), BF),
            pltpu.VMEM((kv_local, group_len, LANES), F32),
            pltpu.VMEM((kv_local, group_len, LANES), F32),
            pltpu.VMEM((tokens, width), F32),
            pltpu.VMEM((2, n, tokens, width), BF),
            pltpu.SemaphoreType.DMA((12,)),
            pltpu.SemaphoreType.DMA((chunks, n)),
            pltpu.SemaphoreType.DMA,
            pltpu.SemaphoreType.DMA((4,)),
            pltpu.SemaphoreType.DMA((PIECES,)),
            pltpu.SemaphoreType.DMA((2, n, PIECES)),
            pltpu.SemaphoreType.DMA((2, n, PIECES)),
            pltpu.SemaphoreType.DMA((2, n, PIECES)),
            pltpu.SemaphoreType.DMA((2, n, PIECES)),
            pltpu.SemaphoreType.DMA((2, dp // 2)),
            pltpu.SemaphoreType.DMA((2, dp)),
            pltpu.SemaphoreType.DMA((2, dp)),
        ],
        compiler_params=pltpu.CompilerParams(
            collective_id=4, has_side_effects=True, vmem_limit_bytes=VMEM_LIMIT
        ),
        cost_estimate=pl.CostEstimate(
            flops=8 * group_len * width * ff, bytes_accessed=200 * tokens * width * 2, transcendentals=0
        ),
        name="attend_backward",
    )(ga, wout, wd, z_all, prob, gf, dwgu, m, q, k, v, o, *tables)


class Sharing:
    def __init__(self, axis, size, source, slots, send_sem, recv_sem):
        self.axis, self.size, self.source, self.slots = axis, size, source, slots
        self.send_sem, self.recv_sem = send_sem, recv_sem
        self.me = lax.axis_index(axis)

    def copy(self, offset):
        return pltpu.make_async_remote_copy(
            src_ref=self.source,
            dst_ref=self.slots.at[self.me],
            send_sem=self.send_sem.at[offset],
            recv_sem=self.recv_sem.at[offset],
            device_id={self.axis: (self.me + offset) % self.size},
            device_id_type=MESH,
        )

    def arrival(self, offset):
        place = self.slots.at[(self.me + self.size - offset) % self.size]
        return pltpu.make_async_remote_copy(
            src_ref=place,
            dst_ref=place,
            send_sem=self.send_sem.at[offset],
            recv_sem=self.recv_sem.at[offset],
            device_id={self.axis: (self.me + self.size - offset) % self.size},
            device_id_type=MESH,
        )

    def begin(self):
        for offset in range(1, self.size):
            self.copy(offset).start()
        self.slots[self.me] = self.source[...]

    def total(self):
        for offset in range(1, self.size):
            self.arrival(offset).wait_recv()
        total = self.slots[0]
        for index in range(1, self.size):
            total = total + self.slots[index]
        return total

    def drain(self):
        for offset in range(1, self.size):
            self.copy(offset).wait_send()


def last_kernel(
    n,
    dp,
    cells,
    out_heads,
    dqkv_hbm,
    wqkv_hbm,
    x_hbm,
    dm_hbm,
    gain_ref,
    dgain_two_ref,
    stat_one_ref,
    stat_two_ref,
    g1_hbm,
    ga_hbm,
    o_hbm,
    dwd_hbm,
    dx_hbm,
    gains_ref,
    rms_ref,
    grad_out_ref,
    grad_qkv_ref,
    grad_down_ref,
    dx_ref,
    dqkv,
    wqkv,
    x,
    dm,
    g1,
    ga,
    o,
    dw,
    part,
    sums,
    down_keep,
    down_held,
    head_keep,
    head_held,
    vector,
    packed,
    group_sum,
    dp_slots,
    z_slots,
    load_sem,
    piece_sem,
    rs_send,
    rs_recv,
    down_keep_sem,
    down_send,
    down_recv,
    head_keep_sem,
    head_send,
    head_recv,
    dp_slot_send,
    dp_slot_recv,
    z_slot_send,
    z_slot_recv,
):
    z = lax.axis_index("tensor")
    me = lax.axis_index("dp")
    tokens, width = x.shape
    dp_bits = dp.bit_length() - 1
    others = [{"dp": (me + offset) % dp} for offset in range(1, dp)]
    others += [{"tensor": (z + offset) % n} for offset in range(1, n)]
    barrier = pltpu.get_barrier_semaphore()
    for other in others:
        pl.semaphore_signal(barrier, inc=1, device_id=other, device_id_type=MESH)
    owned = grad_out_ref.shape[0]
    loads = [
        pltpu.make_async_copy(source, target, load_sem.at[index])
        for index, (source, target) in enumerate(
            [
                (wqkv_hbm, wqkv),
                (dqkv_hbm, dqkv),
                (g1_hbm, g1),
                (ga_hbm, ga),
                (o_hbm, o),
                (x_hbm, x),
                (dm_hbm, dm),
            ]
        )
    ]
    for load in loads:
        load.start()
    pl.semaphore_wait(barrier, len(others))
    down = Halving(dp, owned, dwd_hbm, down_keep, down_held, down_keep_sem, down_send, down_recv)
    down.begin()
    halving = Halving(dp, owned, dw, head_keep, head_held, head_keep_sem, head_send, head_recv)
    scatter = Scatter(n, sums, rs_send, rs_recv)
    gain = gain_ref[0, 0:1, :]
    vector[...] = jnp.zeros_like(vector)
    vector[1:2, :] = dgain_two_ref[0:1, :]
    vector[2:3, :] = stat_one_ref[0:1, :]
    vector[3:4, :] = stat_two_ref[0:1, :]
    vector[4:5, :] = stat_one_ref[1:2, :]
    vector[5:6, :] = stat_two_ref[1:2, :]
    for load in loads[:3]:
        load.wait()
    out_lanes = o.shape[1]

    def grad_qkv(index, carry):
        place = pl.ds(pl.multiple_of(out_lanes + index * 256, 256), 256)
        dw[:, place] = tn(g1[...], dqkv[:, rows_at(index, 256)]).astype(BF)
        return carry

    def grad_out(index, carry):
        cols = rows_at(index, 256)
        dw[:, cols] = tn(ga[...], o[:, cols]).astype(BF)
        return carry

    def compute(index, carry):
        step, side = index // 2 + 1, index % 2
        target, due = scatter.turn(step, side)

        @pl.when(due)
        def _():
            rows = rows_at(target, tokens)

            def block(number, carry):
                cols = rows_at(number, 256)
                values = nt(dqkv[rows, :], wqkv[cols, :])
                part[rows, cols] = values
                vector[0:1, cols] += jnp.sum(
                    values * g1[rows, cols].astype(F32), axis=0, keepdims=True
                )
                return carry

            lax.fori_loop(0, width // 256, block, 0)

            @pl.when((step < n - 1) & jnp.logical_not(scatter.has_source(side)))
            def _():
                scatter.push(step, side, part, target * tokens)

        return carry

    def compute_and_grads(index, carry):
        compute(index, 0)

        @pl.when(index == 1)
        def _():
            for load in loads[3:]:
                load.wait()
            lax.fori_loop(0, dqkv.shape[1] // 256, grad_qkv, 0)
            lax.fori_loop(0, out_lanes // 256, grad_out, 0)
            halving.begin()

        return carry

    lax.fori_loop(0, 2 * n - 1, compute_and_grads, 0)
    vector[0:1, :] = vector[0:1, :] / gain

    blocks = width // LANES
    packed[...] = jnp.zeros_like(packed)
    for row in range(6):
        parts = [
            vector[row : row + 1, index * LANES : (index + 1) * LANES] for index in range(blocks)
        ]
        if row < 2:
            for index, values in enumerate(parts):
                packed[row * blocks + index : row * blocks + index + 1, :] = values
        else:
            place = 2 * blocks + row - 2
            packed[place : place + 1, :] = functools.reduce(jnp.add, parts)
    near = Sharing("dp", dp, packed, dp_slots, dp_slot_send, dp_slot_recv)
    far = Sharing("tensor", n, group_sum, z_slots, z_slot_send, z_slot_recv)
    near.begin()
    down.advance(0)
    halving.advance(0)

    def push_came(step):
        for side in range(2):
            target, sends = scatter.turn(step, side)

            @pl.when(sends & scatter.has_source(side))
            def _(side=side, target=target):
                scatter.push(step, side, part, target * tokens)

    def push_last_start():
        for side in range(2):
            target, sends = scatter.turn(n - 1, side)

            @pl.when(sends & jnp.logical_not(scatter.has_source(side)))
            def _(side=side, target=target):
                scatter.push(n - 1, side, part, target * tokens)

    done = 1
    for step in range(2, n):
        push_came(step)
        if step == 2:
            group_sum[...] = near.total()
            far.begin()
            push_last_start()
        until = 1 + (dp_bits - 1) * (step - 1) // (n - 1)
        for stage in range(done, until):
            down.advance(stage)
            halving.advance(stage)
        done = until
    for stage in range(done, dp_bits):
        down.advance(stage)
        halving.advance(stage)
    for half in range(2):
        columns = down.columns(half)
        grad_down_ref[:, columns] = down.result(half)
    place = 0
    for half in range(2):
        block = halving.result(half)
        for index in range(block.shape[1] // LANES):
            values = block[:, index * LANES : index * LANES + HEAD_WIDTH]
            if place < out_heads:
                grad_out_ref[:, place * HEAD_WIDTH : (place + 1) * HEAD_WIDTH] = values
            else:
                head = place - out_heads
                grad_qkv_ref[:, head * HEAD_WIDTH : (head + 1) * HEAD_WIDTH] = values
            place += 1
    total = far.total()
    for which in range(2):
        for index in range(blocks):
            gains_ref[0, which : which + 1, index * LANES : (index + 1) * LANES] = total[
                which * blocks + index : which * blocks + index + 1, :
            ]
    squares = jnp.sqrt(jnp.sum(total, axis=1, keepdims=True) * (1.0 / cells))
    row = lax.broadcasted_iota(jnp.int32, (total.shape[0], 4), 0)
    column = lax.broadcasted_iota(jnp.int32, (total.shape[0], 4), 1)
    rms_ref[...] = jnp.sum(jnp.where(row == column + 2 * blocks, squares, 0.0), axis=0, keepdims=True)
    own = part.at[rows_at(z, tokens)]

    def finish(rows):
        values = x[rows, :]
        dn = own[rows, :]
        inverse = lax.rsqrt(jnp.mean(values * values, axis=-1, keepdims=True) + norm_eps)
        scaled = dn * gain
        dx_ref[rows, :] = (
            inverse * scaled
            - values * inverse**3 * jnp.mean(scaled * values, axis=-1, keepdims=True)
            + dm[rows, :]
        )

    def piece_out(piece):
        size = tokens // PIECES
        rows = pl.ds(piece * size, size)
        return pltpu.make_async_copy(dx_ref.at[rows], dx_hbm.at[rows], piece_sem.at[piece])

    def settled(piece, first, rows):
        by_rows(rows, finish, first)
        piece_out(piece).start()

    scatter.settle(own, settled)
    for piece in range(PIECES):
        piece_out(piece).wait()
    near.drain()
    far.drain()
    down.drain()
    halving.drain()
    scatter.drain()


def last(n, dqkv, wqkv, x, dm, gain, dgain_two, stat_one, stat_two, g1, ga, o, dwd, out_columns, qkv_columns):
    tokens, width = x.shape
    dp = lax.axis_size("dp")
    owned = width // dp
    ff = dwd.shape[1]
    columns = o.shape[1] + dqkv.shape[1]
    small = -(-(2 * width // LANES + 4) // 8) * 8
    vmem = pl.BlockSpec(memory_space=pltpu.VMEM)
    hbm = pl.BlockSpec(memory_space=pl.ANY)
    return pl.pallas_call(
        functools.partial(last_kernel, n, dp, tokens * width * dp * n, out_columns // HEAD_WIDTH),
        out_shape=(
            jax.ShapeDtypeStruct((tokens, width), F32),
            jax.ShapeDtypeStruct((1, 2, width), F32),
            jax.ShapeDtypeStruct((1, 4), F32),
            jax.ShapeDtypeStruct((owned, out_columns), F32),
            jax.ShapeDtypeStruct((owned, qkv_columns), F32),
            jax.ShapeDtypeStruct((owned, ff), F32),
        ),
        in_specs=[hbm] * 4 + [vmem] * 4 + [hbm] * 4,
        out_specs=(hbm,) + (vmem,) * 5,
        scratch_shapes=[
            pltpu.VMEM(x.shape, F32),
            pltpu.VMEM(dqkv.shape, BF),
            pltpu.VMEM(wqkv.shape, BF),
            pltpu.VMEM(x.shape, F32),
            pltpu.VMEM(dm.shape, F32),
            pltpu.VMEM(g1.shape, BF),
            pltpu.VMEM(ga.shape, BF),
            pltpu.VMEM(o.shape, BF),
            pltpu.VMEM((width, columns), BF),
            pltpu.VMEM((n * tokens, width), F32),
            pltpu.VMEM((2, n, tokens, width), BF),
            pltpu.VMEM((2, dp // 2, owned, ff // 2), BF),
            pltpu.VMEM((2, dp - 1, owned, ff // 2), BF),
            pltpu.VMEM((2, dp // 2, owned, columns // 2), BF),
            pltpu.VMEM((2, dp - 1, owned, columns // 2), BF),
            pltpu.VMEM((8, width), F32),
            pltpu.VMEM((small, LANES), F32),
            pltpu.VMEM((small, LANES), F32),
            pltpu.VMEM((dp, small, LANES), F32),
            pltpu.VMEM((n, small, LANES), F32),
            pltpu.SemaphoreType.DMA((7,)),
            pltpu.SemaphoreType.DMA((PIECES,)),
            pltpu.SemaphoreType.DMA((2, n, PIECES)),
            pltpu.SemaphoreType.DMA((2, n, PIECES)),
            *[
                pltpu.SemaphoreType.DMA((2, dp // 2)),
                pltpu.SemaphoreType.DMA((2, dp)),
                pltpu.SemaphoreType.DMA((2, dp)),
            ]
            * 2,
            pltpu.SemaphoreType.DMA((dp,)),
            pltpu.SemaphoreType.DMA((dp,)),
            pltpu.SemaphoreType.DMA((n,)),
            pltpu.SemaphoreType.DMA((n,)),
        ],
        compiler_params=pltpu.CompilerParams(
            collective_id=5, has_side_effects=True, vmem_limit_bytes=VMEM_LIMIT
        ),
        cost_estimate=pl.CostEstimate(
            flops=2 * dqkv.size * width, bytes_accessed=150 * tokens * width * 2, transcendentals=0
        ),
        name="input_gradient",
    )(dqkv, wqkv, x, dm, gain, dgain_two, stat_one, stat_two, g1, ga, o, dwd)


def deliver_kernel(*refs):
    count = len(refs) // 3
    sources, targets, held = refs[:count], refs[count : 2 * count], refs[2 * count : 3 * count]
    sem = refs[-1]
    ins = [
        pltpu.make_async_copy(source, place, sem.at[0, index])
        for index, (source, place) in enumerate(zip(sources, held, strict=True))
    ]
    outs = [
        pltpu.make_async_copy(place, target, sem.at[1, index])
        for index, (place, target) in enumerate(zip(held, targets, strict=True))
    ]
    for copy in ins:
        copy.start()
    for copy, out in zip(ins, outs, strict=True):
        copy.wait()
        out.start()
    for out in outs:
        out.wait()


def deliver(*arrays):
    hbm = pl.BlockSpec(memory_space=pl.ANY)
    return pl.pallas_call(
        deliver_kernel,
        out_shape=[jax.ShapeDtypeStruct(array.shape, array.dtype) for array in arrays],
        in_specs=[hbm] * len(arrays),
        out_specs=[hbm] * len(arrays),
        scratch_shapes=[
            *[pltpu.VMEM(array.shape, array.dtype) for array in arrays],
            pltpu.SemaphoreType.DMA((2, len(arrays))),
        ],
        compiler_params=pltpu.CompilerParams(vmem_limit_bytes=VMEM_LIMIT),
        name="deliver",
    )(*arrays)


def per_device(inputs, norm_gains, w_qkv, w_gate_up, w_out, w_down, segments, positions, cotangent):
    n, dp = lax.axis_size("tensor"), lax.axis_size("dp")
    tokens, width = inputs.shape
    kv_local = w_out.shape[2] // (REPEAT * HEAD_WIDTH)
    chunks = 8
    half = HEAD_WIDTH // 2
    freq_steps = jnp.arange(half, dtype=F32) * (2.0 / HEAD_WIDTH)
    inverse = jnp.power(rope_base, -freq_steps)
    freq = jnp.concatenate([inverse, inverse, jnp.zeros((LANES - HEAD_WIDTH,), F32)])[None]

    (
        wqkv,
        wout,
        wgu,
        wd,
        g1,
        q,
        k,
        v,
        o,
        cosine,
        low,
        high,
        prob,
        gf_all,
        m,
        n2,
        stat_one,
    ) = forward(
        n,
        dp,
        kv_local,
        inputs,
        norm_gains,
        w_qkv,
        w_gate_up,
        w_out,
        w_down,
        cotangent,
        segments.reshape(n, 1, tokens),
        positions.reshape(n, 1, tokens),
        freq,
    )
    z_all, dm, ga, dgain_two, dwgu = feed(n, chunks, n2, gf_all, wgu, wd, m, norm_gains, cotangent)
    output, stat_two, dqkv, dwd, ga_all, grad_gu = attend_back(
        n,
        dp,
        kv_local,
        chunks,
        ga,
        wout,
        wd,
        z_all,
        prob,
        gf_all,
        dwgu,
        m,
        q,
        k,
        v,
        o,
        (cosine, low, high),
    )
    input_grad, gain_total, rms, grad_out, grad_qkv, grad_down = last(
        n,
        dqkv,
        wqkv,
        inputs,
        dm,
        norm_gains,
        dgain_two,
        stat_one,
        stat_two,
        g1,
        ga_all,
        o,
        dwd,
        w_out.shape[2],
        w_qkv.shape[2],
    )
    output, input_grad, grad_qkv, grad_gu, grad_out, grad_down, gain_total, rms = deliver(
        output, input_grad, grad_qkv, grad_gu, grad_out, grad_down, gain_total, rms
    )
    return (
        output,
        input_grad,
        grad_qkv[None],
        grad_gu[None],
        grad_out[None],
        grad_down[None],
        gain_total,
        rms,
    )


def solution(mesh):
    rows = P(("dp", "tensor"), None)
    weights = P(None, "dp", "tensor")
    pairs = P(None, "dp", None, "tensor")
    return jax.shard_map(
        per_device,
        mesh=mesh,
        in_specs=(rows, P(), weights, pairs, weights, weights, P("dp"), P("dp"), rows),
        out_specs=(rows, rows, weights, pairs, weights, weights, P(), P()),
        check_vma=False,
    )
```
